32 devices in a mesh: seq: 16 (over z, y, core), fsdp: 2 (over x).
Axes of the slice: x: 2, y: 2, z: 4, core: 2. Of those that a mesh axis runs over, the one named last changes fastest.
Arguments:
- inputs: bfloat16 [2, 2, 2048, 1536], P('fsdp', None, 'seq'), may hold values from -6 to 6
- lengths: int32 [2, 2, 4], P('fsdp'), may hold values from 1 to 1024, 2048 in all within a row
- attn_gain: bfloat16 [1536], P(('seq', 'fsdp')), may hold values from 0.25 to 1.75
- query_weight: bfloat16 [1536, 1536], P(('seq', 'fsdp')), may hold values from -0.3125 to 0.3125
- query_bias: bfloat16 [1536], P(('seq', 'fsdp')), may hold values from -3 to 3
- key_matrix: bfloat16 [1536, 256], P(('seq', 'fsdp')), may hold values from -0.15625 to 0.15625
- key_bias_vector: bfloat16 [256], P(('seq', 'fsdp')), may hold values from -3 to 3
- value_matrix: bfloat16 [1536, 256], P(('seq', 'fsdp')), may hold values from -0.15625 to 0.15625
- value_bias_vector: bfloat16 [256], P(('seq', 'fsdp')), may hold values from -3 to 3
- output_weight: bfloat16 [1536, 1536], P(('seq', 'fsdp')), may hold values from -0.625 to 0.625
- mlp_gain: bfloat16 [1536], P(('seq', 'fsdp')), may hold values from 0.25 to 1.75
- gate_weight: bfloat16 [1536, 8960], P(('seq', 'fsdp')), may hold values from -0.15625 to 0.15625
- up_weight: bfloat16 [1536, 8960], P(('seq', 'fsdp')), may hold values from -0.15625 to 0.15625
- down_weight: bfloat16 [8960, 1536], P(('seq', 'fsdp')), may hold values from -0.0625 to 0.0625
- cotangent: bfloat16 [2, 2, 2048, 1536], P('fsdp', None, 'seq'), may hold values from -6 to 6
Outputs:
- outputs: bfloat16 [2, 2, 2048, 1536], P('fsdp', None, 'seq')
- input_grad: float32 [2, 2, 2048, 1536], P('fsdp', None, 'seq')
- attn_gain_grad: float32 [1536], P(('seq', 'fsdp'))
- query_weight_grad: float32 [1536, 1536], P(('seq', 'fsdp'))
- query_bias_grad: float32 [1536], P(('seq', 'fsdp'))
- key_weight_grad: float32 [1536, 256], P(('seq', 'fsdp'))
- key_bias_grad: float32 [256], P(('seq', 'fsdp'))
- value_weight_grad: float32 [1536, 256], P(('seq', 'fsdp'))
- value_bias_grad: float32 [256], P(('seq', 'fsdp'))
- output_weight_grad: float32 [1536, 1536], P(('seq', 'fsdp'))
- mlp_gain_grad: float32 [1536], P(('seq', 'fsdp'))
- gate_weight_grad: float32 [1536, 8960], P(('seq', 'fsdp'))
- up_weight_grad: float32 [1536, 8960], P(('seq', 'fsdp'))
- down_weight_grad: float32 [8960, 1536], P(('seq', 'fsdp'))
The draws below stay inside these ranges and needn't reach their ends.
Inputs may be any that keep to these rules, and one draw needn't show every extreme that they name: Each stream's 4 item lengths sum to 2048, and the longest is exactly half of 2048.
All inputs are finite; a program needn't handle non-finite values.
Results may differ from the reference program's by a relative error of at most 0.018.
Values may be sent and summed in bfloat16 or wider, within the bound.
A program may use at most 448 MiB of HBM per device.

```python
import math
import jax
import jax.numpy as jnp
import numpy as np
from jax import lax

MODEL_WIDTH = 1536
QUERY_HEADS = 12
KEY_VALUE_HEADS = 2
HEAD_WIDTH = 128
FF = 8960
MB = 2
SEGS = 4
STREAM = 2048
N_FSDP = 2


def steps_of(own_key, shape, cuts, low, largest):
    def one(dim, blocks):
        heights = jax.random.uniform(jax.random.fold_in(jax.random.fold_in(own_key, 6), dim), (blocks,), jnp.float32, low / len(cuts), largest / len(cuts))
        return jnp.repeat(jnp.exp(heights), shape[dim] // blocks).reshape((-1,) + (1,) * (len(shape) - dim - 1))

    loudness = one(*cuts[0])
    for cut in cuts[1:]:
        loudness = loudness * one(*cut)
    return loudness


def split_up(amount, total, most, skew):
    portions = [(1 << 20) // math.isqrt(standing ** skew) + 1 for standing in range(2, amount + 1)]
    spare, holding = total - most - (amount - 1), [1] * (amount - 1)
    while spare > 0:
        movable = [i for i in range(amount - 1) if holding[i] < most]
        mass, budget = sum([portions[i] for i in movable]), spare
        for i in movable:
            addition = min(most - holding[i], max(1, budget * portions[i] // mass), spare)
            holding[i] = holding[i] + addition
            spare = spare - addition
    return np.array([most] + holding)


def uneven(stream_key, number_of, total, reach, skew):
    if number_of == 2:
        one = jax.random.randint(stream_key, (), max(1, total - reach), min(reach, total - 1) + 1)
        return jnp.stack([one, total - one])
    sizes = jnp.asarray(split_up(number_of, total, reach, skew), jnp.int32)
    couples = (number_of - 1) // 2
    giver, taker = sizes[1:1 + 2 * couples:2], sizes[2:2 + 2 * couples:2]
    margin = jnp.minimum(giver - 1, reach - taker)
    moved = jax.random.randint(jax.random.fold_in(stream_key, 1), (couples,), 0, 1 << 20) % (margin + 1)
    sizes = sizes.at[1:1 + 2 * couples:2].set(giver - moved).at[2:2 + 2 * couples:2].set(taker + moved)
    return sizes[jax.random.permutation(jax.random.fold_in(stream_key, 2), number_of)]


def gaussian(key, dims, spread, reach, cuts=(), kind=jnp.bfloat16):
    drawn = spread * jax.random.normal(key, dims, jnp.float32)
    if cuts:
        drawn = drawn * steps_of(key, dims, cuts, -0.22, 0.18)
    return jnp.clip(drawn, -reach, reach).astype(kind)


def setup_inputs(seed: int = 0) -> dict:
    key_list = jax.random.split(jax.random.key(seed), 16)
    return {
        "inputs": gaussian(key_list[0], (N_FSDP, MB, STREAM, MODEL_WIDTH), 1.0, 6.0, ((0, 2), (2, 16))),
        "lengths": jax.vmap(lambda own: uneven(own, SEGS, STREAM, STREAM // 2, 2))(jax.random.split(key_list[1], N_FSDP * MB)).reshape((N_FSDP, MB, SEGS)).astype(jnp.int32),
        "attn_gain": jnp.clip(1.0 + 0.15 * jax.random.normal(key_list[2], (MODEL_WIDTH,), jnp.float32), 0.25, 1.75).astype(jnp.bfloat16),
        "query_weight": gaussian(key_list[3], (MODEL_WIDTH, MODEL_WIDTH), (MODEL_WIDTH // 4) ** -0.5, 0.3125, ((0, 32),)),
        "query_bias": gaussian(key_list[4], (MODEL_WIDTH,), 0.5, 3.0, ((0, 32),)),
        "key_matrix": gaussian(key_list[5], (MODEL_WIDTH, KEY_VALUE_HEADS * HEAD_WIDTH), MODEL_WIDTH ** -0.5, 0.15625, ((0, 32),)),
        "key_bias_vector": gaussian(key_list[6], (KEY_VALUE_HEADS * HEAD_WIDTH,), 0.5, 3.0, ((0, 32),)),
        "value_matrix": gaussian(key_list[7], (MODEL_WIDTH, KEY_VALUE_HEADS * HEAD_WIDTH), MODEL_WIDTH ** -0.5, 0.15625, ((0, 32),)),
        "value_bias_vector": gaussian(key_list[8], (KEY_VALUE_HEADS * HEAD_WIDTH,), 0.5, 3.0, ((0, 32),)),
        "output_weight": gaussian(key_list[9], (MODEL_WIDTH, MODEL_WIDTH), (MODEL_WIDTH // 16) ** -0.5, 0.625, ((0, 32),)),
        "mlp_gain": jnp.clip(1.0 + 0.15 * jax.random.normal(key_list[10], (MODEL_WIDTH,), jnp.float32), 0.25, 1.75).astype(jnp.bfloat16),
        "gate_weight": gaussian(key_list[11], (MODEL_WIDTH, FF), MODEL_WIDTH ** -0.5, 0.15625, ((0, 32),)),
        "up_weight": gaussian(key_list[12], (MODEL_WIDTH, FF), MODEL_WIDTH ** -0.5, 0.15625, ((0, 32),)),
        "down_weight": gaussian(key_list[13], (FF, MODEL_WIDTH), FF ** -0.5, 0.0625, ((0, 32),)),
        "cotangent": gaussian(key_list[14], (N_FSDP, MB, STREAM, MODEL_WIDTH), 1.0, 6.0, ((0, 2), (2, 16))),
    }


EPSILON = 1e-06
THETA = 10000.0
HIGHEST = lax.Precision.HIGHEST

@jax.custom_vjp
def low(v):
    return lax.optimization_barrier(v.astype(jnp.bfloat16)).astype(jnp.float32)

@jax.custom_vjp
def low_back(v):
    return v

def low_keep(v):
    return (low(v), None)

def low_pass(kept, grad):
    return (grad,)

def back_keep(v):
    return (v, None)

def back_low(kept, grad):
    return (low(grad),)
low.defvjp(low_keep, low_pass)
low_back.defvjp(back_keep, back_low)

def locate(item_lengths, positions_at):
    item_lengths = item_lengths.astype(jnp.int32)
    ends = jnp.cumsum(item_lengths).astype(jnp.int32)
    starts = (ends - item_lengths).astype(jnp.int32)
    segment_ids = lax.optimization_barrier(jnp.sum((ends[None, :] <= positions_at[:, None]).astype(jnp.int32), axis=1)).astype(jnp.int32)
    onehot = segment_ids[:, None] == jnp.arange(item_lengths.shape[0], dtype=jnp.int32)[None, :]
    first = lax.optimization_barrier(jnp.sum(jnp.where(onehot, starts[None, :], 0), axis=1)).astype(jnp.int32)
    return (segment_ids, (positions_at - first).astype(jnp.int32))

def rotary_tables(offsets, head_size):
    freqs = 1.0 / THETA ** (jnp.arange(0, head_size, 2, dtype=jnp.float32) / head_size)
    angles = offsets.astype(jnp.float32)[:, None] * freqs[None, :]
    cosine_table = jnp.concatenate([jnp.cos(angles), jnp.cos(angles)], axis=1)
    sine_table = jnp.concatenate([jnp.sin(angles), jnp.sin(angles)], axis=1)
    return (cosine_table, sine_table)

def apply_rotary(values, cosine_table, sine_table):
    half = values.shape[-1] // 2
    turned = jnp.concatenate([-values[..., half:], values[..., :half]], axis=-1)
    return values * cosine_table[:, None, :] + turned * sine_table[:, None, :]

def rms_scale(rows, gain):
    return rows * lax.rsqrt(lax.optimization_barrier(jnp.mean(rows * rows, axis=-1, keepdims=True)) + EPSILON) * gain

def layer(rows, item_lengths, weights):
    attn_gain, query_weight, query_bias, key_matrix, key_bias_vector, value_matrix, value_bias_vector, output_weight, mlp_gain, gate_weight, up_weight, down_weight = weights
    residual_stream = rows.shape[0]
    query_groups = QUERY_HEADS // KEY_VALUE_HEADS
    inv_root = HEAD_WIDTH ** (-0.5)
    index_value = jnp.arange(residual_stream, dtype=jnp.int32)
    segment_ids, offsets = locate(item_lengths, index_value)
    cosine_table, sine_table = rotary_tables(offsets, HEAD_WIDTH)
    normed = low(rms_scale(rows, attn_gain))
    query_unrotated = low_back(jnp.dot(normed, query_weight, precision=HIGHEST) + query_bias)
    key_unrotated = low_back(jnp.dot(normed, key_matrix, precision=HIGHEST) + key_bias_vector)
    value_reduced = low_back(low(jnp.dot(normed, value_matrix, precision=HIGHEST) + value_bias_vector))
    query_rotated = low(apply_rotary(query_unrotated.reshape(residual_stream, QUERY_HEADS, HEAD_WIDTH), cosine_table, sine_table)).reshape(residual_stream, KEY_VALUE_HEADS, query_groups, HEAD_WIDTH)
    key_rotated = low(apply_rotary(key_unrotated.reshape(residual_stream, KEY_VALUE_HEADS, HEAD_WIDTH), cosine_table, sine_table))
    value_head_rows = value_reduced.reshape(residual_stream, KEY_VALUE_HEADS, HEAD_WIDTH)
    block_slice = min(512, residual_stream)
    item_count = residual_stream // block_slice

    def attend_heads(pieces):
        query_block, seg_block, index_block = pieces
        scores = jnp.einsum('tghd,kgd->ghtk', query_block, key_rotated, precision=HIGHEST) * inv_root
        allowed = (segment_ids[None, :] == seg_block[:, None]) & (index_value[None, :] <= index_block[:, None])
        scores = low_back(jnp.where(allowed[None, None], scores, -1e+30))
        probs = low(jax.nn.softmax(scores, axis=-1))
        mixed = jnp.einsum('ghtk,kgd->tghd', probs, value_head_rows, precision=HIGHEST)
        return mixed.reshape(query_block.shape[0], QUERY_HEADS * HEAD_WIDTH)
    attended_rows = lax.map(jax.checkpoint(attend_heads), (query_rotated.reshape(item_count, block_slice, KEY_VALUE_HEADS, query_groups, HEAD_WIDTH), segment_ids.reshape(item_count, block_slice), index_value.reshape(item_count, block_slice)))
    attended_rows = low_back(low(attended_rows.reshape(residual_stream, QUERY_HEADS * HEAD_WIDTH)))
    branch = low_back(jnp.dot(attended_rows, output_weight, precision=HIGHEST))
    middle = rows + branch
    normed_two = low(rms_scale(middle, mlp_gain))
    gate_pre = low_back(jnp.dot(normed_two, gate_weight, precision=HIGHEST))
    up_pre = low_back(jnp.dot(normed_two, up_weight, precision=HIGHEST))
    hidden = low(jax.nn.silu(gate_pre) * up_pre)
    return middle + low_back(jnp.dot(hidden, down_weight, precision=HIGHEST))

def reference(inputs, lengths, attn_gain, query_weight, query_bias, key_matrix, key_bias_vector, value_matrix, value_bias_vector, output_weight, mlp_gain, gate_weight, up_weight, down_weight, cotangent):
    params = tuple((weight.astype(jnp.float32) for weight in (attn_gain, query_weight, query_bias, key_matrix, key_bias_vector, value_matrix, value_bias_vector, output_weight, mlp_gain, gate_weight, up_weight, down_weight)))
    totals = [jnp.zeros(weight.shape, jnp.float32) for weight in params]
    results = []
    input_grads = []
    for fsdp_index in range(N_FSDP):
        for micro_index in range(MB):
            rows = inputs[fsdp_index, micro_index].astype(jnp.float32)
            item_lengths = lengths[fsdp_index, micro_index]

            def forward(rows_in, *weights):
                return layer(rows_in, item_lengths, weights)
            out_rows, pull = jax.vjp(forward, rows, *params)
            grads = pull(cotangent[fsdp_index, micro_index].astype(jnp.float32))
            results.append(out_rows.astype(jnp.bfloat16))
            input_grads.append(grads[0])
            totals = [total + grad for total, grad in zip(totals, grads[1:])]
    residual_stream = inputs.shape[2]
    outputs = jnp.stack(results).reshape(N_FSDP, MB, residual_stream, MODEL_WIDTH)
    input_grad = jnp.stack(input_grads).reshape(N_FSDP, MB, residual_stream, MODEL_WIDTH)
    return (outputs, input_grad, totals[0], totals[1], totals[2], totals[3], totals[4], totals[5], totals[6], totals[7], totals[8], totals[9], totals[10], totals[11])
```

```python
import functools

import jax
import jax.numpy as jnp
from jax import lax
from jax.experimental import pallas as pl
from jax.experimental.pallas import tpu as pltpu
from jax.sharding import Mesh, PartitionSpec as P

QUERY_HEADS = 12
KEY_VALUE_HEADS = 2
HEAD_WIDTH = 128
EPSILON = 1e-06
THETA = 10000.0
GROUP = QUERY_HEADS // KEY_VALUE_HEADS
SCALE = HEAD_WIDTH ** (-0.5)
F32 = jnp.float32
BF16 = jnp.bfloat16
SWAP = [(0, 1), (1, 0)]


def locate(item_lengths, positions_at):
    ends = jnp.cumsum(item_lengths)
    starts = ends - item_lengths
    segment_ids = jnp.sum((ends[None, :] <= positions_at[:, None]).astype(jnp.int32), axis=1)
    onehot = segment_ids[:, None] == jnp.arange(item_lengths.shape[0], dtype=jnp.int32)[None, :]
    first = jnp.sum(jnp.where(onehot, starts[None, :], 0), axis=1)
    return (positions_at - first, first)


def rotary_tables(offsets, head_size):
    freqs = 1.0 / THETA ** (jnp.arange(0, head_size, 2, dtype=F32) / head_size)
    angles = offsets.astype(F32)[:, None] * freqs[None, :]
    cosine, sine = jnp.cos(angles), jnp.sin(angles)
    return (jnp.concatenate([cosine, cosine], axis=1), jnp.concatenate([sine, sine], axis=1))


def apply_rotary(values, cosine_table, sine_table):
    half = values.shape[-1] // 2
    turned = jnp.concatenate([-values[..., half:], values[..., :half]], axis=-1)
    return values * cosine_table[:, None, :] + turned * sine_table[:, None, :]


def inverse_rotary(grads, cosine_table, sine_table):
    half = grads.shape[-1] // 2
    scaled = grads * sine_table[:, None, :]
    turned = jnp.concatenate([scaled[..., half:], -scaled[..., :half]], axis=-1)
    return grads * cosine_table[:, None, :] + turned


def rms_forward(rows, gain):
    recip = lax.rsqrt(jnp.mean(rows * rows, axis=-1, keepdims=True) + EPSILON)
    return (rows * recip * gain, recip)


def rms_backward(rows, recip, gain, upstream):
    weighted = upstream * gain
    grad_rows = recip * weighted - rows * (recip * recip * recip) * jnp.mean(
        rows * weighted, axis=-1, keepdims=True
    )
    gain_grad = jnp.sum(upstream * rows * recip, axis=0)
    return (grad_rows, gain_grad)


def dot(left, right, dims, out=F32):
    return lax.dot_general(left, right, ((dims[0], dims[1]), ((), ())), preferred_element_type=out)


def rows_dot(left, right):
    return dot(left, right, ((0,), (0,)))


def cols_dot(left, right):
    return dot(left, right, ((1,), (1,)))


def mat_dot(left, right):
    return dot(left, right, ((1,), (0,)))


def attend_forward_kernel(meta, q_ref, k_ref, v_ref, span_ref, o_ref, lse_ref):
    rows = q_ref.shape[0]
    queries = jnp.concatenate(
        [q_ref[:, h * HEAD_WIDTH : (h + 1) * HEAD_WIDTH] for h in range(GROUP)], axis=0
    )
    first, last = span_ref[0:1, :], span_ref[1:2, :]
    wide = GROUP * rows
    local = lax.broadcasted_iota(jnp.int32, (rows, 1), 0)

    def step(block, carry):
        top, total, accum = carry
        slot = meta[2 + block]
        keys, values = k_ref[slot], v_ref[slot]
        scores = dot(keys, queries, ((1,), (1,))) * SCALE
        index = block * rows + local
        scores = jnp.where((index >= first) & (index <= last), scores, -1e30)
        new_top = jnp.maximum(top, jnp.max(scores, axis=0, keepdims=True))
        fade = jnp.exp(top - new_top)
        probs = jnp.exp(scores - new_top)
        total = total * fade + jnp.sum(probs, axis=0, keepdims=True)
        accum = accum * fade + dot(values, probs.astype(BF16), ((0,), (0,)))
        return (new_top, total, accum)

    top, total, accum = lax.fori_loop(
        meta[0],
        meta[1] + 1,
        step,
        (
            jnp.full((1, wide), -1e30, F32),
            jnp.zeros((1, wide), F32),
            jnp.zeros((HEAD_WIDTH, wide), F32),
        ),
    )
    attended = (accum / total).T.astype(BF16)
    for h in range(GROUP):
        o_ref[:, h * HEAD_WIDTH : (h + 1) * HEAD_WIDTH] = attended[h * rows : (h + 1) * rows]
    lse_ref[0] = top + jnp.log(total)


def attend_forward(meta, queries, stack, span):
    pieces, rows, _ = stack.shape
    width = queries.shape[1]
    part = width // KEY_VALUE_HEADS
    spec = pltpu.PrefetchScalarGridSpec(
        num_scalar_prefetch=1,
        grid=(KEY_VALUE_HEADS,),
        in_specs=[
            pl.BlockSpec((rows, part), lambda g, m: (0, g)),
            pl.BlockSpec((pieces, rows, HEAD_WIDTH), lambda g, m: (0, 0, g)),
            pl.BlockSpec((pieces, rows, HEAD_WIDTH), lambda g, m: (0, 0, KEY_VALUE_HEADS + g)),
            pl.BlockSpec((8, GROUP * rows), lambda g, m: (0, 0)),
        ],
        out_specs=[
            pl.BlockSpec((rows, part), lambda g, m: (0, g)),
            pl.BlockSpec((1, 1, GROUP * rows), lambda g, m: (g, 0, 0)),
        ],
    )
    return pl.pallas_call(
        attend_forward_kernel,
        grid_spec=spec,
        out_shape=(
            jax.ShapeDtypeStruct((rows, width), BF16),
            jax.ShapeDtypeStruct((KEY_VALUE_HEADS, 1, GROUP * rows), F32),
        ),
        cost_estimate=pl.CostEstimate(
            flops=4 * rows * rows * 6 * width, bytes_accessed=stack.size * 2, transcendentals=0
        ),
        name="attend_forward",
    )(meta, queries, stack, stack, span)


def attend_backward_kernel(
    meta, q_ref, do_ref, k_ref, v_ref, span_ref, lse_ref, dq_ref, dk_ref, dv_ref, p_ref, dp_ref
):
    rows = q_ref.shape[0]
    wide = GROUP * rows
    cols = [slice(h * HEAD_WIDTH, (h + 1) * HEAD_WIDTH) for h in range(GROUP)]
    queries = jnp.concatenate([q_ref[:, c] for c in cols], axis=0)
    grads = jnp.concatenate([do_ref[:, c] for c in cols], axis=0)
    first, last = span_ref[0:1, :], span_ref[1:2, :]
    lse = lse_ref[0]
    local = lax.broadcasted_iota(jnp.int32, (rows, 1), 0)
    low = meta[0]
    dk_ref[...] = jnp.zeros_like(dk_ref)
    dv_ref[...] = jnp.zeros_like(dv_ref)

    def collect(block, delta):
        slot = meta[2 + block]
        scores = dot(k_ref[slot], queries, ((1,), (1,))) * SCALE
        index = block * rows + local
        probs = jnp.where((index >= first) & (index <= last), jnp.exp(scores - lse), 0.0)
        grad_probs = dot(v_ref[slot], grads, ((1,), (1,)))
        p_ref[block - low] = probs
        dp_ref[block - low] = grad_probs
        return delta + jnp.sum(probs * grad_probs, axis=0, keepdims=True)

    delta = lax.fori_loop(low, meta[1] + 1, collect, jnp.zeros((1, wide), F32))

    def spread(block, accum):
        slot = meta[2 + block]
        probs = p_ref[block - low]
        grad_scores = (probs * (dp_ref[block - low] - delta)).astype(BF16)
        dk_ref[slot] = (mat_dot(grad_scores, queries) * SCALE).astype(BF16)
        dv_ref[slot] = mat_dot(probs.astype(BF16), grads).astype(BF16)
        return accum + dot(k_ref[slot], grad_scores, ((0,), (0,)))

    accum = lax.fori_loop(low, meta[1] + 1, spread, jnp.zeros((HEAD_WIDTH, wide), F32))
    grad_queries = (accum * SCALE).T
    for h in range(GROUP):
        dq_ref[:, cols[h]] = grad_queries[h * rows : (h + 1) * rows]


def attend_backward(meta, queries, grads, stack, span, lse):
    pieces, rows, _ = stack.shape
    width = queries.shape[1]
    part = width // KEY_VALUE_HEADS
    most = pieces // 2 + 1
    head = (pieces, rows, HEAD_WIDTH)
    spec = pltpu.PrefetchScalarGridSpec(
        num_scalar_prefetch=1,
        grid=(KEY_VALUE_HEADS,),
        in_specs=[
            pl.BlockSpec((rows, part), lambda g, m: (0, g)),
            pl.BlockSpec((rows, part), lambda g, m: (0, g)),
            pl.BlockSpec(head, lambda g, m: (0, 0, g)),
            pl.BlockSpec(head, lambda g, m: (0, 0, KEY_VALUE_HEADS + g)),
            pl.BlockSpec((8, GROUP * rows), lambda g, m: (0, 0)),
            pl.BlockSpec((1, 1, GROUP * rows), lambda g, m: (g, 0, 0)),
        ],
        out_specs=[
            pl.BlockSpec((rows, part), lambda g, m: (0, g)),
            pl.BlockSpec(head, lambda g, m: (0, 0, g)),
            pl.BlockSpec(head, lambda g, m: (0, 0, g)),
        ],
        scratch_shapes=[
            pltpu.VMEM((most, rows, GROUP * rows), F32),
            pltpu.VMEM((most, rows, GROUP * rows), F32),
        ],
    )
    kv_shape = jax.ShapeDtypeStruct((pieces, rows, KEY_VALUE_HEADS * HEAD_WIDTH), BF16)
    return pl.pallas_call(
        attend_backward_kernel,
        grid_spec=spec,
        out_shape=(jax.ShapeDtypeStruct((rows, width), F32), kv_shape, kv_shape),
        cost_estimate=pl.CostEstimate(
            flops=10 * rows * rows * 6 * width, bytes_accessed=stack.size * 4, transcendentals=0
        ),
        name="attend_backward",
    )(meta, queries, grads, stack, stack, span, lse)


def body(
    sizes,
    inputs,
    lengths,
    attn_gain,
    query_weight,
    query_bias,
    key_matrix,
    key_bias_vector,
    value_matrix,
    value_bias_vector,
    output_weight,
    mlp_gain,
    gate_weight,
    up_weight,
    down_weight,
    cotangent,
):
    far, fsdp = sizes
    micro, token_rows, width = inputs.shape[1:]
    shard = query_weight.shape[0]
    kv_width = key_matrix.shape[1]
    hidden_width = gate_weight.shape[1]
    devices = far * 8 * fsdp
    seq = far * 8
    ih, ip, iy, ic, ix = (lax.axis_index(name) for name in ("h", "p", "y", "c", "x"))
    me8 = (ip * 2 + iy) * 2 + ic
    me_seq = ih * 8 + me8

    def hop(array, axis, shift=1):
        if axis == "h":
            return lax.ppermute(array, "h", [(i, (i + shift) % far) for i in range(far)])
        return lax.ppermute(array, axis, SWAP)

    def gather_far(array):
        pair = jnp.concatenate([array, hop(array, "p")], axis=0)
        return jnp.concatenate([pair] + [hop(pair, "h", k) for k in range(1, far)], axis=0)

    def gather_seq(array):
        for axis in ("y", "c"):
            array = array if axis == "c" else gather_far(array)
            array = jnp.concatenate([array, hop(array, axis)], axis=0)
        return array

    def gather_all(array):
        array = gather_far(array)
        for axis in ("y", "x", "c"):
            array = jnp.concatenate([array, hop(array, axis)], axis=0)
        return array

    def halve(array, axis):
        half = array.shape[0] // 2
        received = hop(array[half:].astype(BF16), axis)
        return array[:half].astype(F32) + received.astype(F32)

    def reduce_seq(array):
        array = halve(array, "c").astype(BF16)
        array = halve(array, "y").astype(BF16)
        count = array.shape[0] // far
        total = array[:count].astype(F32)
        for k in range(1, far):
            total = total + hop(array[k * count : (k + 1) * count], "h", -k).astype(F32)
        return halve(total, "p")

    def pick(array, index, axis):
        return lax.dynamic_index_in_dim(array, index, axis, keepdims=False)

    def reduce_all(array):
        def fold(block, axis, name, index):
            sent = pick(block, 1 - index, axis)
            kept = pick(block, index, axis)
            return kept.astype(F32) + hop(sent, name).astype(F32)

        array = fold(array, 3, "c", ic).astype(BF16)
        array = fold(array, 3, "x", ix).astype(BF16)
        array = fold(array, 2, "y", iy).astype(BF16)
        array = fold(array, 1, "p", ip).astype(BF16)
        total = pick(array, ih, 0).astype(F32)
        for k in range(1, far):
            total = total + hop(pick(array, (ih + k) % far, 0), "h", k).astype(F32)
        return total

    def gather8(array):
        half = array.shape[0] // 2
        a, b = array[:half], array[half:]
        ay, bp = hop(a, "y"), hop(b, "p")
        a_far = hop(jnp.concatenate([a, ay], axis=0), "p")
        b_far = hop(jnp.concatenate([b, bp], axis=0), "y")
        quad = jnp.concatenate(
            [a, b, ay, b_far[:half], a_far[:half], bp, a_far[half:], b_far[half:]], axis=0
        )
        return jnp.concatenate([quad, hop(quad, "c")], axis=0)

    def reduce8(array):
        count = array.shape[0] // 16
        quad = halve(array, "c").reshape(2, 2, 2, count, width)
        a, b = quad[:, :, 0], quad[:, :, 1]
        a = a[0] + hop(a[1].astype(BF16), "p").astype(F32)
        b = b[:, 0] + hop(b[:, 1].astype(BF16), "y").astype(F32)
        a = a[0] + hop(a[1].astype(BF16), "y").astype(F32)
        b = b[0] + hop(b[1].astype(BF16), "p").astype(F32)
        return jnp.concatenate([a, b], axis=0)

    def exchange8(array):
        c = jnp.stack([array[:, :, 0], hop(array[:, :, 1], "c")], axis=2)
        y = jnp.stack([c[:, 0], hop(c[:, 1], "y")], axis=1)
        return jnp.stack([y[0], hop(y[1], "p")], axis=0)

    group_index = jnp.arange(8, dtype=jnp.int32) ^ me8
    seq_index = jnp.arange(seq, dtype=jnp.int32)
    seq_slot = (
        (((seq_index % 2) ^ ic) * 2 + ((seq_index // 2 % 2) ^ iy)) * far
        + (ih - seq_index // 8) % far
    ) * 2 + ((seq_index // 4 % 2) ^ ip)
    all_index = jnp.arange(devices, dtype=jnp.int32)
    dx, ds = all_index % fsdp, all_index // fsdp
    all_slot = (
        ((((ds % 2) ^ ic) * 2 + (dx ^ ix)) * 2 + ((ds // 2 % 2) ^ iy)) * far
        + (ih - ds // 8) % far
    ) * 2 + ((ds // 4 % 2) ^ ip)
    weight_slot = ((ds // 8) * fsdp + dx) * 8 + ((ds % 8) ^ me8)
    far_index = jnp.arange(devices, dtype=jnp.int32)
    back_slot = ((far_index // (8 * fsdp)) * 8 + ((far_index % 8) ^ me8)) * fsdp + (
        far_index // 8 % fsdp
    )

    def ordered(array, columns):
        return jnp.take(array.reshape(devices, -1, columns), all_slot, axis=0).reshape(-1, columns)

    vectors = jnp.concatenate(
        [attn_gain, query_bias, key_bias_vector, value_bias_vector, mlp_gain]
    ).astype(F32)[None]
    vectors = jnp.take(gather_all(vectors), all_slot, axis=0)
    cuts = [0]
    for part in (attn_gain, query_bias, key_bias_vector, value_bias_vector, mlp_gain):
        cuts.append(cuts[-1] + part.shape[0])
    gain_attn, b_query, b_key, b_value, gain_mlp = (
        vectors[:, cuts[i] : cuts[i + 1]].reshape(-1) for i in range(5)
    )
    w_kv = ordered(
        gather_all(jnp.concatenate([key_matrix, value_matrix], axis=1)), 2 * kv_width
    )
    w_query = ordered(gather_all(query_weight), width)

    rows = inputs[0].astype(F32).reshape(micro * token_rows, width)
    positions_at = me_seq * token_rows + jnp.arange(token_rows, dtype=jnp.int32)
    tables, spans, metas = [], [], []
    for number in range(micro):
        offsets, first = locate(lengths[0, number], positions_at)
        tables.append(rotary_tables(offsets, HEAD_WIDTH))
        spans.append(
            jnp.concatenate(
                [
                    jnp.tile(first, GROUP)[None],
                    jnp.tile(positions_at, GROUP)[None],
                    jnp.zeros((6, GROUP * token_rows), jnp.int32),
                ],
                axis=0,
            )
        )
        low = jnp.maximum(first[0] // token_rows, me_seq - seq // 2)
        metas.append(jnp.concatenate([jnp.stack([low, me_seq]), seq_slot]).astype(jnp.int32))
    cosine_table = jnp.concatenate([t[0] for t in tables], axis=0)
    sine_table = jnp.concatenate([t[1] for t in tables], axis=0)

    normed, recip_one = rms_forward(rows, gain_attn)
    normed_low = normed.astype(BF16)
    kv_pre = mat_dot(normed_low, w_kv)
    key_rotated = apply_rotary(
        (kv_pre[:, :kv_width] + b_key).reshape(-1, KEY_VALUE_HEADS, HEAD_WIDTH),
        cosine_table,
        sine_table,
    ).reshape(-1, kv_width)
    own_kv = jnp.concatenate([key_rotated, kv_pre[:, kv_width:] + b_value], axis=1).astype(BF16)
    stacks = [
        gather_seq(own_kv[m * token_rows : (m + 1) * token_rows]).reshape(
            seq, token_rows, 2 * kv_width
        )
        for m in range(micro)
    ]
    w_output = ordered(gather_all(output_weight), width)
    query_rotated = (
        apply_rotary(
            (mat_dot(normed_low, w_query) + b_query).reshape(-1, QUERY_HEADS, HEAD_WIDTH),
            cosine_table,
            sine_table,
        )
        .astype(BF16)
        .reshape(-1, width)
    )

    def slices(matrix):
        parts = matrix.reshape(shard, far, 8, hidden_width // (8 * far))
        return parts.transpose(2, 0, 1, 3).reshape(8, shard, hidden_width // 8)

    both = jnp.concatenate([slices(gate_weight), slices(up_weight)], axis=2)
    both = jnp.take(both, group_index, axis=0).reshape(2, 2, 2, shard, -1)
    both = exchange8(both).reshape(8 * shard, -1)
    slice_width = hidden_width // 8

    def whole(part):
        part = lax.all_gather(part, ("h", "x"), axis=0, tiled=True)
        part = jnp.take(part.reshape(devices, shard, slice_width), weight_slot, axis=0)
        return part.reshape(-1, slice_width)

    w_gate, w_up = whole(both[:, :slice_width]), whole(both[:, slice_width:])
    w_down = lax.all_gather(down_weight, ("h", "x"), axis=0, tiled=True)
    upstream_low = [cotangent[0, m] for m in range(micro)]
    upstream_all = [gather8(upstream_low[m]) for m in range(micro)]

    kept = []
    for m in range(micro):
        part = slice(m * token_rows, (m + 1) * token_rows)
        attended, lse = attend_forward(metas[m], query_rotated[part], stacks[m], spans[m])
        middle = rows[part] + mat_dot(attended, w_output)
        normed_two, recip_two = rms_forward(middle, gain_mlp)
        kept.append((attended, lse, middle, recip_two, gather8(normed_two.astype(BF16))))

    results, grads_two = [], []
    g_gate = g_up = g_down = 0.0
    for m in range(micro):
        middle, recip_two, tokens = kept[m][2:]
        gate_pre = mat_dot(tokens, w_gate)
        up_pre = mat_dot(tokens, w_up)
        sigma = jax.nn.sigmoid(gate_pre)
        activated = gate_pre * sigma
        hidden = (activated * up_pre).astype(BF16)
        grad_hidden = cols_dot(upstream_all[m], w_down)
        grad_gate = (grad_hidden * up_pre * sigma * (1.0 + gate_pre * (1.0 - sigma))).astype(BF16)
        grad_up = (grad_hidden * activated).astype(BF16)
        grads_two.append(reduce8(cols_dot(grad_gate, w_gate) + cols_dot(grad_up, w_up)))
        results.append((middle + reduce8(mat_dot(hidden, w_down))).astype(BF16))
        g_gate = g_gate + rows_dot(tokens, grad_gate)
        g_up = g_up + rows_dot(tokens, grad_up)
        g_down = g_down + rows_dot(hidden, upstream_all[m])

    gain_mlp_sum = 0.0
    grad_middles, grad_branches, grad_queries, grad_kvs = [], [], [], []
    for m in range(micro):
        attended, lse, middle, recip_two, _ = kept[m]
        part = slice(m * token_rows, (m + 1) * token_rows)
        grad_norm, gain_part = rms_backward(middle, recip_two, gain_mlp, grads_two[m])
        gain_mlp_sum = gain_mlp_sum + gain_part
        grad_middle = upstream_low[m].astype(F32) + grad_norm
        grad_branch = grad_middle.astype(BF16)
        grad_attended = cols_dot(grad_branch, w_output).astype(BF16)
        grad_query, grad_keys, grad_values = attend_backward(
            metas[m], query_rotated[part], grad_attended, stacks[m], spans[m], lse
        )
        stacked = jnp.concatenate([grad_keys, grad_values], axis=2)
        grad_kvs.append(reduce_seq(stacked.reshape(seq * token_rows, 2 * kv_width)))
        grad_middles.append(grad_middle)
        grad_branches.append(grad_branch)
        grad_queries.append(grad_query)

    blocks = (far, 2, 2, 2, fsdp, shard)
    g_output = rows_dot(
        jnp.concatenate([kept[m][0] for m in range(micro)], axis=0),
        jnp.concatenate(grad_branches, axis=0),
    ).astype(BF16)
    output_part = reduce_all(g_output.reshape(blocks + (width,)))

    grad_middle = jnp.concatenate(grad_middles, axis=0)
    grad_query = (
        inverse_rotary(
            jnp.concatenate(grad_queries, axis=0).reshape(-1, QUERY_HEADS, HEAD_WIDTH),
            cosine_table,
            sine_table,
        )
        .reshape(-1, width)
        .astype(BF16)
    )
    grad_kv = jnp.concatenate(grad_kvs, axis=0)
    grad_key = inverse_rotary(
        grad_kv[:, :kv_width].reshape(-1, KEY_VALUE_HEADS, HEAD_WIDTH), cosine_table, sine_table
    ).reshape(-1, kv_width)
    grad_kv = jnp.concatenate([grad_key, grad_kv[:, kv_width:]], axis=1).astype(BF16)
    grad_normed = cols_dot(grad_query, w_query) + cols_dot(grad_kv, w_kv)
    grad_rows, gain_attn_sum = rms_backward(rows, recip_one, gain_attn, grad_normed)
    input_grad = grad_middle + grad_rows
    query_part = reduce_all(
        rows_dot(normed_low, grad_query).astype(BF16).reshape(blocks + (width,))
    )
    kv_part = reduce_all(
        rows_dot(normed_low, grad_kv).astype(BF16).reshape(blocks + (2 * kv_width,))
    )
    bias_query = jnp.sum(grad_query.astype(F32), axis=0)
    bias_kv = jnp.sum(grad_kv.astype(F32), axis=0)
    vector_sums = jnp.concatenate(
        [
            v.reshape(devices, -1)
            for v in (
                gain_attn_sum,
                bias_query,
                bias_kv[:kv_width],
                bias_kv[kv_width:],
                gain_mlp_sum,
            )
        ],
        axis=1,
    )
    vector_part = lax.psum_scatter(
        vector_sums, ("h", "p", "y", "c", "x"), scatter_dimension=0, tiled=True
    )[0]

    def scattered(grad):
        grad = jnp.take(
            grad.astype(BF16).reshape(devices, shard, slice_width), back_slot, axis=0
        )
        return lax.psum_scatter(
            grad.reshape(devices * shard, slice_width), ("h", "x"), scatter_dimension=0, tiled=True
        )

    down_part = lax.psum_scatter(
        g_down.astype(BF16), ("h", "x"), scatter_dimension=0, tiled=True
    ).astype(F32)
    both = jnp.concatenate([scattered(g_gate), scattered(g_up)], axis=1)
    both = exchange8(both.reshape(2, 2, 2, shard, -1)).reshape(8, shard, -1)
    both = jnp.take(both, group_index, axis=0)

    def joined(part):
        part = part.reshape(8, shard, far, -1).transpose(1, 2, 0, 3)
        return part.reshape(shard, hidden_width).astype(F32)

    return (
        jnp.stack(results)[None],
        input_grad.reshape(1, micro, token_rows, width),
        vector_part[cuts[0] : cuts[1]],
        query_part,
        vector_part[cuts[1] : cuts[2]],
        kv_part[:, :kv_width],
        vector_part[cuts[2] : cuts[3]],
        kv_part[:, kv_width:],
        vector_part[cuts[3] : cuts[4]],
        output_part,
        vector_part[cuts[4] : cuts[5]],
        joined(both[:, :, :slice_width]),
        joined(both[:, :, slice_width:]),
        down_part,
    )


def solution(mesh):
    fsdp = mesh.shape["fsdp"]
    far = mesh.shape["seq"] // 8
    inner = Mesh(mesh.devices.reshape(far, 2, 2, 2, fsdp), ("h", "p", "y", "c", "x"))
    seq = ("h", "p", "y", "c")
    every = seq + ("x",)
    tokens = P("x", None, seq, None)
    matrix, vector = P(every, None), P(every)
    in_specs = (
        tokens,
        P("x", None, None),
        vector,
        matrix,
        vector,
        matrix,
        vector,
        matrix,
        vector,
        matrix,
        vector,
        matrix,
        matrix,
        matrix,
        tokens,
    )
    out_specs = (
        tokens,
        tokens,
        vector,
        matrix,
        vector,
        matrix,
        vector,
        matrix,
        vector,
        matrix,
        vector,
        matrix,
        matrix,
        matrix,
    )
    return jax.shard_map(
        functools.partial(body, (far, fsdp)),
        mesh=inner,
        in_specs=in_specs,
        out_specs=out_specs,
        check_vma=False,
    )
```

```python
import functools

import jax
import jax.numpy as jnp
from jax import lax
from jax.experimental import pallas as pl
from jax.experimental.pallas import tpu as pltpu
from jax.sharding import Mesh, PartitionSpec as P

QUERY_HEADS = 12
KEY_VALUE_HEADS = 2
HEAD_WIDTH = 128
EPSILON = 1e-06
THETA = 10000.0
GROUP = QUERY_HEADS // KEY_VALUE_HEADS
SCALE = HEAD_WIDTH ** (-0.5)
F32 = jnp.float32
BF16 = jnp.bfloat16
SWAP = [(0, 1), (1, 0)]


def locate(item_lengths, positions_at):
    ends = jnp.cumsum(item_lengths)
    starts = ends - item_lengths
    segment_ids = jnp.sum((ends[None, :] <= positions_at[:, None]).astype(jnp.int32), axis=1)
    onehot = segment_ids[:, None] == jnp.arange(item_lengths.shape[0], dtype=jnp.int32)[None, :]
    first = jnp.sum(jnp.where(onehot, starts[None, :], 0), axis=1)
    return (positions_at - first, first)


def rotary_tables(offsets, head_size):
    freqs = 1.0 / THETA ** (jnp.arange(0, head_size, 2, dtype=F32) / head_size)
    angles = offsets.astype(F32)[:, None] * freqs[None, :]
    cosine, sine = jnp.cos(angles), jnp.sin(angles)
    return (jnp.concatenate([cosine, cosine], axis=1), jnp.concatenate([sine, sine], axis=1))


def apply_rotary(values, cosine_table, sine_table):
    half = values.shape[-1] // 2
    turned = jnp.concatenate([-values[..., half:], values[..., :half]], axis=-1)
    return values * cosine_table[:, None, :] + turned * sine_table[:, None, :]


def inverse_rotary(grads, cosine_table, sine_table):
    half = grads.shape[-1] // 2
    scaled = grads * sine_table[:, None, :]
    turned = jnp.concatenate([scaled[..., half:], -scaled[..., :half]], axis=-1)
    return grads * cosine_table[:, None, :] + turned


def rms_forward(rows, gain):
    recip = lax.rsqrt(jnp.mean(rows * rows, axis=-1, keepdims=True) + EPSILON)
    return (rows * recip * gain, recip)


def rms_backward(rows, recip, gain, upstream):
    weighted = upstream * gain
    grad_rows = recip * weighted - rows * (recip * recip * recip) * jnp.mean(
        rows * weighted, axis=-1, keepdims=True
    )
    gain_grad = jnp.sum(upstream * rows * recip, axis=0)
    return (grad_rows, gain_grad)


def dot(left, right, dims, out=F32):
    return lax.dot_general(left, right, ((dims[0], dims[1]), ((), ())), preferred_element_type=out)


def rows_dot(left, right):
    return dot(left, right, ((0,), (0,)))


def cols_dot(left, right):
    return dot(left, right, ((1,), (1,)))


def mat_dot(left, right):
    return dot(left, right, ((1,), (0,)))


def attend_forward_kernel(meta, q_ref, k_ref, v_ref, span_ref, o_ref, lse_ref):
    rows = q_ref.shape[0]
    queries = jnp.concatenate(
        [q_ref[:, h * HEAD_WIDTH : (h + 1) * HEAD_WIDTH] for h in range(GROUP)], axis=0
    )
    first, last = span_ref[0:1, :], span_ref[1:2, :]
    wide = GROUP * rows
    local = lax.broadcasted_iota(jnp.int32, (rows, 1), 0)

    def step(block, carry):
        top, total, accum = carry
        keys, values = k_ref[block], v_ref[block]
        scores = dot(keys, queries, ((1,), (1,))) * SCALE
        index = block * rows + local
        scores = jnp.where((index >= first) & (index <= last), scores, -1e30)
        new_top = jnp.maximum(top, jnp.max(scores, axis=0, keepdims=True))
        fade = jnp.exp(top - new_top)
        probs = jnp.exp(scores - new_top)
        total = total * fade + jnp.sum(probs, axis=0, keepdims=True)
        accum = accum * fade + dot(values, probs.astype(BF16), ((0,), (0,)))
        return (new_top, total, accum)

    top, total, accum = lax.fori_loop(
        meta[0],
        meta[1] + 1,
        step,
        (
            jnp.full((1, wide), -1e30, F32),
            jnp.zeros((1, wide), F32),
            jnp.zeros((HEAD_WIDTH, wide), F32),
        ),
    )
    attended = (accum / total).T.astype(BF16)
    for h in range(GROUP):
        o_ref[:, h * HEAD_WIDTH : (h + 1) * HEAD_WIDTH] = attended[h * rows : (h + 1) * rows]
    lse_ref[0] = top + jnp.log(total)


def attend_forward(meta, queries, stack, span):
    pieces, rows, _ = stack.shape
    width = queries.shape[1]
    part = width // KEY_VALUE_HEADS
    spec = pltpu.PrefetchScalarGridSpec(
        num_scalar_prefetch=1,
        grid=(KEY_VALUE_HEADS,),
        in_specs=[
            pl.BlockSpec((rows, part), lambda g, m: (0, g)),
            pl.BlockSpec((pieces, rows, HEAD_WIDTH), lambda g, m: (0, 0, g)),
            pl.BlockSpec((pieces, rows, HEAD_WIDTH), lambda g, m: (0, 0, KEY_VALUE_HEADS + g)),
            pl.BlockSpec((8, GROUP * rows), lambda g, m: (0, 0)),
        ],
        out_specs=[
            pl.BlockSpec((rows, part), lambda g, m: (0, g)),
            pl.BlockSpec((1, 1, GROUP * rows), lambda g, m: (g, 0, 0)),
        ],
    )
    return pl.pallas_call(
        attend_forward_kernel,
        grid_spec=spec,
        out_shape=(
            jax.ShapeDtypeStruct((rows, width), BF16),
            jax.ShapeDtypeStruct((KEY_VALUE_HEADS, 1, GROUP * rows), F32),
        ),
        cost_estimate=pl.CostEstimate(
            flops=4 * rows * rows * 6 * width, bytes_accessed=stack.size * 2, transcendentals=0
        ),
        name="attend_forward",
    )(meta, queries, stack, stack, span)


def attend_backward_kernel(
    meta, q_ref, do_ref, k_ref, v_ref, span_ref, lse_ref, dq_ref, dk_ref, dv_ref, p_ref, dp_ref
):
    rows = q_ref.shape[0]
    wide = GROUP * rows
    cols = [slice(h * HEAD_WIDTH, (h + 1) * HEAD_WIDTH) for h in range(GROUP)]
    queries = jnp.concatenate([q_ref[:, c] for c in cols], axis=0)
    grads = jnp.concatenate([do_ref[:, c] for c in cols], axis=0)
    first, last = span_ref[0:1, :], span_ref[1:2, :]
    lse = lse_ref[0]
    local = lax.broadcasted_iota(jnp.int32, (rows, 1), 0)
    low = meta[0]
    dk_ref[...] = jnp.zeros_like(dk_ref)
    dv_ref[...] = jnp.zeros_like(dv_ref)

    def collect(block, delta):
        scores = dot(k_ref[block], queries, ((1,), (1,))) * SCALE
        index = block * rows + local
        probs = jnp.where((index >= first) & (index <= last), jnp.exp(scores - lse), 0.0)
        grad_probs = dot(v_ref[block], grads, ((1,), (1,)))
        p_ref[block - low] = probs
        dp_ref[block - low] = grad_probs
        return delta + jnp.sum(probs * grad_probs, axis=0, keepdims=True)

    delta = lax.fori_loop(low, meta[1] + 1, collect, jnp.zeros((1, wide), F32))

    def spread(block, accum):
        probs = p_ref[block - low]
        grad_scores = (probs * (dp_ref[block - low] - delta)).astype(BF16)
        dk_ref[block] = (mat_dot(grad_scores, queries) * SCALE).astype(BF16)
        dv_ref[block] = mat_dot(probs.astype(BF16), grads).astype(BF16)
        return accum + dot(k_ref[block], grad_scores, ((0,), (0,)))

    accum = lax.fori_loop(low, meta[1] + 1, spread, jnp.zeros((HEAD_WIDTH, wide), F32))
    grad_queries = (accum * SCALE).T
    for h in range(GROUP):
        dq_ref[:, cols[h]] = grad_queries[h * rows : (h + 1) * rows]


def attend_backward(meta, queries, grads, stack, span, lse):
    pieces, rows, _ = stack.shape
    width = queries.shape[1]
    part = width // KEY_VALUE_HEADS
    most = pieces // 2 + 1
    head = (pieces, rows, HEAD_WIDTH)
    spec = pltpu.PrefetchScalarGridSpec(
        num_scalar_prefetch=1,
        grid=(KEY_VALUE_HEADS,),
        in_specs=[
            pl.BlockSpec((rows, part), lambda g, m: (0, g)),
            pl.BlockSpec((rows, part), lambda g, m: (0, g)),
            pl.BlockSpec(head, lambda g, m: (0, 0, g)),
            pl.BlockSpec(head, lambda g, m: (0, 0, KEY_VALUE_HEADS + g)),
            pl.BlockSpec((8, GROUP * rows), lambda g, m: (0, 0)),
            pl.BlockSpec((1, 1, GROUP * rows), lambda g, m: (g, 0, 0)),
        ],
        out_specs=[
            pl.BlockSpec((rows, part), lambda g, m: (0, g)),
            pl.BlockSpec(head, lambda g, m: (0, 0, g)),
            pl.BlockSpec(head, lambda g, m: (0, 0, g)),
        ],
        scratch_shapes=[
            pltpu.VMEM((most, rows, GROUP * rows), F32),
            pltpu.VMEM((most, rows, GROUP * rows), F32),
        ],
    )
    kv_shape = jax.ShapeDtypeStruct((pieces, rows, KEY_VALUE_HEADS * HEAD_WIDTH), BF16)
    return pl.pallas_call(
        attend_backward_kernel,
        grid_spec=spec,
        out_shape=(jax.ShapeDtypeStruct((rows, width), F32), kv_shape, kv_shape),
        cost_estimate=pl.CostEstimate(
            flops=10 * rows * rows * 6 * width, bytes_accessed=stack.size * 4, transcendentals=0
        ),
        name="attend_backward",
    )(meta, queries, grads, stack, stack, span, lse)


MESH = pl.DeviceIdType.MESH
ANY = pl.BlockSpec(memory_space=pl.ANY)


class Copies:
    def __init__(self, send_sems, recv_sems):
        self.send_sems, self.recv_sems, self.started = send_sems, recv_sems, []

    def start(self, source, target, device):
        number = len(self.started)
        copy = pltpu.make_async_remote_copy(
            src_ref=source,
            dst_ref=target,
            send_sem=self.send_sems.at[number],
            recv_sem=self.recv_sems.at[number],
            device_id=device,
            device_id_type=MESH,
        )
        copy.start()
        self.started.append(copy)
        return copy


def greet(devices):
    barrier = pltpu.get_barrier_semaphore()
    for device in devices:
        pl.semaphore_signal(barrier, inc=1, device_id=device, device_id_type=MESH)
    pl.semaphore_wait(barrier, len(devices))


def other_h(far, k):
    return {"h": lax.rem(lax.axis_index("h") + k, far)}


def flip(*axes):
    return {axis: 1 - lax.axis_index(axis) for axis in axes}


def gather_steps(kind, far, copies, source, out, local):
    ih, ip, iy, ic, ix = (lax.axis_index(name) for name in ("h", "p", "y", "c", "x"))
    every = kind == "all"

    def block(h, p, y=iy, x=ix):
        return out.at[h, p, y, ic, x] if every else out.at[h, p, y, ic]

    local.start()
    pieces = [(lax.rem(ih - k + far, far), p) for p in (ip, 1 - ip) for k in range(far)]
    count = len(pieces)
    arrivals, plane, cross, core = [None] * count, [None] * count, [None] * count, [None] * count
    columns = source.shape[-1]
    half = columns // 2 if columns % 256 == 0 else columns

    def cut(ref, first):
        if half == columns:
            return ref
        return ref.at[:, pl.ds(0 if first else half, half)]

    for k in range(1, far):
        arrivals[k] = copies.start(source, block(ih, ip), other_h(far, k))
    for step in range(count + 3):
        if step < count:
            if arrivals[step] is not None:
                arrivals[step].wait_recv()
            h, p = pieces[step]
            held = source if step == 0 else block(h, p)
            if step < far:
                arrivals[far + step] = copies.start(held, block(h, p), flip("p"))
            plane[step] = [copies.start(held, block(h, p), flip("y"))]
            if every:
                plane[step].append(copies.start(held, block(h, p), flip("x")))
        if 0 <= step - 1 < count:
            h, p = pieces[step - 1]
            for copy in plane[step - 1]:
                copy.wait_recv()
            cross[step - 1] = []
            if every:
                ref = cut(block(h, p, x=1 - ix), True)
                cross[step - 1].append(copies.start(ref, ref, flip("y")))
                if half < columns:
                    ref = cut(block(h, p, y=1 - iy), False)
                    cross[step - 1].append(copies.start(ref, ref, flip("x")))
        if 0 <= step - 2 < count:
            h, p = pieces[step - 2]
            for copy in cross[step - 2]:
                copy.wait_recv()
            if step == 2:
                local.wait()
            ref = out.at[h, p, :, ic]
            core[step - 2] = copies.start(ref, ref, flip("c"))
        if 0 <= step - 3 < count:
            core[step - 3].wait_recv()
        yield


def group_steps(far, copies, source, out, local):
    ip, iy, ic = (lax.axis_index(name) for name in ("p", "y", "c"))
    half = source.shape[0] // 2
    top, low = pl.ds(0, half), pl.ds(half, half)

    def rows(p, y, part):
        return out.at[p, y, ic, part]

    def forward(ref, axis):
        return copies.start(ref, ref, flip(axis))

    local.start()
    first = [
        copies.start(source.at[top], rows(ip, iy, top), flip("y")),
        copies.start(source.at[low], rows(ip, iy, low), flip("p")),
    ]
    second = [
        copies.start(source.at[top], rows(ip, iy, top), flip("p")),
        copies.start(source.at[low], rows(ip, iy, low), flip("y")),
    ]
    core = [copies.start(source, out.at[ip, iy, ic], flip("c"))]
    yield
    first[0].wait_recv()
    second.append(forward(rows(ip, 1 - iy, top), "p"))
    core.append(forward(rows(ip, 1 - iy, top), "c"))
    first[1].wait_recv()
    second.append(forward(rows(1 - ip, iy, low), "y"))
    core.append(forward(rows(1 - ip, iy, low), "c"))
    yield
    for copy, p, y, part in (
        (second[0], 1 - ip, iy, top),
        (second[1], ip, 1 - iy, low),
        (second[2], 1 - ip, 1 - iy, top),
        (second[3], 1 - ip, 1 - iy, low),
    ):
        copy.wait_recv()
        core.append(forward(rows(p, y, part), "c"))
    yield
    for copy in core:
        copy.wait_recv()
    local.wait()


def pair_steps(far, copies, source, out, local, place):
    ih, ix = lax.axis_index("h"), lax.axis_index("x")
    local.start()
    arrived = [copies.start(source, place(ih, ix), other_h(far, k)) for k in range(1, far)]
    sent = [copies.start(source, place(ih, ix), flip("x"))]
    yield
    for k in range(1, far):
        arrived[k - 1].wait_recv()
        ref = place(lax.rem(ih - k + far, far), ix)
        sent.append(copies.start(ref, ref, flip("x")))
        yield
    for _ in range(far + 1):
        yield
    for copy in sent:
        copy.wait_recv()
    local.wait()


def spread_steps(far, copies, source, out, local):
    ip, iy, ic = (lax.axis_index(name) for name in ("p", "y", "c"))
    me = (ip * 2 + iy) * 2 + ic
    local.start()
    started = []
    for j in (1, 2, 4, 3, 5, 6, 7):
        p = 1 - ip if j & 4 else ip
        y = 1 - iy if j & 2 else iy
        c = 1 - ic if j & 1 else ic
        started.append(
            copies.start(source.at[(p * 2 + y) * 2 + c], out.at[me], {"p": p, "y": y, "c": c})
        )
    for _ in range(2 * far + 2):
        yield
    for copy in started:
        copy.wait_recv()
    local.wait()
    yield


def move_kernel(kinds, far, *refs):
    count = len(kinds)
    sources, outs = refs[:count], refs[count : 2 * count]
    send_sems, recv_sems, local_sems = refs[2 * count :]
    ih, ip, iy, ic, ix = (lax.axis_index(name) for name in ("h", "p", "y", "c", "x"))
    partners = [flip("p"), flip("y"), flip("c")]
    if set(kinds) - {"spread", "group"}:
        partners += [other_h(far, k) for k in range(1, far)]
    if "all" in kinds or "pair" in kinds or "pair8" in kinds:
        partners.append(flip("x"))
    if "spread" in kinds:
        partners += [flip("p", "y"), flip("p", "c"), flip("y", "c"), flip("p", "y", "c")]
    greet(partners)
    copies = Copies(send_sems, recv_sems)
    running = []
    for i, kind in enumerate(kinds):
        if kind == "spread":
            me = (ip * 2 + iy) * 2 + ic
            local = pltpu.make_async_copy(sources[i].at[me], outs[i].at[me], local_sems.at[i])
            running.append(spread_steps(far, copies, sources[i], outs[i], local))
        elif kind == "group":
            place = outs[i].at[ip, iy, ic]
            local = pltpu.make_async_copy(sources[i], place, local_sems.at[i])
            running.append(group_steps(far, copies, sources[i], outs[i], local))
        elif kind in ("pair", "pair8"):

            def place(h, x, out=outs[i], wide=kind == "pair8"):
                return out.at[h, :, x] if wide else out.at[h, x]

            local = pltpu.make_async_copy(sources[i], place(ih, ix), local_sems.at[i])
            running.append(pair_steps(far, copies, sources[i], outs[i], local, place))
        else:
            place = (ih, ip, iy, ic, ix) if kind == "all" else (ih, ip, iy, ic)
            local = pltpu.make_async_copy(sources[i], outs[i].at[place], local_sems.at[i])
            running.append(gather_steps(kind, far, copies, sources[i], outs[i], local))
    while running:
        running = [job for job in running if next(job, "end") != "end"]
    for copy in copies.started:
        copy.wait_send()


def move(name, number, far, fsdp, kinds, arrays):
    shapes, total = [], 0
    pieces = 2 * far
    for kind, array in zip(kinds, arrays):
        if kind == "all":
            lead, total = (far, 2, 2, 2, fsdp), total + (far - 1) + far + 5 * pieces
        elif kind == "seq":
            lead, total = (far, 2, 2, 2), total + (far - 1) + far + 2 * pieces
        elif kind == "group":
            lead, total = (2, 2, 2), total + 13
        elif kind == "pair":
            lead, total = (far, fsdp), total + 2 * far - 1
        elif kind == "pair8":
            lead, total = (far, 8, fsdp), total + 2 * far - 1
        else:
            lead, total = (), total + 7
        tail = array.shape[1:] if kind == "pair8" else array.shape
        shapes.append(jax.ShapeDtypeStruct(lead + tail, array.dtype))
    size = sum(s.size * s.dtype.itemsize for s in shapes)
    return pl.pallas_call(
        functools.partial(move_kernel, kinds, far),
        out_shape=tuple(shapes),
        in_specs=[ANY] * len(arrays),
        out_specs=tuple([ANY] * len(arrays)),
        scratch_shapes=[
            pltpu.SemaphoreType.DMA((total,)),
            pltpu.SemaphoreType.DMA((total,)),
            pltpu.SemaphoreType.DMA((len(arrays),)),
        ],
        compiler_params=pltpu.CompilerParams(collective_id=number, has_side_effects=True),
        cost_estimate=pl.CostEstimate(flops=0, bytes_accessed=8 * size, transcendentals=0),
        name=name,
    )(*arrays)


def reduce_plan(kind, far, fsdp, tail):
    rows, columns = tail
    if kind == "group":
        half = rows // 2
        return ("p", "y"), [
            ((pl.ds(0, half), slice(None)), (half, columns), ("p", "y")),
            ((pl.ds(half, half), slice(None)), (half, columns), ("y", "p")),
        ]
    if kind == "seq":
        return ("h", "p", "y"), [((slice(None), slice(None)), tail, ("y", "p", "h"))]
    names = ("h", "p", "y", "x")
    if columns % 256:
        return names, [((slice(None), slice(None)), tail, ("x", "y", "p", "h"))]
    half = columns // 2
    return names, [
        ((slice(None), pl.ds(0, half)), (rows, half), ("x", "y", "p", "h")),
        ((slice(None), pl.ds(half, half)), (rows, half), ("y", "x", "p", "h")),
    ]


def reduce_shapes(kind, far, fsdp, tail, dtype):
    length = {"h": far, "p": 2, "y": 2, "x": fsdp}
    names, parts = reduce_plan(kind, far, fsdp, tail)
    shapes = []
    for _, small, order in parts:
        left = list(names)
        full = tuple(length[n] for n in left) + small
        shapes += [full, full]
        for axis in order:
            left.remove(axis)
            lead = tuple(length[n] for n in left) + small
            shapes.append((far - 1,) + lead if axis == "h" else lead)
    return shapes


def reduce_steps(kind, far, fsdp, copies, source, out, scratch, local_sem):
    place = {name: lax.axis_index(name) for name in ("h", "p", "y", "x")}
    ic = lax.axis_index("c")
    length = {"h": far, "p": 2, "y": 2, "x": fsdp}
    core_dim = {"group": 2, "seq": 3, "all": 3}[kind]
    names, parts = reduce_plan(kind, far, fsdp, out.shape)
    jobs, position = [], 0
    for cut, small, order in parts:
        count = 2 + len(order)
        jobs.append((cut, small, order, scratch[position : position + count]))
        position += count

    def view(c, cut):
        lead = [slice(None)] * core_dim + [c] + [slice(None)] * (len(names) - core_dim)
        return source.at[tuple(lead) + cut]

    def add(sums, brought, fixed, left, target=None, also=()):
        sizes = [1 if n in fixed_now else length[n] for n in left for fixed_now in (also,)]
        total = 1
        for size in sizes:
            total *= size

        def one(number, _):
            index, rest = {}, number
            for n, size in reversed(list(zip(left, sizes))):
                index[n] = also[n] if n in also else rest % size
                rest = rest // size
            whole = tuple(fixed[n] if n in fixed else index[n] for n in names)
            value = sums[whole].astype(F32) + brought[tuple(index[n] for n in left)].astype(F32)
            if target is None:
                sums[whole] = value.astype(sums.dtype)
            else:
                target(value)
            return 0

        if total == 1:
            one(0, 0)
        else:
            lax.fori_loop(0, total, one, 0)

    loads, sent = [], []
    for i, (cut, small, order, refs) in enumerate(jobs):
        loads.append(pltpu.make_async_copy(view(ic, cut), refs[0], local_sem.at[i]))
        loads[i].start()
        sent.append(copies.start(view(1 - ic, cut), refs[1], flip("c")))
    yield
    for stage in range(len(jobs[0][2]) + 1):
        for i, (cut, small, order, refs) in enumerate(jobs):
            sums, brought = refs[0], refs[1 + stage]
            done = order[:stage]
            left = tuple(n for n in names if n not in done)
            fixed = {n: place[n] for n in done}
            if stage == 0:
                loads[i].wait()
            if stage > 0 and order[stage - 1] == "h":
                for copy in sent[i]:
                    copy.wait_recv()
            else:
                sent[i].wait_recv()
            if stage == len(order):
                if order[-1] == "h":
                    whole = tuple(place[n] for n in names)
                    value = sums[whole].astype(F32)
                    for k in range(far - 1):
                        value = value + brought[k].astype(F32)
                    out[cut] = value
                else:

                    def put(value, cut=cut):
                        out[cut] = value

                    add(sums, brought, fixed, left, put)
                continue
            axis = order[stage]
            if axis == "h":
                add(sums, brought, fixed, left)
                sent[i] = []
                for k in range(1, far):
                    goal = lax.rem(place["h"] + k, far)
                    whole = tuple(goal if n == "h" else place[n] for n in names)
                    sent[i].append(
                        copies.start(sums.at[whole], refs[2 + stage].at[k - 1], other_h(far, k))
                    )
            else:
                add(sums, brought, fixed, left, also={axis: 1 - place[axis]})
                index = tuple(
                    1 - place[n] if n == axis else fixed.get(n, slice(None)) for n in names
                )
                sent[i] = copies.start(sums.at[index], refs[2 + stage], flip(axis))
                add(sums, brought, fixed, left, also={axis: place[axis]})
        yield


def reduce_kernel(kinds, far, fsdp, counts, *refs):
    n = len(kinds)
    sources, outs = refs[:n], refs[n : 2 * n]
    scratch = refs[2 * n : -3]
    send_sems, recv_sems, local_sems = refs[-3:]
    partners = [flip("p"), flip("y"), flip("c")]
    if set(kinds) - {"group"}:
        partners += [other_h(far, k) for k in range(1, far)]
    if "all" in kinds:
        partners.append(flip("x"))
    greet(partners)
    copies = Copies(send_sems, recv_sems)
    running, position = [], 0
    for i, kind in enumerate(kinds):
        part = scratch[position : position + counts[i]]
        position += counts[i]
        running.append(
            reduce_steps(
                kind, far, fsdp, copies, sources[i], outs[i], part, local_sems.at[i]
            )
        )
    while running:
        running = [job for job in running if next(job, "end") != "end"]
    for copy in copies.started:
        copy.wait_send()


def reduce(name, number, far, fsdp, kinds, arrays):
    shapes, scratch, counts, total = [], [], [], 0
    for kind, array in zip(kinds, arrays):
        tail = array.shape[-2:]
        parts = reduce_plan(kind, far, fsdp, tail)[1]
        own = reduce_shapes(kind, far, fsdp, tail, array.dtype)
        counts.append(len(own))
        scratch += [pltpu.VMEM(shape, array.dtype) for shape in own]
        shapes.append(jax.ShapeDtypeStruct(tail, F32))
        total += sum(1 + len(order) + (far - 2 if "h" in order else 0) for _, _, order in parts)
    size = sum(a.size * a.dtype.itemsize for a in arrays)
    return pl.pallas_call(
        functools.partial(reduce_kernel, kinds, far, fsdp, tuple(counts)),
        out_shape=tuple(shapes),
        in_specs=[ANY] * len(arrays),
        out_specs=tuple([pl.BlockSpec(memory_space=pltpu.VMEM)] * len(arrays)),
        scratch_shapes=scratch
        + [
            pltpu.SemaphoreType.DMA((total,)),
            pltpu.SemaphoreType.DMA((total,)),
            pltpu.SemaphoreType.DMA((len(arrays), 2)),
        ],
        compiler_params=pltpu.CompilerParams(collective_id=number, has_side_effects=True),
        cost_estimate=pl.CostEstimate(flops=0, bytes_accessed=8 * size, transcendentals=0),
        name=name,
    )(*arrays)


def body(
    sizes,
    inputs,
    lengths,
    attn_gain,
    query_weight,
    query_bias,
    key_matrix,
    key_bias_vector,
    value_matrix,
    value_bias_vector,
    output_weight,
    mlp_gain,
    gate_weight,
    up_weight,
    down_weight,
    cotangent,
):
    far, fsdp = sizes
    micro, token_rows, width = inputs.shape[1:]
    shard = query_weight.shape[0]
    kv_width = key_matrix.shape[1]
    hidden_width = gate_weight.shape[1]
    devices = far * 8 * fsdp
    seq = far * 8
    ih, ip, iy, ic, ix = (lax.axis_index(name) for name in ("h", "p", "y", "c", "x"))
    me8 = (ip * 2 + iy) * 2 + ic
    me_seq = ih * 8 + me8

    def hop(array, axis, shift=1):
        if axis == "h":
            return lax.ppermute(array, "h", [(i, (i + shift) % far) for i in range(far)])
        return lax.ppermute(array, axis, SWAP)

    def pick(array, index, axis):
        return lax.dynamic_index_in_dim(array, index, axis, keepdims=False)

    slice_width = hidden_width // 8

    def slices(matrix):
        parts = matrix.reshape(shard, far, 8, hidden_width // (8 * far))
        return parts.transpose(2, 0, 1, 3).reshape(8, shard, slice_width)

    vectors = jnp.concatenate(
        [attn_gain, query_bias, key_bias_vector, value_bias_vector, mlp_gain]
    ).astype(F32)
    vectors = jnp.pad(vectors, (0, 1024 - vectors.shape[0])).reshape(8, 128)
    w_qkv, vectors, gate_parts, up_parts, w_down = move(
        "gather_first",
        0,
        far,
        fsdp,
        ("all", "all", "spread", "spread", "pair"),
        (
            jnp.concatenate([key_matrix, value_matrix, query_weight], axis=1),
            vectors,
            slices(gate_weight),
            slices(up_weight),
            down_weight,
        ),
    )
    w_down = w_down.reshape(slice_width, width)
    w_qkv = w_qkv.reshape(width, -1)
    vectors = vectors.reshape(devices, 1024)
    cuts = [0]
    for part in (attn_gain, query_bias, key_bias_vector, value_bias_vector, mlp_gain):
        cuts.append(cuts[-1] + part.shape[0])
    gain_attn, b_query, b_key, b_value, gain_mlp = (
        vectors[:, cuts[i] : cuts[i + 1]].reshape(-1) for i in range(5)
    )
    rows = inputs[0].astype(F32).reshape(micro * token_rows, width)
    upstream_low = cotangent[0].reshape(micro * token_rows, width)
    positions_at = me_seq * token_rows + jnp.arange(token_rows, dtype=jnp.int32)
    tables, spans, metas = [], [], []
    for number in range(micro):
        offsets, first = locate(lengths[0, number], positions_at)
        tables.append(rotary_tables(offsets, HEAD_WIDTH))
        spans.append(
            jnp.concatenate(
                [
                    jnp.tile(first, GROUP)[None],
                    jnp.tile(positions_at, GROUP)[None],
                    jnp.zeros((6, GROUP * token_rows), jnp.int32),
                ],
                axis=0,
            )
        )
        low = jnp.maximum(first[0] // token_rows, me_seq - seq // 2)
        metas.append(jnp.stack([low, me_seq]).astype(jnp.int32))
    cosine_table = jnp.concatenate([t[0] for t in tables], axis=0)
    sine_table = jnp.concatenate([t[1] for t in tables], axis=0)

    normed, recip_one = rms_forward(rows, gain_attn)
    normed_low = normed.astype(BF16)
    pre = mat_dot(normed_low, w_qkv)
    kv_pre = pre[:, : 2 * kv_width]
    key_rotated = apply_rotary(
        (kv_pre[:, :kv_width] + b_key).reshape(-1, KEY_VALUE_HEADS, HEAD_WIDTH),
        cosine_table,
        sine_table,
    ).reshape(-1, kv_width)
    own_kv = jnp.concatenate([key_rotated, kv_pre[:, kv_width:] + b_value], axis=1).astype(BF16)
    moved = move(
        "gather_second",
        1,
        far,
        fsdp,
        ("seq",) * micro + ("all", "pair8", "pair8", "group"),
        tuple(own_kv[m * token_rows : (m + 1) * token_rows] for m in range(micro))
        + (output_weight, gate_parts, up_parts, upstream_low),
    )
    stacks = [part.reshape(seq, token_rows, 2 * kv_width) for part in moved[:micro]]
    w_output = moved[micro].reshape(width, width)
    w_gate, w_up = (part.reshape(width, slice_width) for part in moved[micro + 1 : micro + 3])
    upstream_all = moved[micro + 3].reshape(-1, width)
    query_rotated = (
        apply_rotary(
            (pre[:, 2 * kv_width :] + b_query).reshape(-1, QUERY_HEADS, HEAD_WIDTH),
            cosine_table,
            sine_table,
        )
        .astype(BF16)
        .reshape(-1, width)
    )

    attended, lses = [], []
    for m in range(micro):
        part = slice(m * token_rows, (m + 1) * token_rows)
        result, lse = attend_forward(metas[m], query_rotated[part], stacks[m], spans[m])
        attended.append(result)
        lses.append(lse)
    attended = jnp.concatenate(attended, axis=0)
    middle = rows + mat_dot(attended, w_output)
    normed_two, recip_two = rms_forward(middle, gain_mlp)
    (tokens,) = move("gather_tokens", 2, far, fsdp, ("group",), (normed_two.astype(BF16),))
    tokens = tokens.reshape(-1, width)

    gate_pre = mat_dot(tokens, w_gate)
    up_pre = mat_dot(tokens, w_up)
    sigma = jax.nn.sigmoid(gate_pre)
    activated = gate_pre * sigma
    hidden = (activated * up_pre).astype(BF16)
    grad_hidden = cols_dot(upstream_all, w_down)
    grad_gate = (grad_hidden * up_pre * sigma * (1.0 + gate_pre * (1.0 - sigma))).astype(BF16)
    grad_up = (grad_hidden * activated).astype(BF16)
    group = (2, 2, 2, micro * token_rows, width)
    grad_two = (cols_dot(grad_gate, w_gate) + cols_dot(grad_up, w_up)).astype(BF16)
    final = mat_dot(hidden, w_down).astype(BF16)

    def paired(grad, axis):
        grad = grad.astype(BF16)
        kept = pick(grad, ix, axis).astype(F32) + hop(pick(grad, 1 - ix, axis), "x").astype(F32)
        kept = kept.astype(BF16)
        total = pick(kept, ih, 0).astype(F32)
        for k in range(1, far):
            total = total + hop(pick(kept, (ih + k) % far, 0), "h", k).astype(F32)
        return total

    eight = (far, 8, fsdp, shard, slice_width)
    gate_sum = paired(rows_dot(tokens, grad_gate).reshape(eight), 2).astype(BF16)
    up_sum = paired(rows_dot(tokens, grad_up).reshape(eight), 2).astype(BF16)
    down_part = paired(rows_dot(hidden, upstream_all).reshape(far, fsdp, -1, width), 1)

    (grad_two,) = reduce("reduce_tokens", 3, far, fsdp, ("group",), (grad_two.reshape(group),))
    grad_norm, gain_mlp_sum = rms_backward(middle, recip_two, gain_mlp, grad_two)
    grad_middle = upstream_low.astype(F32) + grad_norm
    grad_branch = grad_middle.astype(BF16)
    grad_attended = cols_dot(grad_branch, w_output).astype(BF16)
    grad_kvs, grad_query = [], []
    for m in range(micro):
        part = slice(m * token_rows, (m + 1) * token_rows)
        query_part, grad_keys, grad_values = attend_backward(
            metas[m], query_rotated[part], grad_attended[part], stacks[m], spans[m], lses[m]
        )
        stacked = jnp.concatenate([grad_keys, grad_values], axis=2)
        grad_kvs.append(stacked.reshape(far, 2, 2, 2, token_rows, 2 * kv_width))
        grad_query.append(query_part)

    blocks = (far, 2, 2, 2, fsdp, shard)
    g_output = rows_dot(attended, grad_branch).astype(BF16)
    reduced = reduce(
        "reduce_second",
        4,
        far,
        fsdp,
        ("seq",) * micro + ("all", "group"),
        tuple(grad_kvs) + (g_output.reshape(blocks + (width,)), final.reshape(group)),
    )
    grad_kvs, output_part = reduced[:micro], reduced[micro]
    results = (middle + reduced[micro + 1]).astype(BF16)
    grad_query = (
        inverse_rotary(
            jnp.concatenate(grad_query, axis=0).reshape(-1, QUERY_HEADS, HEAD_WIDTH),
            cosine_table,
            sine_table,
        )
        .reshape(-1, width)
        .astype(BF16)
    )
    grad_kv = jnp.concatenate(grad_kvs, axis=0)
    grad_key = inverse_rotary(
        grad_kv[:, :kv_width].reshape(-1, KEY_VALUE_HEADS, HEAD_WIDTH), cosine_table, sine_table
    ).reshape(-1, kv_width)
    grad_kv = jnp.concatenate([grad_key, grad_kv[:, kv_width:]], axis=1).astype(BF16)
    grad_normed = cols_dot(jnp.concatenate([grad_kv, grad_query], axis=1), w_qkv)
    grad_rows, gain_attn_sum = rms_backward(rows, recip_one, gain_attn, grad_normed)
    input_grad = grad_middle + grad_rows
    g_qkv = rows_dot(normed_low, jnp.concatenate([grad_kv, grad_query], axis=1)).astype(BF16)
    bias_query = jnp.sum(grad_query.astype(F32), axis=0)
    bias_kv = jnp.sum(grad_kv.astype(F32), axis=0)
    vector_sums = jnp.concatenate(
        [
            v.reshape(devices, -1)
            for v in (
                gain_attn_sum,
                bias_query,
                bias_kv[:kv_width],
                bias_kv[kv_width:],
                gain_mlp_sum,
            )
        ],
        axis=1,
    )
    vector_sums = jnp.pad(vector_sums, ((0, 0), (0, 1024 - vector_sums.shape[1])))
    qkv_part, vector_part = reduce(
        "reduce_last",
        5,
        far,
        fsdp,
        ("all", "all"),
        (g_qkv.reshape(blocks + (-1,)), vector_sums.reshape(far, 2, 2, 2, fsdp, 8, 128)),
    )
    kv_part, query_part = qkv_part[:, : 2 * kv_width], qkv_part[:, 2 * kv_width :]
    vector_part = vector_part.reshape(-1)
    gate_sum, up_sum = move("spread_last", 6, far, fsdp, ("spread", "spread"), (gate_sum, up_sum))

    def joined(part):
        part = part.reshape(8, shard, far, -1).transpose(1, 2, 0, 3)
        return part.reshape(shard, hidden_width).astype(F32)

    return (
        results.reshape(1, micro, token_rows, width),
        input_grad.reshape(1, micro, token_rows, width),
        vector_part[cuts[0] : cuts[1]],
        query_part,
        vector_part[cuts[1] : cuts[2]],
        kv_part[:, :kv_width],
        vector_part[cuts[2] : cuts[3]],
        kv_part[:, kv_width:],
        vector_part[cuts[3] : cuts[4]],
        output_part,
        vector_part[cuts[4] : cuts[5]],
        joined(gate_sum),
        joined(up_sum),
        down_part,
    )


def solution(mesh):
    fsdp = mesh.shape["fsdp"]
    far = mesh.shape["seq"] // 8
    inner = Mesh(mesh.devices.reshape(far, 2, 2, 2, fsdp), ("h", "p", "y", "c", "x"))
    seq = ("h", "p", "y", "c")
    every = seq + ("x",)
    tokens = P("x", None, seq, None)
    matrix, vector = P(every, None), P(every)
    in_specs = (
        tokens,
        P("x", None, None),
        vector,
        matrix,
        vector,
        matrix,
        vector,
        matrix,
        vector,
        matrix,
        vector,
        matrix,
        matrix,
        matrix,
        tokens,
    )
    out_specs = (
        tokens,
        tokens,
        vector,
        matrix,
        vector,
        matrix,
        vector,
        matrix,
        vector,
        matrix,
        vector,
        matrix,
        matrix,
        matrix,
    )
    return jax.shard_map(
        functools.partial(body, (far, fsdp)),
        mesh=inner,
        in_specs=in_specs,
        out_specs=out_specs,
        check_vma=False,
    )
```

```python
import functools

import jax
import jax.numpy as jnp
from jax import lax
from jax.experimental import pallas as pl
from jax.experimental.pallas import tpu as pltpu
from jax.sharding import Mesh, PartitionSpec as P

QUERY_HEADS = 12
KEY_VALUE_HEADS = 2
HEAD_WIDTH = 128
EPSILON = 1e-06
THETA = 10000.0
GROUP = QUERY_HEADS // KEY_VALUE_HEADS
SCALE = HEAD_WIDTH ** (-0.5)
F32 = jnp.float32
BF16 = jnp.bfloat16
SWAP = [(0, 1), (1, 0)]


def locate(item_lengths, positions_at):
    ends = jnp.cumsum(item_lengths)
    starts = ends - item_lengths
    segment_ids = jnp.sum((ends[None, :] <= positions_at[:, None]).astype(jnp.int32), axis=1)
    onehot = segment_ids[:, None] == jnp.arange(item_lengths.shape[0], dtype=jnp.int32)[None, :]
    first = jnp.sum(jnp.where(onehot, starts[None, :], 0), axis=1)
    return (positions_at - first, first)


def rotary_tables(offsets, head_size):
    freqs = 1.0 / THETA ** (jnp.arange(0, head_size, 2, dtype=F32) / head_size)
    angles = offsets.astype(F32)[:, None] * freqs[None, :]
    cosine, sine = jnp.cos(angles), jnp.sin(angles)
    return (jnp.concatenate([cosine, cosine], axis=1), jnp.concatenate([-sine, sine], axis=1))


def rms_forward(rows, gain):
    recip = lax.rsqrt(jnp.mean(rows * rows, axis=-1, keepdims=True) + EPSILON)
    return (rows * recip * gain, recip)


def rms_backward(rows, recip, gain, upstream):
    weighted = upstream * gain
    grad_rows = recip * weighted - rows * (recip * recip * recip) * jnp.mean(
        rows * weighted, axis=-1, keepdims=True
    )
    gain_grad = jnp.sum(upstream * rows * recip, axis=0)
    return (grad_rows, gain_grad)


def dot(left, right, dims, out=F32):
    return lax.dot_general(left, right, ((dims[0], dims[1]), ((), ())), preferred_element_type=out)


def rows_dot(left, right):
    return dot(left, right, ((0,), (0,)))


def cols_dot(left, right):
    return dot(left, right, ((1,), (1,)))


def mat_dot(left, right):
    return dot(left, right, ((1,), (0,)))


def attend_forward_kernel(meta, q_ref, k_ref, v_ref, span_ref, o_ref, lse_ref):
    rows = q_ref.shape[0]
    queries = jnp.concatenate(
        [q_ref[:, h * HEAD_WIDTH : (h + 1) * HEAD_WIDTH] for h in range(GROUP)], axis=0
    )
    first, last = span_ref[0:1, :], span_ref[1:2, :]
    wide = GROUP * rows
    local = lax.broadcasted_iota(jnp.int32, (rows, 1), 0)

    def step(block, carry):
        top, total, accum = carry
        keys, values = k_ref[block], v_ref[block]
        scores = dot(keys, queries, ((1,), (1,))) * SCALE
        index = block * rows + local
        scores = jnp.where((index >= first) & (index <= last), scores, -1e30)
        new_top = jnp.maximum(top, jnp.max(scores, axis=0, keepdims=True))
        fade = jnp.exp(top - new_top)
        probs = jnp.exp(scores - new_top)
        total = total * fade + jnp.sum(probs, axis=0, keepdims=True)
        accum = accum * fade + dot(values, probs.astype(BF16), ((0,), (0,)))
        return (new_top, total, accum)

    top, total, accum = lax.fori_loop(
        meta[0],
        meta[1] + 1,
        step,
        (
            jnp.full((1, wide), -1e30, F32),
            jnp.zeros((1, wide), F32),
            jnp.zeros((HEAD_WIDTH, wide), F32),
        ),
    )
    attended = (accum / total).T.astype(BF16)
    for h in range(GROUP):
        o_ref[:, h * HEAD_WIDTH : (h + 1) * HEAD_WIDTH] = attended[h * rows : (h + 1) * rows]
    lse_ref[0] = top + jnp.log(total)


def attend_forward(number, meta, queries, stack, span):
    pieces, rows, _ = stack.shape
    width = queries.shape[1]
    part = width // KEY_VALUE_HEADS
    spec = pltpu.PrefetchScalarGridSpec(
        num_scalar_prefetch=1,
        grid=(KEY_VALUE_HEADS,),
        in_specs=[
            pl.BlockSpec((rows, part), lambda g, m: (number, g)),
            pl.BlockSpec((pieces, rows, HEAD_WIDTH), lambda g, m: (0, 0, g)),
            pl.BlockSpec((pieces, rows, HEAD_WIDTH), lambda g, m: (0, 0, KEY_VALUE_HEADS + g)),
            pl.BlockSpec((8, GROUP * rows), lambda g, m: (0, 0)),
        ],
        out_specs=[
            pl.BlockSpec((rows, part), lambda g, m: (0, g)),
            pl.BlockSpec((1, 1, GROUP * rows), lambda g, m: (g, 0, 0)),
        ],
    )
    return pl.pallas_call(
        attend_forward_kernel,
        grid_spec=spec,
        out_shape=(
            jax.ShapeDtypeStruct((rows, width), BF16),
            jax.ShapeDtypeStruct((KEY_VALUE_HEADS, 1, GROUP * rows), F32),
        ),
        cost_estimate=pl.CostEstimate(
            flops=4 * rows * rows * 6 * width, bytes_accessed=stack.size * 2, transcendentals=0
        ),
        name="attend_forward",
    )(meta, queries, stack, stack, span)


def attend_backward_kernel(
    meta, q_ref, do_ref, kv_ref, span_ref, lse_ref, cos_ref, sin_ref, dq_ref, dkv_ref, p_ref, dp_ref
):
    rows = q_ref.shape[0]
    wide = GROUP * rows
    first, last = span_ref[0:1, :], span_ref[1:2, :]
    local = lax.broadcasted_iota(jnp.int32, (rows, 1), 0)
    low = meta[0]
    cosine, sine = cos_ref[...], sin_ref[...]
    dkv_ref[...] = jnp.zeros_like(dkv_ref)
    for group in range(KEY_VALUE_HEADS):
        heads = range(group * GROUP, (group + 1) * GROUP)
        cols = [slice(h * HEAD_WIDTH, (h + 1) * HEAD_WIDTH) for h in heads]
        key_cols = slice(group * HEAD_WIDTH, (group + 1) * HEAD_WIDTH)
        start = (KEY_VALUE_HEADS + group) * HEAD_WIDTH
        value_cols = slice(start, start + HEAD_WIDTH)
        queries = jnp.concatenate([q_ref[:, c] for c in cols], axis=0)
        grads = jnp.concatenate([do_ref[:, c] for c in cols], axis=0)
        lse = lse_ref[group]

        def collect(block, delta):
            scores = dot(kv_ref[block, :, key_cols], queries, ((1,), (1,))) * SCALE
            index = block * rows + local
            probs = jnp.where((index >= first) & (index <= last), jnp.exp(scores - lse), 0.0)
            grad_probs = dot(kv_ref[block, :, value_cols], grads, ((1,), (1,)))
            p_ref[block - low] = probs
            dp_ref[block - low] = grad_probs
            return delta + jnp.sum(probs * grad_probs, axis=0, keepdims=True)

        delta = lax.fori_loop(low, meta[1] + 1, collect, jnp.zeros((1, wide), F32))

        def spread(block, accum):
            probs = p_ref[block - low]
            grad_scores = (probs * (dp_ref[block - low] - delta)).astype(BF16)
            dkv_ref[block, :, key_cols] = (mat_dot(grad_scores, queries) * SCALE).astype(BF16)
            dkv_ref[block, :, value_cols] = mat_dot(probs.astype(BF16), grads).astype(BF16)
            return accum + dot(kv_ref[block, :, key_cols], grad_scores, ((0,), (0,)))

        accum = lax.fori_loop(low, meta[1] + 1, spread, jnp.zeros((HEAD_WIDTH, wide), F32))
        grad_queries = (accum * SCALE).T
        for h in range(GROUP):
            part = grad_queries[h * rows : (h + 1) * rows]
            turned = pltpu.roll(part, HEAD_WIDTH // 2, 1)
            dq_ref[:, cols[h]] = (part * cosine - turned * sine).astype(BF16)


def attend_backward(number, meta, queries, grads, stack, span, lse, cosine, sine):
    pieces, rows, wide = stack.shape
    width = queries.shape[1]
    most = pieces // 2 + 1

    def own(columns):
        return pl.BlockSpec((rows, columns), lambda i, m: (number, 0))

    def whole(shape):
        return pl.BlockSpec(shape, lambda i, m: (0,) * len(shape))

    spec = pltpu.PrefetchScalarGridSpec(
        num_scalar_prefetch=1,
        grid=(1,),
        in_specs=[
            own(width),
            own(width),
            whole(stack.shape),
            whole(span.shape),
            whole(lse.shape),
            own(HEAD_WIDTH),
            own(HEAD_WIDTH),
        ],
        out_specs=[whole((rows, width)), whole(stack.shape)],
        scratch_shapes=[
            pltpu.VMEM((most, rows, GROUP * rows), F32),
            pltpu.VMEM((most, rows, GROUP * rows), F32),
        ],
    )
    return pl.pallas_call(
        attend_backward_kernel,
        grid_spec=spec,
        out_shape=(
            jax.ShapeDtypeStruct((rows, width), BF16),
            jax.ShapeDtypeStruct(stack.shape, BF16),
        ),
        cost_estimate=pl.CostEstimate(
            flops=0, bytes_accessed=COST, transcendentals=0
        ),
        name="attend_backward",
    )(meta, queries, grads, stack, span, lse, cosine, sine)


def rotate_kernel(turned_heads, splits, sign, pre_ref, bias_ref, cos_ref, sin_ref, *outs):
    cosine, sine = cos_ref[...], sin_ref[...] * sign
    for head in range(pre_ref.shape[1] // HEAD_WIDTH):
        cols = slice(head * HEAD_WIDTH, (head + 1) * HEAD_WIDTH)
        part = pre_ref[:, cols] + bias_ref[:, cols]
        if head in turned_heads:
            part = part * cosine + pltpu.roll(part, HEAD_WIDTH // 2, 1) * sine
        part = part.astype(BF16)
        for (top, height, left, wide), out in zip(splits, outs):
            if left <= head * HEAD_WIDTH < left + wide:
                at = head * HEAD_WIDTH - left
                out[:, at : at + HEAD_WIDTH] = part[top : top + height]


def rotate(pre, bias, cosine, sine, turned_heads, splits, sign):
    return pl.pallas_call(
        functools.partial(rotate_kernel, tuple(turned_heads), splits, sign),
        out_shape=tuple(
            jax.ShapeDtypeStruct((height, wide), BF16) for _, height, _, wide in splits
        ),
        cost_estimate=pl.CostEstimate(flops=0, bytes_accessed=8 * pre.size, transcendentals=0),
        name="rotate",
    )(pre, bias, cosine, sine)


def cut_kernel(far, whole, *refs):
    count = len(refs) // 2
    for source, out in zip(refs[:count], refs[count:]):
        small = (out if whole else source).shape[1] // (8 * far)
        for h in range(far):
            for g in range(8):
                left, right = (h * 8 + g) * small, h * small
                if whole:
                    out[:, left : left + small] = source[g, :, right : right + small].astype(F32)
                else:
                    out[g, :, right : right + small] = source[:, left : left + small]


def cut_columns(far, whole, arrays):
    shapes = []
    for array in arrays:
        if whole:
            shapes.append(jax.ShapeDtypeStruct((array.shape[1], 8 * array.shape[2]), F32))
        else:
            shape = (8, array.shape[0], array.shape[1] // 8)
            shapes.append(jax.ShapeDtypeStruct(shape, array.dtype))
    return pl.pallas_call(
        functools.partial(cut_kernel, far, whole),
        out_shape=tuple(shapes),
        name="join_columns" if whole else "cut_columns",
    )(*arrays)


MESH = pl.DeviceIdType.MESH
PARTS, AHEAD = 4, 2
COST = 1024
ANY = pl.BlockSpec(memory_space=pl.ANY)


class Local:
    def __init__(self, source, buffer, target, sems):
        self.load = pltpu.make_async_copy(source, buffer, sems.at[0])
        self.store = pltpu.make_async_copy(buffer, target, sems.at[1])

    def start(self):
        self.load.start()

    def turn(self):
        self.load.wait()
        self.store.start()

    def wait(self):
        self.store.wait()


class Copies:
    def __init__(self, send_sems, recv_sems):
        self.send_sems, self.recv_sems, self.started = send_sems, recv_sems, []

    def start(self, source, target, device):
        number = len(self.started)
        copy = pltpu.make_async_remote_copy(
            src_ref=source,
            dst_ref=target,
            send_sem=self.send_sems.at[number],
            recv_sem=self.recv_sems.at[number],
            device_id=device,
            device_id_type=MESH,
        )
        copy.start()
        self.started.append(copy)
        return copy


def greet(devices):
    barrier = pltpu.get_barrier_semaphore()
    for device in devices:
        pl.semaphore_signal(barrier, inc=1, device_id=device, device_id_type=MESH)
    pl.semaphore_wait(barrier, len(devices))


def other_h(far, k):
    return {"h": lax.rem(lax.axis_index("h") + k, far)}


def flip(*axes):
    return {axis: 1 - lax.axis_index(axis) for axis in axes}


def corners():
    return [flip("p", "y"), flip("p", "c"), flip("y", "c"), flip("p", "y", "c")]


def gather_steps(kind, far, copies, source, out, local):
    ih, ip, iy, ic, ix = (lax.axis_index(name) for name in ("h", "p", "y", "c", "x"))
    every = kind in ("all", "all_y")

    def block(h, p, y=iy, x=ix):
        return out.at[h, p, y, ic, x] if every else out.at[h, p, y, ic]

    local.start()
    pieces = [(lax.rem(ih - k + far, far), p) for p in (ip, 1 - ip) for k in range(far)]
    count = len(pieces)
    arrivals, plane, cross, core = [None] * count, [None] * count, [None] * count, [None] * count
    columns = source.shape[-1]
    half = columns // 2 if columns % 256 == 0 and kind == "all" else columns

    def cut(ref, first):
        if half == columns:
            return ref
        return ref.at[:, pl.ds(0 if first else half, half)]

    for k in range(1, far):
        arrivals[k] = copies.start(source, block(ih, ip), other_h(far, k))
    for step in range(count + 3):
        if step < count:
            if arrivals[step] is not None:
                arrivals[step].wait_recv()
            h, p = pieces[step]
            held = source if step == 0 else block(h, p)
            if step < far:
                arrivals[far + step] = copies.start(held, block(h, p), flip("p"))
            plane[step] = [copies.start(held, block(h, p), flip("y"))]
            if every:
                plane[step].append(copies.start(held, block(h, p), flip("x")))
        if 0 <= step - 1 < count:
            h, p = pieces[step - 1]
            for copy in plane[step - 1]:
                copy.wait_recv()
            cross[step - 1] = []
            if every:
                ref = cut(block(h, p, x=1 - ix), True)
                cross[step - 1].append(copies.start(ref, ref, flip("y")))
                if half < columns:
                    ref = cut(block(h, p, y=1 - iy), False)
                    cross[step - 1].append(copies.start(ref, ref, flip("x")))
        if 0 <= step - 2 < count:
            h, p = pieces[step - 2]
            for copy in cross[step - 2]:
                copy.wait_recv()
            if step == 2:
                local.wait()
            ref = out.at[h, p, :, ic]
            core[step - 2] = copies.start(ref, ref, flip("c"))
        if 0 <= step - 3 < count:
            core[step - 3].wait_recv()
        yield


def group_steps(far, copies, source, out, local, delay):
    ip, iy, ic = (lax.axis_index(name) for name in ("p", "y", "c"))
    half = source.shape[0] // 2
    top, low = pl.ds(0, half), pl.ds(half, half)

    def rows(p, y, part):
        return out.at[p, y, ic, part]

    def forward(ref, axis):
        return copies.start(ref, ref, flip(axis))

    local.start()
    for _ in range(delay):
        yield
    first = [
        copies.start(source.at[top], rows(ip, iy, top), flip("y")),
        copies.start(source.at[low], rows(ip, iy, low), flip("p")),
    ]
    second = [
        copies.start(source.at[top], rows(ip, iy, top), flip("p")),
        copies.start(source.at[low], rows(ip, iy, low), flip("y")),
    ]
    core = [copies.start(source, out.at[ip, iy, ic], flip("c"))]
    yield
    first[0].wait_recv()
    second.append(forward(rows(ip, 1 - iy, top), "p"))
    core.append(forward(rows(ip, 1 - iy, top), "c"))
    first[1].wait_recv()
    second.append(forward(rows(1 - ip, iy, low), "y"))
    core.append(forward(rows(1 - ip, iy, low), "c"))
    yield
    for copy, p, y, part in (
        (second[0], 1 - ip, iy, top),
        (second[1], ip, 1 - iy, low),
        (second[2], 1 - ip, 1 - iy, top),
        (second[3], 1 - ip, 1 - iy, low),
    ):
        copy.wait_recv()
        core.append(forward(rows(p, y, part), "c"))
    yield
    for copy in core:
        copy.wait_recv()
    local.wait()


def pair_steps(far, copies, parts, place, local, delay):
    ih, ix = lax.axis_index("h"), lax.axis_index("x")
    local.start()
    for _ in range(delay):
        yield
    arrived, sent = [], []

    def send(i):
        if i < len(parts):
            target = place(ih, ix, i)
            arrived.append([copies.start(parts[i], target, other_h(far, k)) for k in range(1, far)])
            sent.append(copies.start(parts[i], target, flip("x")))

    for i in range(AHEAD):
        send(i)
    for i in range(len(parts)):
        yield
        send(i + AHEAD)
        for k in range(1, far):
            arrived[i][k - 1].wait_recv()
            ref = place(lax.rem(ih - k + far, far), ix, i)
            sent.append(copies.start(ref, ref, flip("x")))
    yield
    for copy in sent:
        copy.wait_recv()
    local.wait()


def spread_steps(far, copies, source, out, local, delay):
    ip, iy, ic = (lax.axis_index(name) for name in ("p", "y", "c"))
    me = (ip * 2 + iy) * 2 + ic
    local.start()
    for _ in range(delay):
        yield
    started = []
    for j in (1, 2, 4, 3, 5, 6, 7):
        p = 1 - ip if j & 4 else ip
        y = 1 - iy if j & 2 else iy
        c = 1 - ic if j & 1 else ic
        started.append(
            copies.start(source.at[(p * 2 + y) * 2 + c], out.at[me], {"p": p, "y": y, "c": c})
        )
    for _ in range(2 * far + 2):
        yield
    for copy in started:
        copy.wait_recv()
    local.wait()
    yield


def move_kernel(kinds, far, *refs):
    count = len(kinds)
    sources, outs = refs[:count], refs[count : 2 * count]
    buffers = refs[2 * count : 3 * count]
    send_sems, recv_sems, local_sems = refs[3 * count :]
    locals_ = []

    def local_copy(i, source, target):
        locals_.append(Local(source, buffers[i], target, local_sems.at[i]))
        return locals_[-1]

    ih, ip, iy, ic, ix = (lax.axis_index(name) for name in ("h", "p", "y", "c", "x"))
    partners = [flip("p"), flip("y"), flip("c")]
    if set(kinds) - {"spread", "group"}:
        partners += [other_h(far, k) for k in range(1, far)]
    if set(kinds) - {"seq", "group", "spread"}:
        partners.append(flip("x"))
    if "spread" in kinds:
        partners += corners()
    greet(partners)
    copies = Copies(send_sems, recv_sems)
    running = []
    for i, kind in enumerate(kinds):
        if kind == "spread":
            me = (ip * 2 + iy) * 2 + ic
            local = local_copy(i, sources[i].at[me], outs[i].at[me])
            running.append(spread_steps(far, copies, sources[i], outs[i], local, 0))
        elif kind == "group":
            place = outs[i].at[ip, iy, ic]
            local = local_copy(i, sources[i], place)
            delay = 3 if count > 1 else 0
            running.append(group_steps(far, copies, sources[i], outs[i], local, delay))
        elif kind in ("pair", "pair8"):
            local = outs[i].at[ih, :, ix] if kind == "pair8" else outs[i].at[ih, ix]
            local = local_copy(i, sources[i], local)
            step = (8 if kind == "pair8" else sources[i].shape[1]) // PARTS
            cuts = [pl.ds(part * step, step) for part in range(PARTS)]
            if kind == "pair8":
                parts = [sources[i].at[c] for c in cuts]
            else:
                parts = [sources[i].at[:, c] for c in cuts]

            def place(h, x, part, out=outs[i], cuts=cuts, wide=kind == "pair8"):
                return out.at[h, cuts[part], x] if wide else out.at[h, x, :, cuts[part]]

            wait = (PARTS - AHEAD + 1) * kinds[:i].count("pair8")
            running.append(pair_steps(far, copies, parts, place, local, wait))
        else:
            place = (ih, ip, iy, ic) if kind == "seq" else (ih, ip, iy, ic, ix)
            local = local_copy(i, sources[i], outs[i].at[place])
            running.append(gather_steps(kind, far, copies, sources[i], outs[i], local))
    running = [job for job in running if next(job, "end") != "end"]
    for local in locals_:
        local.turn()
    while running:
        running = [job for job in running if next(job, "end") != "end"]
    for copy in copies.started:
        copy.wait_send()


def move(name, number, far, fsdp, kinds, arrays):
    shapes, total = [], 0
    pieces = 2 * far
    for kind, array in zip(kinds, arrays):
        if kind in ("all", "all_y"):
            lead, total = (far, 2, 2, 2, fsdp), total + (far - 1) + far + 5 * pieces
        elif kind == "seq":
            lead, total = (far, 2, 2, 2), total + (far - 1) + far + 2 * pieces
        elif kind == "group":
            lead, total = (2, 2, 2), total + 13
        elif kind == "pair":
            lead, total = (far, fsdp), total + PARTS * (2 * far - 1)
        elif kind == "pair8":
            lead, total = (far, 8, fsdp), total + PARTS * (2 * far - 1)
        else:
            lead, total = (), total + 7
        tail = array.shape[1:] if kind == "pair8" else array.shape
        shapes.append(jax.ShapeDtypeStruct(lead + tail, array.dtype))
    return pl.pallas_call(
        functools.partial(move_kernel, kinds, far),
        out_shape=tuple(shapes),
        in_specs=[ANY] * len(arrays),
        out_specs=tuple([ANY] * len(arrays)),
        scratch_shapes=[
            pltpu.VMEM(a.shape[1:] if kind == "spread" else a.shape, a.dtype)
            for kind, a in zip(kinds, arrays)
        ]
        + [
            pltpu.SemaphoreType.DMA((total,)),
            pltpu.SemaphoreType.DMA((total,)),
            pltpu.SemaphoreType.DMA((len(arrays), 2)),
        ],
        compiler_params=pltpu.CompilerParams(collective_id=number, has_side_effects=True),
        cost_estimate=pl.CostEstimate(flops=0, bytes_accessed=COST, transcendentals=0),
        name=name,
    )(*arrays)


def reduce_plan(kind, far, fsdp, tail):
    rows, columns = tail
    if kind == "group":
        half = rows // 2
        return ("p", "y"), [
            ((pl.ds(0, half), slice(None)), (half, columns), ("p", "y")),
            ((pl.ds(half, half), slice(None)), (half, columns), ("y", "p")),
        ]
    if kind in ("seq", "seq_turned"):
        order = ("y", "p", "h") if kind == "seq" else ("p", "y", "h")
        return ("h", "p", "y"), [((slice(None), slice(None)), tail, order)]
    names = ("h", "p", "y", "x")
    if columns % 256:
        return names, [((slice(None), slice(None)), tail, ("x", "y", "p", "h"))]
    count = 4 if columns % 512 == 0 else 2
    step = columns // count
    orders = (("x", "y", "p", "h"), ("y", "x", "p", "h")) if kind == "all" else (("x", "y", "p", "h"),) * 2
    return names, [
        ((slice(None), pl.ds(i * step, step)), (rows, step), orders[i % 2]) for i in range(count)
    ]


def reduce_shapes(kind, far, fsdp, tail, dtype):
    length = {"h": far, "p": 2, "y": 2, "x": fsdp}
    names, parts = reduce_plan(kind, far, fsdp, tail)
    shapes = []
    for _, small, order in parts:
        left = list(names)
        full = tuple(length[n] for n in left) + small
        shapes += [full, full]
        for axis in order:
            left.remove(axis)
            lead = tuple(length[n] for n in left) + small
            shapes.append((far - 1,) + lead if axis == "h" else lead)
    return shapes


def reduce_steps(kind, far, fsdp, copies, source, out, scratch, local_sem):
    place = {name: lax.axis_index(name) for name in ("h", "p", "y", "x")}
    ic = lax.axis_index("c")
    length = {"h": far, "p": 2, "y": 2, "x": fsdp}
    core_dim = 2 if kind == "group" else 3
    names, parts = reduce_plan(kind, far, fsdp, out.shape)
    jobs, position = [], 0
    for cut, small, order in parts:
        count = 2 + len(order)
        jobs.append((cut, small, order, scratch[position : position + count]))
        position += count

    def view(c, cut):
        lead = [slice(None)] * core_dim + [c] + [slice(None)] * (len(names) - core_dim)
        return source.at[tuple(lead) + cut]

    def add(sums, brought, fixed, left, target=None, also=()):
        sizes = [1 if n in also else length[n] for n in left]
        total = 1
        for size in sizes:
            total *= size

        def one(number, _):
            index, rest = {}, number
            for n, size in reversed(list(zip(left, sizes))):
                index[n] = also[n] if n in also else rest % size
                rest = rest // size
            whole = tuple(fixed[n] if n in fixed else index[n] for n in names)
            value = sums[whole].astype(F32) + brought[tuple(index[n] for n in left)].astype(F32)
            if target is None:
                sums[whole] = value.astype(sums.dtype)
            else:
                target(value)
            return 0

        if total == 1:
            one(0, 0)
        else:
            lax.fori_loop(0, total, one, 0)

    loads, sent = [], []
    for i, (cut, small, order, refs) in enumerate(jobs):
        loads.append(pltpu.make_async_copy(view(ic, cut), refs[0], local_sem.at[i]))
        loads[i].start()
        sent.append(copies.start(view(1 - ic, cut), refs[1], flip("c")))
    yield
    for stage in range(len(jobs[0][2]) + 1):
        for i, (cut, small, order, refs) in enumerate(jobs):
            sums, brought = refs[0], refs[1 + stage]
            done = order[:stage]
            left = tuple(n for n in names if n not in done)
            fixed = {n: place[n] for n in done}
            if stage == 0:
                loads[i].wait()
            if stage > 0 and order[stage - 1] == "h":
                for copy in sent[i]:
                    copy.wait_recv()
            else:
                sent[i].wait_recv()
            if stage == len(order):
                if order[-1] == "h":
                    whole = tuple(place[n] for n in names)
                    value = sums[whole].astype(F32)
                    for k in range(far - 1):
                        value = value + brought[k].astype(F32)
                    out[cut] = value
                else:

                    def put(value, cut=cut):
                        out[cut] = value

                    add(sums, brought, fixed, left, put)
                continue
            axis = order[stage]
            if axis == "h":
                add(sums, brought, fixed, left)
                sent[i] = []
                for k in range(1, far):
                    goal = lax.rem(place["h"] + k, far)
                    whole = tuple(goal if n == "h" else place[n] for n in names)
                    sent[i].append(
                        copies.start(sums.at[whole], refs[2 + stage].at[k - 1], other_h(far, k))
                    )
            else:
                add(sums, brought, fixed, left, also={axis: 1 - place[axis]})
                index = tuple(
                    1 - place[n] if n == axis else fixed.get(n, slice(None)) for n in names
                )
                sent[i] = copies.start(sums.at[index], refs[2 + stage], flip(axis))
                add(sums, brought, fixed, left, also={axis: place[axis]})
        yield


def reduce_kernel(kinds, far, fsdp, counts, *refs):
    n = len(kinds)
    sources, outs = refs[:n], refs[n : 2 * n]
    scratch = refs[2 * n : -3]
    send_sems, recv_sems, local_sems = refs[-3:]
    partners = [flip("p"), flip("y"), flip("c")]
    if set(kinds) - {"group", "spread"}:
        partners += [other_h(far, k) for k in range(1, far)]
    if "all" in kinds or "all_x" in kinds:
        partners.append(flip("x"))
    if "spread" in kinds:
        partners += corners()
    greet(partners)
    copies = Copies(send_sems, recv_sems)
    running, position = [], 0
    for i, kind in enumerate(kinds):
        if kind == "spread":
            me = (lax.axis_index("p") * 2 + lax.axis_index("y")) * 2 + lax.axis_index("c")
            local = pltpu.make_async_copy(
                sources[i].at[me], outs[i].at[me], local_sems.at[i, 0]
            )
            running.append(spread_steps(far, copies, sources[i], outs[i], local, 1))
            continue
        part = scratch[position : position + counts[i]]
        position += counts[i]
        running.append(
            reduce_steps(
                kind, far, fsdp, copies, sources[i], outs[i], part, local_sems.at[i]
            )
        )
    while running:
        running = [job for job in running if next(job, "end") != "end"]
    for copy in copies.started:
        copy.wait_send()


def reduce(name, number, far, fsdp, kinds, arrays):
    shapes, scratch, counts, total = [], [], [], 0
    for kind, array in zip(kinds, arrays):
        if kind == "spread":
            shapes.append(jax.ShapeDtypeStruct(array.shape, array.dtype))
            counts.append(0)
            total += 7
            continue
        tail = array.shape[-2:]
        parts = reduce_plan(kind, far, fsdp, tail)[1]
        own = reduce_shapes(kind, far, fsdp, tail, array.dtype)
        counts.append(len(own))
        scratch += [pltpu.VMEM(shape, array.dtype) for shape in own]
        shapes.append(jax.ShapeDtypeStruct(tail, F32))
        total += sum(1 + len(order) + (far - 2 if "h" in order else 0) for _, _, order in parts)
    return pl.pallas_call(
        functools.partial(reduce_kernel, kinds, far, fsdp, tuple(counts)),
        out_shape=tuple(shapes),
        in_specs=[ANY] * len(arrays),
        out_specs=tuple(
            ANY if kind == "spread" else pl.BlockSpec(memory_space=pltpu.VMEM) for kind in kinds
        ),
        scratch_shapes=scratch
        + [
            pltpu.SemaphoreType.DMA((total,)),
            pltpu.SemaphoreType.DMA((total,)),
            pltpu.SemaphoreType.DMA((len(arrays), 4)),
        ],
        compiler_params=pltpu.CompilerParams(collective_id=number, has_side_effects=True),
        cost_estimate=pl.CostEstimate(flops=0, bytes_accessed=COST, transcendentals=0),
        name=name,
    )(*arrays)


def body(
    sizes,
    inputs,
    lengths,
    attn_gain,
    query_weight,
    query_bias,
    key_matrix,
    key_bias_vector,
    value_matrix,
    value_bias_vector,
    output_weight,
    mlp_gain,
    gate_weight,
    up_weight,
    down_weight,
    cotangent,
):
    far, fsdp = sizes
    micro, token_rows, width = inputs.shape[1:]
    shard = query_weight.shape[0]
    kv_width = key_matrix.shape[1]
    hidden_width = gate_weight.shape[1]
    devices = far * 8 * fsdp
    seq = far * 8
    ih, ip, iy, ic, ix = (lax.axis_index(name) for name in ("h", "p", "y", "c", "x"))
    me8 = (ip * 2 + iy) * 2 + ic
    me_seq = ih * 8 + me8

    def hop(array, axis, shift=1):
        if axis == "h":
            return lax.ppermute(array, "h", [(i, (i + shift) % far) for i in range(far)])
        return lax.ppermute(array, axis, SWAP)

    def pick(array, index, axis):
        return lax.dynamic_index_in_dim(array, index, axis, keepdims=False)

    slice_width = hidden_width // 8

    gate_cut, up_cut = cut_columns(far, False, (gate_weight, up_weight))

    vectors = jnp.concatenate(
        [attn_gain, query_bias, key_bias_vector, value_bias_vector, mlp_gain]
    ).astype(F32)
    vectors = jnp.pad(vectors, (0, 1024 - vectors.shape[0])).reshape(8, 128)
    w_qkv, vectors, gate_parts, up_parts, w_down = move(
        "gather_first",
        0,
        far,
        fsdp,
        ("all", "all", "spread", "spread", "pair"),
        (
            jnp.concatenate([query_weight, key_matrix, value_matrix], axis=1),
            vectors,
            gate_cut,
            up_cut,
            down_weight,
        ),
    )
    w_down = w_down.reshape(slice_width, width)
    w_qkv = w_qkv.reshape(width, -1)
    vectors = vectors.reshape(devices, 1024)
    cuts = [0]
    for part in (attn_gain, query_bias, key_bias_vector, value_bias_vector, mlp_gain):
        cuts.append(cuts[-1] + part.shape[0])
    gain_attn, b_query, b_key, b_value, gain_mlp = (
        vectors[:, cuts[i] : cuts[i + 1]].reshape(-1) for i in range(5)
    )
    rows = inputs[0].astype(F32).reshape(micro * token_rows, width)
    upstream_low = cotangent[0].reshape(micro * token_rows, width)
    positions_at = me_seq * token_rows + jnp.arange(token_rows, dtype=jnp.int32)
    tables, spans, metas = [], [], []
    for number in range(micro):
        offsets, first = locate(lengths[0, number], positions_at)
        tables.append(rotary_tables(offsets, HEAD_WIDTH))
        spans.append(
            jnp.concatenate(
                [
                    jnp.tile(first, GROUP)[None],
                    jnp.tile(positions_at, GROUP)[None],
                    jnp.zeros((6, GROUP * token_rows), jnp.int32),
                ],
                axis=0,
            )
        )
        low = jnp.maximum(first[0] // token_rows, me_seq - seq // 2)
        metas.append(jnp.stack([low, me_seq]).astype(jnp.int32))
    cosine_table = jnp.concatenate([t[0] for t in tables], axis=0)
    sine_table = jnp.concatenate([t[1] for t in tables], axis=0)

    normed, recip_one = rms_forward(rows, gain_attn)
    normed_low = normed.astype(BF16)
    pre = mat_dot(normed_low, w_qkv)
    heads = range(QUERY_HEADS + KEY_VALUE_HEADS)
    splits = ((0, micro * token_rows, 0, width),) + tuple(
        (m * token_rows, token_rows, width, 2 * kv_width) for m in range(micro)
    )
    biases = jnp.concatenate([b_query, b_key, b_value])[None]
    query_rotated, *own_kv = rotate(pre, biases, cosine_table, sine_table, heads, splits, 1.0)
    moved = move(
        "gather_second",
        1,
        far,
        fsdp,
        ("seq",) * micro + ("all_y", "pair8", "pair8", "group"),
        tuple(own_kv) + (output_weight, gate_parts, up_parts, upstream_low),
    )
    stacks = [part.reshape(seq, token_rows, 2 * kv_width) for part in moved[:micro]]
    w_output = moved[micro].reshape(width, width)
    w_gate, w_up = (part.reshape(width, slice_width) for part in moved[micro + 1 : micro + 3])
    upstream_all = moved[micro + 3].reshape(-1, width)
    attended, lses = [], []
    for m in range(micro):
        result, lse = attend_forward(m, metas[m], query_rotated, stacks[m], spans[m])
        attended.append(result)
        lses.append(lse)
    attended = jnp.concatenate(attended, axis=0)
    middle = rows + mat_dot(attended, w_output)
    normed_two, recip_two = rms_forward(middle, gain_mlp)
    (tokens,) = move("gather_tokens", 2, far, fsdp, ("group",), (normed_two.astype(BF16),))
    tokens = tokens.reshape(-1, width)

    gate_pre = mat_dot(tokens, w_gate)
    up_pre = mat_dot(tokens, w_up)
    sigma = jax.nn.sigmoid(gate_pre)
    activated = gate_pre * sigma
    hidden = (activated * up_pre).astype(BF16)
    grad_hidden = cols_dot(upstream_all, w_down)
    grad_gate = (grad_hidden * up_pre * sigma * (1.0 + gate_pre * (1.0 - sigma))).astype(BF16)
    grad_up = (grad_hidden * activated).astype(BF16)
    group = (2, 2, 2, micro * token_rows, width)

    def over_x(grad, axis, other):
        grad = grad.astype(BF16)
        sent, other = lax.optimization_barrier((pick(grad, 1 - ix, axis), other))
        kept = pick(grad, ix, axis).astype(F32) + hop(sent, "x").astype(F32)
        return kept.astype(BF16), other

    def over_h(kept):
        total = pick(kept, ih, 0).astype(F32)
        for k in range(1, far):
            total = total + hop(pick(kept, (ih + k) % far, 0), "h", k).astype(F32)
        return total

    eight = (far, 8, fsdp, shard, slice_width)
    down_part, _ = over_x(
        rows_dot(hidden, upstream_all).reshape(far, fsdp, -1, width), 1, upstream_all
    )
    gate_sum, grad_up_last = over_x(rows_dot(tokens, grad_gate).reshape(eight), 2, grad_up)
    up_sum = over_x(rows_dot(tokens, grad_up_last).reshape(eight), 2, ())[0]
    grad_two = (cols_dot(grad_gate, w_gate) + cols_dot(grad_up, w_up)).astype(BF16)

    (grad_two,) = reduce("reduce_tokens", 3, far, fsdp, ("group",), (grad_two.reshape(group),))
    grad_norm, gain_mlp_sum = rms_backward(middle, recip_two, gain_mlp, grad_two)
    grad_middle = upstream_low.astype(F32) + grad_norm
    grad_branch = grad_middle.astype(BF16)
    grad_branch, gate_sum, up_sum, hidden = lax.optimization_barrier(
        (grad_branch, gate_sum, up_sum, hidden)
    )
    final = mat_dot(hidden, w_down).astype(BF16)
    gate_sum = over_h(gate_sum).astype(BF16)
    up_sum = over_h(up_sum).astype(BF16)
    grad_attended = cols_dot(grad_branch, w_output).astype(BF16)
    grad_kvs, grad_query = [], []
    for m in range(micro):
        query_part, grad_kv = attend_backward(
            m,
            metas[m],
            query_rotated,
            grad_attended,
            stacks[m],
            spans[m],
            lses[m],
            cosine_table,
            sine_table,
        )
        grad_kvs.append(grad_kv.reshape(far, 2, 2, 2, token_rows, 2 * kv_width))
        grad_query.append(query_part)

    blocks = (far, 2, 2, 2, fsdp, shard)
    grad_kvs[0], gate_sum = lax.optimization_barrier((grad_kvs[0], gate_sum))
    g_output = rows_dot(attended, grad_branch).astype(BF16)
    reduced = reduce(
        "reduce_second",
        4,
        far,
        fsdp,
        tuple("seq_turned" if m % 2 else "seq" for m in range(micro)) + ("all_x", "group"),
        tuple(grad_kvs) + (g_output.reshape(blocks + (width,)), final.reshape(group)),
    )
    grad_kvs, output_part = list(reduced[:micro]), reduced[micro]
    grad_kvs[0], down_part = lax.optimization_barrier((grad_kvs[0], down_part))
    down_part = over_h(down_part)
    results = (middle + reduced[micro + 1]).astype(BF16)
    grad_query = jnp.concatenate(grad_query, axis=0)
    grad_kv = jnp.concatenate(grad_kvs, axis=0)
    (grad_kv,) = rotate(
        grad_kv,
        jnp.zeros((1, 2 * kv_width), F32),
        cosine_table,
        sine_table,
        range(KEY_VALUE_HEADS),
        ((0, micro * token_rows, 0, 2 * kv_width),),
        -1.0,
    )
    grad_pre = jnp.concatenate([grad_query, grad_kv], axis=1)
    grad_normed = cols_dot(grad_pre, w_qkv)
    grad_rows, gain_attn_sum = rms_backward(rows, recip_one, gain_attn, grad_normed)
    input_grad = grad_middle + grad_rows
    g_qkv = rows_dot(normed_low, grad_pre).astype(BF16)
    bias_sum = jnp.sum(grad_pre.astype(F32), axis=0)
    vector_sums = jnp.concatenate(
        [
            v.reshape(devices, -1)
            for v in (
                gain_attn_sum,
                bias_sum[:width],
                bias_sum[width : width + kv_width],
                bias_sum[width + kv_width :],
                gain_mlp_sum,
            )
        ],
        axis=1,
    )
    vector_sums = jnp.pad(vector_sums, ((0, 0), (0, 1024 - vector_sums.shape[1])))
    qkv_part, vector_part, gate_sum, up_sum = reduce(
        "reduce_last",
        5,
        far,
        fsdp,
        ("all", "all", "spread", "spread"),
        (
            g_qkv.reshape(blocks + (-1,)),
            vector_sums.reshape(far, 2, 2, 2, fsdp, 8, 128),
            gate_sum,
            up_sum,
        ),
    )
    vector_part = vector_part.reshape(-1)

    gate_grad, up_grad = cut_columns(far, True, (gate_sum, up_sum))

    return (
        results.reshape(1, micro, token_rows, width),
        input_grad.reshape(1, micro, token_rows, width),
        vector_part[cuts[0] : cuts[1]],
        qkv_part[:, :width],
        vector_part[cuts[1] : cuts[2]],
        qkv_part[:, width : width + kv_width],
        vector_part[cuts[2] : cuts[3]],
        qkv_part[:, width + kv_width :],
        vector_part[cuts[3] : cuts[4]],
        output_part,
        vector_part[cuts[4] : cuts[5]],
        gate_grad,
        up_grad,
        down_part,
    )


def solution(mesh):
    fsdp = mesh.shape["fsdp"]
    far = mesh.shape["seq"] // 8
    inner = Mesh(mesh.devices.reshape(far, 2, 2, 2, fsdp), ("h", "p", "y", "c", "x"))
    seq = ("h", "p", "y", "c")
    every = seq + ("x",)
    tokens = P("x", None, seq, None)
    matrix, vector = P(every, None), P(every)
    in_specs = (
        tokens,
        P("x", None, None),
        vector,
        matrix,
        vector,
        matrix,
        vector,
        matrix,
        vector,
        matrix,
        vector,
        matrix,
        matrix,
        matrix,
        tokens,
    )
    out_specs = (
        tokens,
        tokens,
        vector,
        matrix,
        vector,
        matrix,
        vector,
        matrix,
        vector,
        matrix,
        vector,
        matrix,
        matrix,
        matrix,
    )
    return jax.shard_map(
        functools.partial(body, (far, fsdp)),
        mesh=inner,
        in_specs=in_specs,
        out_specs=out_specs,
        check_vma=False,
    )
```

```python
import functools

import jax
import jax.numpy as jnp
from jax import lax
from jax.experimental import pallas as pl
from jax.experimental.pallas import tpu as pltpu
from jax.sharding import Mesh, PartitionSpec as P

QUERY_HEADS = 12
KEY_VALUE_HEADS = 2
HEAD_WIDTH = 128
EPSILON = 1e-06
THETA = 10000.0
GROUP = QUERY_HEADS // KEY_VALUE_HEADS
SCALE = HEAD_WIDTH ** (-0.5)
F32 = jnp.float32
BF16 = jnp.bfloat16
SWAP = [(0, 1), (1, 0)]


def locate(item_lengths, positions_at):
    ends = jnp.cumsum(item_lengths)
    starts = ends - item_lengths
    segment_ids = jnp.sum((ends[None, :] <= positions_at[:, None]).astype(jnp.int32), axis=1)
    onehot = segment_ids[:, None] == jnp.arange(item_lengths.shape[0], dtype=jnp.int32)[None, :]
    first = jnp.sum(jnp.where(onehot, starts[None, :], 0), axis=1)
    return (positions_at - first, first)


def rotary_tables(offsets, head_size):
    freqs = 1.0 / THETA ** (jnp.arange(0, head_size, 2, dtype=F32) / head_size)
    angles = offsets.astype(F32)[:, None] * freqs[None, :]
    cosine, sine = jnp.cos(angles), jnp.sin(angles)
    return (jnp.concatenate([cosine, cosine], axis=1), jnp.concatenate([-sine, sine], axis=1))


def rms_forward(rows, gain):
    recip = lax.rsqrt(jnp.mean(rows * rows, axis=-1, keepdims=True) + EPSILON)
    return (rows * recip * gain, recip)


def rms_backward(rows, recip, gain, upstream):
    weighted = upstream * gain
    grad_rows = recip * weighted - rows * (recip * recip * recip) * jnp.mean(
        rows * weighted, axis=-1, keepdims=True
    )
    gain_grad = jnp.sum(upstream * rows * recip, axis=0)
    return (grad_rows, gain_grad)


def dot(left, right, dims, out=F32):
    return lax.dot_general(left, right, ((dims[0], dims[1]), ((), ())), preferred_element_type=out)


def rows_dot(left, right):
    return dot(left, right, ((0,), (0,)))


def cols_dot(left, right):
    return dot(left, right, ((1,), (1,)))


def mat_dot(left, right):
    return dot(left, right, ((1,), (0,)))


def attend_forward_kernel(meta, q_ref, k_ref, v_ref, span_ref, o_ref, lse_ref):
    rows = q_ref.shape[0]
    queries = jnp.concatenate(
        [q_ref[:, h * HEAD_WIDTH : (h + 1) * HEAD_WIDTH] for h in range(GROUP)], axis=0
    )
    first, last = span_ref[0:1, :], span_ref[1:2, :]
    wide = GROUP * rows
    local = lax.broadcasted_iota(jnp.int32, (rows, 1), 0)

    def step(block, carry):
        top, total, accum = carry
        keys, values = k_ref[block], v_ref[block]
        scores = dot(keys, queries, ((1,), (1,))) * SCALE
        index = block * rows + local
        scores = jnp.where((index >= first) & (index <= last), scores, -1e30)
        new_top = jnp.maximum(top, jnp.max(scores, axis=0, keepdims=True))
        fade = jnp.exp(top - new_top)
        probs = jnp.exp(scores - new_top)
        total = total * fade + jnp.sum(probs, axis=0, keepdims=True)
        accum = accum * fade + dot(values, probs.astype(BF16), ((0,), (0,)))
        return (new_top, total, accum)

    top, total, accum = lax.fori_loop(
        meta[0],
        meta[1] + 1,
        step,
        (
            jnp.full((1, wide), -1e30, F32),
            jnp.zeros((1, wide), F32),
            jnp.zeros((HEAD_WIDTH, wide), F32),
        ),
    )
    attended = (accum / total).T.astype(BF16)
    for h in range(GROUP):
        o_ref[:, h * HEAD_WIDTH : (h + 1) * HEAD_WIDTH] = attended[h * rows : (h + 1) * rows]
    lse_ref[0] = top + jnp.log(total)


def attend_forward(number, meta, queries, stack, span):
    pieces, rows, _ = stack.shape
    width = queries.shape[1]
    part = width // KEY_VALUE_HEADS
    spec = pltpu.PrefetchScalarGridSpec(
        num_scalar_prefetch=1,
        grid=(KEY_VALUE_HEADS,),
        in_specs=[
            pl.BlockSpec((rows, part), lambda g, m: (number, g)),
            pl.BlockSpec((pieces, rows, HEAD_WIDTH), lambda g, m: (0, 0, g)),
            pl.BlockSpec((pieces, rows, HEAD_WIDTH), lambda g, m: (0, 0, KEY_VALUE_HEADS + g)),
            pl.BlockSpec((8, GROUP * rows), lambda g, m: (0, 0)),
        ],
        out_specs=[
            pl.BlockSpec((rows, part), lambda g, m: (0, g)),
            pl.BlockSpec((1, 1, GROUP * rows), lambda g, m: (g, 0, 0)),
        ],
    )
    return pl.pallas_call(
        attend_forward_kernel,
        grid_spec=spec,
        out_shape=(
            jax.ShapeDtypeStruct((rows, width), BF16),
            jax.ShapeDtypeStruct((KEY_VALUE_HEADS, 1, GROUP * rows), F32),
        ),
        cost_estimate=pl.CostEstimate(
            flops=4 * rows * rows * 6 * width, bytes_accessed=stack.size * 2, transcendentals=0
        ),
        name="attend_forward",
    )(meta, queries, stack, stack, span)


def attend_backward_kernel(
    meta, q_ref, do_ref, kv_ref, span_ref, lse_ref, cos_ref, sin_ref, dq_ref, dkv_ref, p_ref, dp_ref
):
    rows = q_ref.shape[0]
    wide = GROUP * rows
    first, last = span_ref[0:1, :], span_ref[1:2, :]
    local = lax.broadcasted_iota(jnp.int32, (rows, 1), 0)
    low = meta[0]
    cosine, sine = cos_ref[...], sin_ref[...]
    dkv_ref[...] = jnp.zeros_like(dkv_ref)
    for group in range(KEY_VALUE_HEADS):
        heads = range(group * GROUP, (group + 1) * GROUP)
        cols = [slice(h * HEAD_WIDTH, (h + 1) * HEAD_WIDTH) for h in heads]
        key_cols = slice(group * HEAD_WIDTH, (group + 1) * HEAD_WIDTH)
        start = (KEY_VALUE_HEADS + group) * HEAD_WIDTH
        value_cols = slice(start, start + HEAD_WIDTH)
        queries = jnp.concatenate([q_ref[:, c] for c in cols], axis=0)
        grads = jnp.concatenate([do_ref[:, c] for c in cols], axis=0)
        lse = lse_ref[group]

        def collect(block, delta):
            scores = dot(kv_ref[block, :, key_cols], queries, ((1,), (1,))) * SCALE
            index = block * rows + local
            probs = jnp.where((index >= first) & (index <= last), jnp.exp(scores - lse), 0.0)
            grad_probs = dot(kv_ref[block, :, value_cols], grads, ((1,), (1,)))
            p_ref[block - low] = probs
            dp_ref[block - low] = grad_probs
            return delta + jnp.sum(probs * grad_probs, axis=0, keepdims=True)

        delta = lax.fori_loop(low, meta[1] + 1, collect, jnp.zeros((1, wide), F32))

        def spread(block, accum):
            probs = p_ref[block - low]
            grad_scores = (probs * (dp_ref[block - low] - delta)).astype(BF16)
            dkv_ref[block, :, key_cols] = (mat_dot(grad_scores, queries) * SCALE).astype(BF16)
            dkv_ref[block, :, value_cols] = mat_dot(probs.astype(BF16), grads).astype(BF16)
            return accum + dot(kv_ref[block, :, key_cols], grad_scores, ((0,), (0,)))

        accum = lax.fori_loop(low, meta[1] + 1, spread, jnp.zeros((HEAD_WIDTH, wide), F32))
        grad_queries = (accum * SCALE).T
        for h in range(GROUP):
            part = grad_queries[h * rows : (h + 1) * rows]
            turned = pltpu.roll(part, HEAD_WIDTH // 2, 1)
            dq_ref[:, cols[h]] = (part * cosine - turned * sine).astype(BF16)


def attend_backward(number, meta, queries, grads, stack, span, lse, cosine, sine):
    pieces, rows, wide = stack.shape
    width = queries.shape[1]
    most = pieces // 2 + 1

    def own(columns):
        return pl.BlockSpec((rows, columns), lambda i, m: (number, 0))

    def whole(shape):
        return pl.BlockSpec(shape, lambda i, m: (0,) * len(shape))

    spec = pltpu.PrefetchScalarGridSpec(
        num_scalar_prefetch=1,
        grid=(1,),
        in_specs=[
            own(width),
            own(width),
            whole(stack.shape),
            whole(span.shape),
            whole(lse.shape),
            own(HEAD_WIDTH),
            own(HEAD_WIDTH),
        ],
        out_specs=[whole((rows, width)), whole(stack.shape)],
        scratch_shapes=[
            pltpu.VMEM((most, rows, GROUP * rows), F32),
            pltpu.VMEM((most, rows, GROUP * rows), F32),
        ],
    )
    return pl.pallas_call(
        attend_backward_kernel,
        grid_spec=spec,
        out_shape=(
            jax.ShapeDtypeStruct((rows, width), BF16),
            jax.ShapeDtypeStruct(stack.shape, BF16),
        ),
        cost_estimate=pl.CostEstimate(
            flops=0, bytes_accessed=COST, transcendentals=0
        ),
        name="attend_backward",
    )(meta, queries, grads, stack, span, lse, cosine, sine)


def hidden_kernel(
    token_ref,
    grad_ref,
    gate_ref,
    up_ref,
    down_ref,
    token_turned_ref,
    hidden_ref,
    turned_ref,
    dgate_ref,
    dup_ref,
):
    tokens = token_ref[...]
    token_turned_ref[...] = tokens.T
    gate_pre = mat_dot(tokens, gate_ref[...])
    up_pre = mat_dot(tokens, up_ref[...])
    grad_hidden = cols_dot(grad_ref[...], down_ref[...])
    sigma = jax.nn.sigmoid(gate_pre)
    activated = gate_pre * sigma
    hidden = activated * up_pre
    hidden_ref[...] = hidden.astype(BF16)
    turned_ref[...] = hidden.T.astype(BF16)
    dgate_ref[...] = (grad_hidden * up_pre * sigma * (1.0 + gate_pre * (1.0 - sigma))).astype(BF16)
    dup_ref[...] = (grad_hidden * activated).astype(BF16)


def hidden_units(rows, tokens, grads, w_gate, w_up, w_down):
    total, width = tokens.shape
    units = w_gate.shape[1]

    def tile(columns):
        return pl.BlockSpec((rows, columns), lambda i: (i, 0))

    def fixed(array):
        return pl.BlockSpec(array.shape, lambda i: (0, 0))

    return pl.pallas_call(
        hidden_kernel,
        grid=(total // rows,),
        in_specs=[tile(width), tile(width), fixed(w_gate), fixed(w_up), fixed(w_down)],
        out_specs=[
            pl.BlockSpec((width, rows), lambda i: (0, i)),
            tile(units),
            pl.BlockSpec((units, rows), lambda i: (0, i)),
            tile(units),
            tile(units),
        ],
        out_shape=(
            jax.ShapeDtypeStruct((width, total), BF16),
            jax.ShapeDtypeStruct((total, units), BF16),
            jax.ShapeDtypeStruct((units, total), BF16),
            jax.ShapeDtypeStruct((total, units), BF16),
            jax.ShapeDtypeStruct((total, units), BF16),
        ),
        cost_estimate=pl.CostEstimate(
            flops=6 * total * width * units, bytes_accessed=8 * total * width, transcendentals=0
        ),
        name="hidden_units",
    )(tokens, grads, w_gate, w_up, w_down)


def rotate_kernel(turned_heads, splits, sign, pre_ref, bias_ref, cos_ref, sin_ref, *outs):
    cosine, sine = cos_ref[...], sin_ref[...] * sign
    for head in range(pre_ref.shape[1] // HEAD_WIDTH):
        cols = slice(head * HEAD_WIDTH, (head + 1) * HEAD_WIDTH)
        part = pre_ref[:, cols] + bias_ref[:, cols]
        if head in turned_heads:
            part = part * cosine + pltpu.roll(part, HEAD_WIDTH // 2, 1) * sine
        part = part.astype(BF16)
        for (top, height, left, wide), out in zip(splits, outs):
            if left <= head * HEAD_WIDTH < left + wide:
                at = head * HEAD_WIDTH - left
                out[:, at : at + HEAD_WIDTH] = part[top : top + height]


def rotate(pre, bias, cosine, sine, turned_heads, splits, sign):
    return pl.pallas_call(
        functools.partial(rotate_kernel, tuple(turned_heads), splits, sign),
        out_shape=tuple(
            jax.ShapeDtypeStruct((height, wide), BF16) for _, height, _, wide in splits
        ),
        cost_estimate=pl.CostEstimate(flops=0, bytes_accessed=8 * pre.size, transcendentals=0),
        name="rotate",
    )(pre, bias, cosine, sine)


def cut_kernel(far, whole, *refs):
    count = len(refs) // 2
    for source, out in zip(refs[:count], refs[count:]):
        small = (out if whole else source).shape[1] // (8 * far)
        for h in range(far):
            for g in range(8):
                left, right = (h * 8 + g) * small, h * small
                if whole:
                    out[:, left : left + small] = source[g, :, right : right + small].astype(F32)
                else:
                    out[g, :, right : right + small] = source[:, left : left + small]


def cut_columns(far, whole, arrays):
    shapes = []
    for array in arrays:
        if whole:
            shapes.append(jax.ShapeDtypeStruct((array.shape[1], 8 * array.shape[2]), F32))
        else:
            shape = (8, array.shape[0], array.shape[1] // 8)
            shapes.append(jax.ShapeDtypeStruct(shape, array.dtype))
    return pl.pallas_call(
        functools.partial(cut_kernel, far, whole),
        out_shape=tuple(shapes),
        name="join_columns" if whole else "cut_columns",
    )(*arrays)


MESH = pl.DeviceIdType.MESH
PARTS, AHEAD = 4, 2
COST = 1024
ANY = pl.BlockSpec(memory_space=pl.ANY)


class Local:
    def __init__(self, source, buffer, target, sems):
        self.load = pltpu.make_async_copy(source, buffer, sems.at[0])
        self.store = pltpu.make_async_copy(buffer, target, sems.at[1])

    def start(self):
        self.load.start()

    def turn(self):
        self.load.wait()
        self.store.start()

    def wait(self):
        self.store.wait()


class Copies:
    def __init__(self, send_sems, recv_sems):
        self.send_sems, self.recv_sems, self.started = send_sems, recv_sems, []

    def start(self, source, target, device):
        number = len(self.started)
        copy = pltpu.make_async_remote_copy(
            src_ref=source,
            dst_ref=target,
            send_sem=self.send_sems.at[number],
            recv_sem=self.recv_sems.at[number],
            device_id=device,
            device_id_type=MESH,
        )
        copy.start()
        self.started.append(copy)
        return copy


def greet(devices):
    barrier = pltpu.get_barrier_semaphore()
    for device in devices:
        pl.semaphore_signal(barrier, inc=1, device_id=device, device_id_type=MESH)
    pl.semaphore_wait(barrier, len(devices))


def other_h(far, k):
    return {"h": lax.rem(lax.axis_index("h") + k, far)}


def flip(*axes):
    return {axis: 1 - lax.axis_index(axis) for axis in axes}


def corners():
    return [flip("p", "y"), flip("p", "c"), flip("y", "c"), flip("p", "y", "c")]


def gather_steps(kind, far, copies, source, out, local):
    ih, ip, iy, ic, ix = (lax.axis_index(name) for name in ("h", "p", "y", "c", "x"))
    every = kind in ("all", "all_y")

    def block(h, p, y=iy, x=ix):
        return out.at[h, p, y, ic, x] if every else out.at[h, p, y, ic]

    local.start()
    pieces = [(lax.rem(ih - k + far, far), p) for p in (ip, 1 - ip) for k in range(far)]
    count = len(pieces)
    arrivals, plane, cross, core = [None] * count, [None] * count, [None] * count, [None] * count
    columns = source.shape[-1]
    half = columns // 2 if columns % 256 == 0 and kind == "all" else columns

    def cut(ref, first):
        if half == columns:
            return ref
        return ref.at[:, pl.ds(0 if first else half, half)]

    for k in range(1, far):
        arrivals[k] = copies.start(source, block(ih, ip), other_h(far, k))
    for step in range(count + 3):
        if step < count:
            if arrivals[step] is not None:
                arrivals[step].wait_recv()
            h, p = pieces[step]
            held = source if step == 0 else block(h, p)
            if step < far:
                arrivals[far + step] = copies.start(held, block(h, p), flip("p"))
            plane[step] = [copies.start(held, block(h, p), flip("y"))]
            if every:
                plane[step].append(copies.start(held, block(h, p), flip("x")))
        if 0 <= step - 1 < count:
            h, p = pieces[step - 1]
            for copy in plane[step - 1]:
                copy.wait_recv()
            cross[step - 1] = []
            if every:
                ref = cut(block(h, p, x=1 - ix), True)
                cross[step - 1].append(copies.start(ref, ref, flip("y")))
                if half < columns:
                    ref = cut(block(h, p, y=1 - iy), False)
                    cross[step - 1].append(copies.start(ref, ref, flip("x")))
        if 0 <= step - 2 < count:
            h, p = pieces[step - 2]
            for copy in cross[step - 2]:
                copy.wait_recv()
            if step == 2:
                local.wait()
            ref = out.at[h, p, :, ic]
            core[step - 2] = copies.start(ref, ref, flip("c"))
        if 0 <= step - 3 < count:
            core[step - 3].wait_recv()
        yield


def group_steps(far, copies, source, out, local, delay):
    ip, iy, ic = (lax.axis_index(name) for name in ("p", "y", "c"))
    half = source.shape[0] // 2
    top, low = pl.ds(0, half), pl.ds(half, half)

    def rows(p, y, part):
        return out.at[p, y, ic, part]

    def forward(ref, axis):
        return copies.start(ref, ref, flip(axis))

    local.start()
    for _ in range(delay):
        yield
    first = [
        copies.start(source.at[top], rows(ip, iy, top), flip("y")),
        copies.start(source.at[low], rows(ip, iy, low), flip("p")),
    ]
    second = [
        copies.start(source.at[top], rows(ip, iy, top), flip("p")),
        copies.start(source.at[low], rows(ip, iy, low), flip("y")),
    ]
    core = [copies.start(source, out.at[ip, iy, ic], flip("c"))]
    yield
    first[0].wait_recv()
    second.append(forward(rows(ip, 1 - iy, top), "p"))
    core.append(forward(rows(ip, 1 - iy, top), "c"))
    first[1].wait_recv()
    second.append(forward(rows(1 - ip, iy, low), "y"))
    core.append(forward(rows(1 - ip, iy, low), "c"))
    yield
    for copy, p, y, part in (
        (second[0], 1 - ip, iy, top),
        (second[1], ip, 1 - iy, low),
        (second[2], 1 - ip, 1 - iy, top),
        (second[3], 1 - ip, 1 - iy, low),
    ):
        copy.wait_recv()
        core.append(forward(rows(p, y, part), "c"))
    yield
    for copy in core:
        copy.wait_recv()
    local.wait()


def pair_steps(far, copies, parts, place, local, delay):
    ih, ix = lax.axis_index("h"), lax.axis_index("x")
    local.start()
    for _ in range(delay):
        yield
    arrived, sent = [], []

    def send(i):
        if i < len(parts):
            target = place(ih, ix, i)
            arrived.append([copies.start(parts[i], target, other_h(far, k)) for k in range(1, far)])
            sent.append(copies.start(parts[i], target, flip("x")))

    for i in range(AHEAD):
        send(i)
    for i in range(len(parts)):
        yield
        send(i + AHEAD)
        for k in range(1, far):
            arrived[i][k - 1].wait_recv()
            ref = place(lax.rem(ih - k + far, far), ix, i)
            sent.append(copies.start(ref, ref, flip("x")))
    yield
    for copy in sent:
        copy.wait_recv()
    local.wait()


def spread_steps(far, copies, source, out, local, delay):
    ip, iy, ic = (lax.axis_index(name) for name in ("p", "y", "c"))
    me = (ip * 2 + iy) * 2 + ic
    local.start()
    for _ in range(delay):
        yield
    started = []
    for j in (1, 2, 4, 3, 5, 6, 7):
        p = 1 - ip if j & 4 else ip
        y = 1 - iy if j & 2 else iy
        c = 1 - ic if j & 1 else ic
        started.append(
            copies.start(source.at[(p * 2 + y) * 2 + c], out.at[me], {"p": p, "y": y, "c": c})
        )
    for _ in range(2 * far + 2):
        yield
    for copy in started:
        copy.wait_recv()
    local.wait()
    yield


def move_kernel(kinds, far, *refs):
    count = len(kinds)
    sources, outs = refs[:count], refs[count : 2 * count]
    buffers = refs[2 * count : 3 * count]
    send_sems, recv_sems, local_sems = refs[3 * count :]
    locals_ = []

    def local_copy(i, source, target):
        locals_.append(Local(source, buffers[i], target, local_sems.at[i]))
        return locals_[-1]

    ih, ip, iy, ic, ix = (lax.axis_index(name) for name in ("h", "p", "y", "c", "x"))
    partners = [flip("p"), flip("y"), flip("c")]
    if set(kinds) - {"spread", "group"}:
        partners += [other_h(far, k) for k in range(1, far)]
    if set(kinds) - {"seq", "group", "spread"}:
        partners.append(flip("x"))
    if "spread" in kinds:
        partners += corners()
    greet(partners)
    copies = Copies(send_sems, recv_sems)
    running = []
    for i, kind in enumerate(kinds):
        if kind == "spread":
            me = (ip * 2 + iy) * 2 + ic
            local = local_copy(i, sources[i].at[me], outs[i].at[me])
            running.append(spread_steps(far, copies, sources[i], outs[i], local, 0))
        elif kind == "group":
            place = outs[i].at[ip, iy, ic]
            local = local_copy(i, sources[i], place)
            delay = 3 if count > 1 else 0
            running.append(group_steps(far, copies, sources[i], outs[i], local, delay))
        elif kind in ("pair", "pair8"):
            local = outs[i].at[ih, :, ix] if kind == "pair8" else outs[i].at[ih, ix]
            local = local_copy(i, sources[i], local)
            step = (8 if kind == "pair8" else sources[i].shape[1]) // PARTS
            cuts = [pl.ds(part * step, step) for part in range(PARTS)]
            if kind == "pair8":
                parts = [sources[i].at[c] for c in cuts]
            else:
                parts = [sources[i].at[:, c] for c in cuts]

            def place(h, x, part, out=outs[i], cuts=cuts, wide=kind == "pair8"):
                return out.at[h, cuts[part], x] if wide else out.at[h, x, :, cuts[part]]

            wait = (PARTS - AHEAD + 1) * kinds[:i].count("pair8")
            running.append(pair_steps(far, copies, parts, place, local, wait))
        else:
            place = (ih, ip, iy, ic) if kind == "seq" else (ih, ip, iy, ic, ix)
            local = local_copy(i, sources[i], outs[i].at[place])
            running.append(gather_steps(kind, far, copies, sources[i], outs[i], local))
    running = [job for job in running if next(job, "end") != "end"]
    for local in locals_:
        local.turn()
    while running:
        running = [job for job in running if next(job, "end") != "end"]
    for copy in copies.started:
        copy.wait_send()


def move(name, number, far, fsdp, kinds, arrays):
    shapes, total = [], 0
    pieces = 2 * far
    for kind, array in zip(kinds, arrays):
        if kind in ("all", "all_y"):
            lead, total = (far, 2, 2, 2, fsdp), total + (far - 1) + far + 5 * pieces
        elif kind == "seq":
            lead, total = (far, 2, 2, 2), total + (far - 1) + far + 2 * pieces
        elif kind == "group":
            lead, total = (2, 2, 2), total + 13
        elif kind == "pair":
            lead, total = (far, fsdp), total + PARTS * (2 * far - 1)
        elif kind == "pair8":
            lead, total = (far, 8, fsdp), total + PARTS * (2 * far - 1)
        else:
            lead, total = (), total + 7
        tail = array.shape[1:] if kind == "pair8" else array.shape
        shapes.append(jax.ShapeDtypeStruct(lead + tail, array.dtype))
    return pl.pallas_call(
        functools.partial(move_kernel, kinds, far),
        out_shape=tuple(shapes),
        in_specs=[ANY] * len(arrays),
        out_specs=tuple([ANY] * len(arrays)),
        scratch_shapes=[
            pltpu.VMEM(a.shape[1:] if kind == "spread" else a.shape, a.dtype)
            for kind, a in zip(kinds, arrays)
        ]
        + [
            pltpu.SemaphoreType.DMA((total,)),
            pltpu.SemaphoreType.DMA((total,)),
            pltpu.SemaphoreType.DMA((len(arrays), 2)),
        ],
        compiler_params=pltpu.CompilerParams(collective_id=number, has_side_effects=True),
        cost_estimate=pl.CostEstimate(flops=0, bytes_accessed=COST, transcendentals=0),
        name=name,
    )(*arrays)


def reduce_plan(kind, far, fsdp, tail):
    rows, columns = tail
    if kind == "group":
        half = rows // 2
        return ("p", "y"), [
            ((pl.ds(0, half), slice(None)), (half, columns), ("p", "y")),
            ((pl.ds(half, half), slice(None)), (half, columns), ("y", "p")),
        ]
    if kind in ("seq", "seq_turned"):
        order = ("y", "p", "h") if kind == "seq" else ("p", "y", "h")
        return ("h", "p", "y"), [((slice(None), slice(None)), tail, order)]
    names = ("h", "p", "y", "x")
    if columns % 256:
        return names, [((slice(None), slice(None)), tail, ("x", "y", "p", "h"))]
    count = 4 if columns % 512 == 0 else 2
    step = columns // count
    orders = (("x", "y", "p", "h"), ("y", "x", "p", "h")) if kind == "all" else (("x", "y", "p", "h"),) * 2
    return names, [
        ((slice(None), pl.ds(i * step, step)), (rows, step), orders[i % 2]) for i in range(count)
    ]


def reduce_shapes(kind, far, fsdp, tail, dtype):
    length = {"h": far, "p": 2, "y": 2, "x": fsdp}
    names, parts = reduce_plan(kind, far, fsdp, tail)
    shapes = []
    for _, small, order in parts:
        left = list(names)
        full = tuple(length[n] for n in left) + small
        shapes += [full, full]
        for axis in order:
            left.remove(axis)
            lead = tuple(length[n] for n in left) + small
            shapes.append((far - 1,) + lead if axis == "h" else lead)
    return shapes


def reduce_steps(kind, far, fsdp, copies, source, out, scratch, local_sem):
    place = {name: lax.axis_index(name) for name in ("h", "p", "y", "x")}
    ic = lax.axis_index("c")
    length = {"h": far, "p": 2, "y": 2, "x": fsdp}
    core_dim = 2 if kind == "group" else 3
    names, parts = reduce_plan(kind, far, fsdp, out.shape)
    jobs, position = [], 0
    for cut, small, order in parts:
        count = 2 + len(order)
        jobs.append((cut, small, order, scratch[position : position + count]))
        position += count

    def view(c, cut):
        lead = [slice(None)] * core_dim + [c] + [slice(None)] * (len(names) - core_dim)
        return source.at[tuple(lead) + cut]

    def add(sums, brought, fixed, left, target=None, also=()):
        sizes = [1 if n in also else length[n] for n in left]
        total = 1
        for size in sizes:
            total *= size

        def one(number, _):
            index, rest = {}, number
            for n, size in reversed(list(zip(left, sizes))):
                index[n] = also[n] if n in also else rest % size
                rest = rest // size
            whole = tuple(fixed[n] if n in fixed else index[n] for n in names)
            value = sums[whole].astype(F32) + brought[tuple(index[n] for n in left)].astype(F32)
            if target is None:
                sums[whole] = value.astype(sums.dtype)
            else:
                target(value)
            return 0

        if total == 1:
            one(0, 0)
        else:
            lax.fori_loop(0, total, one, 0)

    loads, sent = [], []
    for i, (cut, small, order, refs) in enumerate(jobs):
        loads.append(pltpu.make_async_copy(view(ic, cut), refs[0], local_sem.at[i]))
        loads[i].start()
        sent.append(copies.start(view(1 - ic, cut), refs[1], flip("c")))
    yield
    for stage in range(len(jobs[0][2]) + 1):
        for i, (cut, small, order, refs) in enumerate(jobs):
            sums, brought = refs[0], refs[1 + stage]
            done = order[:stage]
            left = tuple(n for n in names if n not in done)
            fixed = {n: place[n] for n in done}
            if stage == 0:
                loads[i].wait()
            if stage > 0 and order[stage - 1] == "h":
                for copy in sent[i]:
                    copy.wait_recv()
            else:
                sent[i].wait_recv()
            if stage == len(order):
                if order[-1] == "h":
                    whole = tuple(place[n] for n in names)
                    value = sums[whole].astype(F32)
                    for k in range(far - 1):
                        value = value + brought[k].astype(F32)
                    out[cut] = value
                else:

                    def put(value, cut=cut):
                        out[cut] = value

                    add(sums, brought, fixed, left, put)
                continue
            axis = order[stage]
            if axis == "h":
                add(sums, brought, fixed, left)
                sent[i] = []
                for k in range(1, far):
                    goal = lax.rem(place["h"] + k, far)
                    whole = tuple(goal if n == "h" else place[n] for n in names)
                    sent[i].append(
                        copies.start(sums.at[whole], refs[2 + stage].at[k - 1], other_h(far, k))
                    )
            else:
                add(sums, brought, fixed, left, also={axis: 1 - place[axis]})
                index = tuple(
                    1 - place[n] if n == axis else fixed.get(n, slice(None)) for n in names
                )
                sent[i] = copies.start(sums.at[index], refs[2 + stage], flip(axis))
                add(sums, brought, fixed, left, also={axis: place[axis]})
        yield


def reduce_kernel(kinds, far, fsdp, counts, *refs):
    n = len(kinds)
    sources, outs = refs[:n], refs[n : 2 * n]
    scratch = refs[2 * n : -3]
    send_sems, recv_sems, local_sems = refs[-3:]
    partners = [flip("p"), flip("y"), flip("c")]
    if set(kinds) - {"group", "spread"}:
        partners += [other_h(far, k) for k in range(1, far)]
    if "all" in kinds or "all_x" in kinds:
        partners.append(flip("x"))
    if "spread" in kinds:
        partners += corners()
    greet(partners)
    copies = Copies(send_sems, recv_sems)
    running, position = [], 0
    for i, kind in enumerate(kinds):
        if kind == "spread":
            me = (lax.axis_index("p") * 2 + lax.axis_index("y")) * 2 + lax.axis_index("c")
            local = pltpu.make_async_copy(
                sources[i].at[me], outs[i].at[me], local_sems.at[i, 0]
            )
            running.append(spread_steps(far, copies, sources[i], outs[i], local, 1))
            continue
        part = scratch[position : position + counts[i]]
        position += counts[i]
        running.append(
            reduce_steps(
                kind, far, fsdp, copies, sources[i], outs[i], part, local_sems.at[i]
            )
        )
    while running:
        running = [job for job in running if next(job, "end") != "end"]
    for copy in copies.started:
        copy.wait_send()


def reduce(name, number, far, fsdp, kinds, arrays):
    shapes, scratch, counts, total = [], [], [], 0
    for kind, array in zip(kinds, arrays):
        if kind == "spread":
            shapes.append(jax.ShapeDtypeStruct(array.shape, array.dtype))
            counts.append(0)
            total += 7
            continue
        tail = array.shape[-2:]
        parts = reduce_plan(kind, far, fsdp, tail)[1]
        own = reduce_shapes(kind, far, fsdp, tail, array.dtype)
        counts.append(len(own))
        scratch += [pltpu.VMEM(shape, array.dtype) for shape in own]
        shapes.append(jax.ShapeDtypeStruct(tail, F32))
        total += sum(1 + len(order) + (far - 2 if "h" in order else 0) for _, _, order in parts)
    return pl.pallas_call(
        functools.partial(reduce_kernel, kinds, far, fsdp, tuple(counts)),
        out_shape=tuple(shapes),
        in_specs=[ANY] * len(arrays),
        out_specs=tuple(
            ANY if kind == "spread" else pl.BlockSpec(memory_space=pltpu.VMEM) for kind in kinds
        ),
        scratch_shapes=scratch
        + [
            pltpu.SemaphoreType.DMA((total,)),
            pltpu.SemaphoreType.DMA((total,)),
            pltpu.SemaphoreType.DMA((len(arrays), 4)),
        ],
        compiler_params=pltpu.CompilerParams(collective_id=number, has_side_effects=True),
        cost_estimate=pl.CostEstimate(flops=0, bytes_accessed=COST, transcendentals=0),
        name=name,
    )(*arrays)


def body(
    sizes,
    inputs,
    lengths,
    attn_gain,
    query_weight,
    query_bias,
    key_matrix,
    key_bias_vector,
    value_matrix,
    value_bias_vector,
    output_weight,
    mlp_gain,
    gate_weight,
    up_weight,
    down_weight,
    cotangent,
):
    far, fsdp = sizes
    micro, token_rows, width = inputs.shape[1:]
    shard = query_weight.shape[0]
    kv_width = key_matrix.shape[1]
    hidden_width = gate_weight.shape[1]
    devices = far * 8 * fsdp
    seq = far * 8
    ih, ip, iy, ic, ix = (lax.axis_index(name) for name in ("h", "p", "y", "c", "x"))
    me8 = (ip * 2 + iy) * 2 + ic
    me_seq = ih * 8 + me8

    def hop(array, axis, shift=1):
        if axis == "h":
            return lax.ppermute(array, "h", [(i, (i + shift) % far) for i in range(far)])
        return lax.ppermute(array, axis, SWAP)

    def pick(array, index, axis):
        return lax.dynamic_index_in_dim(array, index, axis, keepdims=False)

    slice_width = hidden_width // 8

    gate_cut, up_cut = cut_columns(far, False, (gate_weight, up_weight))

    vectors = jnp.concatenate(
        [attn_gain, query_bias, key_bias_vector, value_bias_vector, mlp_gain]
    ).astype(F32)
    vectors = jnp.pad(vectors, (0, 1024 - vectors.shape[0])).reshape(8, 128)
    w_qkv, vectors, gate_parts, up_parts, w_down = move(
        "gather_first",
        0,
        far,
        fsdp,
        ("all", "all", "spread", "spread", "pair"),
        (
            jnp.concatenate([query_weight, key_matrix, value_matrix], axis=1),
            vectors,
            gate_cut,
            up_cut,
            down_weight,
        ),
    )
    w_down = w_down.reshape(slice_width, width)
    w_qkv = w_qkv.reshape(width, -1)
    vectors = vectors.reshape(devices, 1024)
    cuts = [0]
    for part in (attn_gain, query_bias, key_bias_vector, value_bias_vector, mlp_gain):
        cuts.append(cuts[-1] + part.shape[0])
    gain_attn, b_query, b_key, b_value, gain_mlp = (
        vectors[:, cuts[i] : cuts[i + 1]].reshape(-1) for i in range(5)
    )
    rows = inputs[0].astype(F32).reshape(micro * token_rows, width)
    upstream_low = cotangent[0].reshape(micro * token_rows, width)
    positions_at = me_seq * token_rows + jnp.arange(token_rows, dtype=jnp.int32)
    tables, spans, metas = [], [], []
    for number in range(micro):
        offsets, first = locate(lengths[0, number], positions_at)
        tables.append(rotary_tables(offsets, HEAD_WIDTH))
        spans.append(
            jnp.concatenate(
                [
                    jnp.tile(first, GROUP)[None],
                    jnp.tile(positions_at, GROUP)[None],
                    jnp.zeros((6, GROUP * token_rows), jnp.int32),
                ],
                axis=0,
            )
        )
        low = jnp.maximum(first[0] // token_rows, me_seq - seq // 2)
        metas.append(jnp.stack([low, me_seq]).astype(jnp.int32))
    cosine_table = jnp.concatenate([t[0] for t in tables], axis=0)
    sine_table = jnp.concatenate([t[1] for t in tables], axis=0)

    normed, recip_one = rms_forward(rows, gain_attn)
    normed_low = normed.astype(BF16)
    pre = mat_dot(normed_low, w_qkv)
    heads = range(QUERY_HEADS + KEY_VALUE_HEADS)
    splits = ((0, micro * token_rows, 0, width),) + tuple(
        (m * token_rows, token_rows, width, 2 * kv_width) for m in range(micro)
    )
    biases = jnp.concatenate([b_query, b_key, b_value])[None]
    query_rotated, *own_kv = rotate(pre, biases, cosine_table, sine_table, heads, splits, 1.0)
    moved = move(
        "gather_second",
        1,
        far,
        fsdp,
        ("seq",) * micro + ("all_y", "pair8", "pair8", "group"),
        tuple(own_kv) + (output_weight, gate_parts, up_parts, upstream_low),
    )
    stacks = [part.reshape(seq, token_rows, 2 * kv_width) for part in moved[:micro]]
    w_output = moved[micro].reshape(width, width)
    w_gate, w_up = (part.reshape(width, slice_width) for part in moved[micro + 1 : micro + 3])
    upstream_all = moved[micro + 3].reshape(-1, width)
    attended, lses = [], []
    for m in range(micro):
        result, lse = attend_forward(m, metas[m], query_rotated, stacks[m], spans[m])
        attended.append(result)
        lses.append(lse)
    attended = jnp.concatenate(attended, axis=0)
    middle = rows + mat_dot(attended, w_output)
    normed_two, recip_two = rms_forward(middle, gain_mlp)
    (tokens,) = move("gather_tokens", 2, far, fsdp, ("group",), (normed_two.astype(BF16),))
    tokens = tokens.reshape(-1, width)

    tokens_turned, hidden, hidden_turned, grad_gate, grad_up = hidden_units(
        micro * token_rows, tokens, upstream_all, w_gate, w_up, w_down
    )
    group = (2, 2, 2, micro * token_rows, width)

    def over_x(grad, axis, other):
        grad = grad.astype(BF16)
        sent, other = lax.optimization_barrier((pick(grad, 1 - ix, axis), other))
        kept = pick(grad, ix, axis).astype(F32) + hop(sent, "x").astype(F32)
        return kept.astype(BF16), other

    def over_h(kept):
        total = pick(kept, ih, 0).astype(F32)
        for k in range(1, far):
            total = total + hop(pick(kept, (ih + k) % far, 0), "h", k).astype(F32)
        return total

    eight = (far, 8, fsdp, shard, slice_width)
    turned = tokens_turned.reshape(far, 8, fsdp, shard, -1)
    gate_sum, grad_up_last = over_x(dot(turned, grad_gate, ((4,), (0,))), 2, grad_up)
    up_sum, _ = over_x(dot(turned, grad_up_last, ((4,), (0,))), 2, ())
    grad_two = (cols_dot(grad_gate, w_gate) + cols_dot(grad_up, w_up)).astype(BF16)

    (grad_two,) = reduce("reduce_tokens", 3, far, fsdp, ("group",), (grad_two.reshape(group),))
    grad_norm, gain_mlp_sum = rms_backward(middle, recip_two, gain_mlp, grad_two)
    grad_middle = upstream_low.astype(F32) + grad_norm
    grad_branch = grad_middle.astype(BF16)
    grad_branch, gate_sum, up_sum = lax.optimization_barrier((grad_branch, gate_sum, up_sum))
    gate_sum = over_h(gate_sum).astype(BF16)
    up_sum = over_h(up_sum).astype(BF16)
    grad_attended = cols_dot(grad_branch, w_output).astype(BF16)
    grad_kvs, grad_query = [], []
    for m in range(micro):
        query_part, grad_kv = attend_backward(
            m,
            metas[m],
            query_rotated,
            grad_attended,
            stacks[m],
            spans[m],
            lses[m],
            cosine_table,
            sine_table,
        )
        grad_kvs.append(grad_kv.reshape(far, 2, 2, 2, token_rows, 2 * kv_width))
        grad_query.append(query_part)

    blocks = (far, 2, 2, 2, fsdp, shard)
    grad_kvs, gate_sum, hidden, hidden_turned = lax.optimization_barrier(
        (grad_kvs, gate_sum, hidden, hidden_turned)
    )
    down_part, _ = over_x(
        mat_dot(hidden_turned, upstream_all).reshape(far, fsdp, -1, width), 1, ()
    )
    final = mat_dot(hidden, w_down).astype(BF16)
    g_output = rows_dot(attended, grad_branch).astype(BF16)
    reduced = reduce(
        "reduce_second",
        4,
        far,
        fsdp,
        tuple("seq_turned" if m % 2 else "seq" for m in range(micro)) + ("all_x", "group"),
        tuple(grad_kvs) + (g_output.reshape(blocks + (width,)), final.reshape(group)),
    )
    grad_kvs, output_part = list(reduced[:micro]), reduced[micro]
    grad_kvs[0], down_part = lax.optimization_barrier((grad_kvs[0], down_part))
    down_part = over_h(down_part)
    results = (middle + reduced[micro + 1]).astype(BF16)
    grad_query = jnp.concatenate(grad_query, axis=0)
    grad_kv = jnp.concatenate(grad_kvs, axis=0)
    (grad_kv,) = rotate(
        grad_kv,
        jnp.zeros((1, 2 * kv_width), F32),
        cosine_table,
        sine_table,
        range(KEY_VALUE_HEADS),
        ((0, micro * token_rows, 0, 2 * kv_width),),
        -1.0,
    )
    grad_pre = jnp.concatenate([grad_query, grad_kv], axis=1)
    grad_normed = cols_dot(grad_pre, w_qkv)
    grad_rows, gain_attn_sum = rms_backward(rows, recip_one, gain_attn, grad_normed)
    input_grad = grad_middle + grad_rows
    g_qkv = rows_dot(normed_low, grad_pre).astype(BF16)
    bias_sum = jnp.sum(grad_pre.astype(F32), axis=0)
    vector_sums = jnp.concatenate(
        [
            v.reshape(devices, -1)
            for v in (
                gain_attn_sum,
                bias_sum[:width],
                bias_sum[width : width + kv_width],
                bias_sum[width + kv_width :],
                gain_mlp_sum,
            )
        ],
        axis=1,
    )
    vector_sums = jnp.pad(vector_sums, ((0, 0), (0, 1024 - vector_sums.shape[1])))
    qkv_part, vector_part, gate_sum, up_sum = reduce(
        "reduce_last",
        5,
        far,
        fsdp,
        ("all", "all", "spread", "spread"),
        (
            g_qkv.reshape(blocks + (-1,)),
            vector_sums.reshape(far, 2, 2, 2, fsdp, 8, 128),
            gate_sum,
            up_sum,
        ),
    )
    vector_part = vector_part.reshape(-1)

    gate_grad, up_grad = cut_columns(far, True, (gate_sum, up_sum))

    return (
        results.reshape(1, micro, token_rows, width),
        input_grad.reshape(1, micro, token_rows, width),
        vector_part[cuts[0] : cuts[1]],
        qkv_part[:, :width],
        vector_part[cuts[1] : cuts[2]],
        qkv_part[:, width : width + kv_width],
        vector_part[cuts[2] : cuts[3]],
        qkv_part[:, width + kv_width :],
        vector_part[cuts[3] : cuts[4]],
        output_part,
        vector_part[cuts[4] : cuts[5]],
        gate_grad,
        up_grad,
        down_part,
    )


def solution(mesh):
    fsdp = mesh.shape["fsdp"]
    far = mesh.shape["seq"] // 8
    inner = Mesh(mesh.devices.reshape(far, 2, 2, 2, fsdp), ("h", "p", "y", "c", "x"))
    seq = ("h", "p", "y", "c")
    every = seq + ("x",)
    tokens = P("x", None, seq, None)
    matrix, vector = P(every, None), P(every)
    in_specs = (
        tokens,
        P("x", None, None),
        vector,
        matrix,
        vector,
        matrix,
        vector,
        matrix,
        vector,
        matrix,
        vector,
        matrix,
        matrix,
        matrix,
        tokens,
    )
    out_specs = (
        tokens,
        tokens,
        vector,
        matrix,
        vector,
        matrix,
        vector,
        matrix,
        vector,
        matrix,
        vector,
        matrix,
        matrix,
        matrix,
    )
    return jax.shard_map(
        functools.partial(body, (far, fsdp)),
        mesh=inner,
        in_specs=in_specs,
        out_specs=out_specs,
        check_vma=False,
    )
```

```python
import functools

import jax
import jax.numpy as jnp
from jax import lax
from jax.experimental import pallas as pl
from jax.experimental.pallas import tpu as pltpu
from jax.sharding import Mesh, PartitionSpec as P

QUERY_HEADS = 12
KEY_VALUE_HEADS = 2
HEAD_WIDTH = 128
EPSILON = 1e-06
THETA = 10000.0
GROUP = QUERY_HEADS // KEY_VALUE_HEADS
SCALE = HEAD_WIDTH ** (-0.5)
F32 = jnp.float32
BF16 = jnp.bfloat16
SWAP = [(0, 1), (1, 0)]


def locate(item_lengths, positions_at):
    ends = jnp.cumsum(item_lengths)
    starts = ends - item_lengths
    segment_ids = jnp.sum((ends[None, :] <= positions_at[:, None]).astype(jnp.int32), axis=1)
    onehot = segment_ids[:, None] == jnp.arange(item_lengths.shape[0], dtype=jnp.int32)[None, :]
    first = jnp.sum(jnp.where(onehot, starts[None, :], 0), axis=1)
    return (positions_at - first, first)


def rotary_tables(offsets, head_size):
    freqs = 1.0 / THETA ** (jnp.arange(0, head_size, 2, dtype=F32) / head_size)
    angles = offsets.astype(F32)[:, None] * freqs[None, :]
    cosine, sine = jnp.cos(angles), jnp.sin(angles)
    return (jnp.concatenate([cosine, cosine], axis=1), jnp.concatenate([-sine, sine], axis=1))


def rms_forward(rows, gain):
    recip = lax.rsqrt(jnp.mean(rows * rows, axis=-1, keepdims=True) + EPSILON)
    return (rows * recip * gain, recip)


def rms_backward(rows, recip, gain, upstream):
    weighted = upstream * gain
    grad_rows = recip * weighted - rows * (recip * recip * recip) * jnp.mean(
        rows * weighted, axis=-1, keepdims=True
    )
    gain_grad = jnp.sum(upstream * rows * recip, axis=0)
    return (grad_rows, gain_grad)


def dot(left, right, dims, out=F32):
    return lax.dot_general(left, right, ((dims[0], dims[1]), ((), ())), preferred_element_type=out)


def rows_dot(left, right):
    return dot(left, right, ((0,), (0,)))


def cols_dot(left, right):
    return dot(left, right, ((1,), (1,)))


def mat_dot(left, right):
    return dot(left, right, ((1,), (0,)))


def attend_forward_kernel(meta, q_ref, k_ref, v_ref, span_ref, o_ref, lse_ref):
    rows = q_ref.shape[0]
    queries = jnp.concatenate(
        [q_ref[:, h * HEAD_WIDTH : (h + 1) * HEAD_WIDTH] for h in range(GROUP)], axis=0
    )
    first, last = span_ref[0:1, :], span_ref[1:2, :]
    wide = GROUP * rows
    local = lax.broadcasted_iota(jnp.int32, (rows, 1), 0)

    def step(block, carry):
        top, total, accum = carry
        keys, values = k_ref[block], v_ref[block]
        scores = dot(keys, queries, ((1,), (1,))) * SCALE
        index = block * rows + local
        scores = jnp.where((index >= first) & (index <= last), scores, -1e30)
        new_top = jnp.maximum(top, jnp.max(scores, axis=0, keepdims=True))
        fade = jnp.exp(top - new_top)
        probs = jnp.exp(scores - new_top)
        total = total * fade + jnp.sum(probs, axis=0, keepdims=True)
        accum = accum * fade + dot(values, probs.astype(BF16), ((0,), (0,)))
        return (new_top, total, accum)

    top, total, accum = lax.fori_loop(
        meta[0],
        meta[1] + 1,
        step,
        (
            jnp.full((1, wide), -1e30, F32),
            jnp.zeros((1, wide), F32),
            jnp.zeros((HEAD_WIDTH, wide), F32),
        ),
    )
    attended = (accum / total).T.astype(BF16)
    for h in range(GROUP):
        o_ref[:, h * HEAD_WIDTH : (h + 1) * HEAD_WIDTH] = attended[h * rows : (h + 1) * rows]
    lse_ref[0] = top + jnp.log(total)


def attend_forward(number, meta, queries, stack, span):
    pieces, rows, _ = stack.shape
    width = queries.shape[1]
    part = width // KEY_VALUE_HEADS
    spec = pltpu.PrefetchScalarGridSpec(
        num_scalar_prefetch=1,
        grid=(KEY_VALUE_HEADS,),
        in_specs=[
            pl.BlockSpec((rows, part), lambda g, m: (number, g)),
            pl.BlockSpec((pieces, rows, HEAD_WIDTH), lambda g, m: (0, 0, g)),
            pl.BlockSpec((pieces, rows, HEAD_WIDTH), lambda g, m: (0, 0, KEY_VALUE_HEADS + g)),
            pl.BlockSpec((8, GROUP * rows), lambda g, m: (0, 0)),
        ],
        out_specs=[
            pl.BlockSpec((rows, part), lambda g, m: (0, g)),
            pl.BlockSpec((1, 1, GROUP * rows), lambda g, m: (g, 0, 0)),
        ],
    )
    return pl.pallas_call(
        attend_forward_kernel,
        grid_spec=spec,
        out_shape=(
            jax.ShapeDtypeStruct((rows, width), BF16),
            jax.ShapeDtypeStruct((KEY_VALUE_HEADS, 1, GROUP * rows), F32),
        ),
        cost_estimate=pl.CostEstimate(
            flops=4 * rows * rows * 6 * width, bytes_accessed=stack.size * 2, transcendentals=0
        ),
        name="attend_forward",
    )(meta, queries, stack, stack, span)


def attend_backward_kernel(
    meta, q_ref, do_ref, kv_ref, span_ref, lse_ref, cos_ref, sin_ref, dq_ref, dkv_ref, p_ref, dp_ref
):
    rows = q_ref.shape[0]
    wide = GROUP * rows
    first, last = span_ref[0:1, :], span_ref[1:2, :]
    local = lax.broadcasted_iota(jnp.int32, (rows, 1), 0)
    low = meta[0]
    cosine, sine = cos_ref[...], sin_ref[...]
    dkv_ref[...] = jnp.zeros_like(dkv_ref)
    for group in range(KEY_VALUE_HEADS):
        heads = range(group * GROUP, (group + 1) * GROUP)
        cols = [slice(h * HEAD_WIDTH, (h + 1) * HEAD_WIDTH) for h in heads]
        key_cols = slice(group * HEAD_WIDTH, (group + 1) * HEAD_WIDTH)
        start = (KEY_VALUE_HEADS + group) * HEAD_WIDTH
        value_cols = slice(start, start + HEAD_WIDTH)
        queries = jnp.concatenate([q_ref[:, c] for c in cols], axis=0)
        grads = jnp.concatenate([do_ref[:, c] for c in cols], axis=0)
        lse = lse_ref[group]

        def collect(block, delta):
            scores = dot(kv_ref[block, :, key_cols], queries, ((1,), (1,))) * SCALE
            index = block * rows + local
            probs = jnp.where((index >= first) & (index <= last), jnp.exp(scores - lse), 0.0)
            grad_probs = dot(kv_ref[block, :, value_cols], grads, ((1,), (1,)))
            p_ref[block - low] = probs
            dp_ref[block - low] = grad_probs
            return delta + jnp.sum(probs * grad_probs, axis=0, keepdims=True)

        delta = lax.fori_loop(low, meta[1] + 1, collect, jnp.zeros((1, wide), F32))

        def spread(block, accum):
            probs = p_ref[block - low]
            grad_scores = (probs * (dp_ref[block - low] - delta)).astype(BF16)
            dkv_ref[block, :, key_cols] = (mat_dot(grad_scores, queries) * SCALE).astype(BF16)
            dkv_ref[block, :, value_cols] = mat_dot(probs.astype(BF16), grads).astype(BF16)
            return accum + dot(kv_ref[block, :, key_cols], grad_scores, ((0,), (0,)))

        accum = lax.fori_loop(low, meta[1] + 1, spread, jnp.zeros((HEAD_WIDTH, wide), F32))
        grad_queries = (accum * SCALE).T
        for h in range(GROUP):
            part = grad_queries[h * rows : (h + 1) * rows]
            turned = pltpu.roll(part, HEAD_WIDTH // 2, 1)
            dq_ref[:, cols[h]] = (part * cosine - turned * sine).astype(BF16)


def attend_backward(number, meta, queries, grads, stack, span, lse, cosine, sine):
    pieces, rows, wide = stack.shape
    width = queries.shape[1]
    most = pieces // 2 + 1

    def own(columns):
        return pl.BlockSpec((rows, columns), lambda i, m: (number, 0))

    def whole(shape):
        return pl.BlockSpec(shape, lambda i, m: (0,) * len(shape))

    spec = pltpu.PrefetchScalarGridSpec(
        num_scalar_prefetch=1,
        grid=(1,),
        in_specs=[
            own(width),
            own(width),
            whole(stack.shape),
            whole(span.shape),
            whole(lse.shape),
            own(HEAD_WIDTH),
            own(HEAD_WIDTH),
        ],
        out_specs=[whole((rows, width)), whole(stack.shape)],
        scratch_shapes=[
            pltpu.VMEM((most, rows, GROUP * rows), F32),
            pltpu.VMEM((most, rows, GROUP * rows), F32),
        ],
    )
    return pl.pallas_call(
        attend_backward_kernel,
        grid_spec=spec,
        out_shape=(
            jax.ShapeDtypeStruct((rows, width), BF16),
            jax.ShapeDtypeStruct(stack.shape, BF16),
        ),
        cost_estimate=pl.CostEstimate(
            flops=0, bytes_accessed=COST, transcendentals=0
        ),
        name="attend_backward",
    )(meta, queries, grads, stack, span, lse, cosine, sine)


def hidden_kernel(
    token_ref,
    grad_ref,
    gate_ref,
    up_ref,
    down_ref,
    token_turned_ref,
    hidden_ref,
    turned_ref,
    dgate_ref,
    dup_ref,
):
    tokens = token_ref[...]
    token_turned_ref[...] = tokens.T
    gate_pre = mat_dot(tokens, gate_ref[...])
    up_pre = mat_dot(tokens, up_ref[...])
    grad_hidden = cols_dot(grad_ref[...], down_ref[...])
    sigma = jax.nn.sigmoid(gate_pre)
    activated = gate_pre * sigma
    hidden = activated * up_pre
    hidden_ref[...] = hidden.astype(BF16)
    turned_ref[...] = hidden.T.astype(BF16)
    dgate_ref[...] = (grad_hidden * up_pre * sigma * (1.0 + gate_pre * (1.0 - sigma))).astype(BF16)
    dup_ref[...] = (grad_hidden * activated).astype(BF16)


def hidden_units(rows, tokens, grads, w_gate, w_up, w_down):
    total, width = tokens.shape
    units = w_gate.shape[1]

    def tile(columns):
        return pl.BlockSpec((rows, columns), lambda i: (i, 0))

    def fixed(array):
        return pl.BlockSpec(array.shape, lambda i: (0, 0))

    return pl.pallas_call(
        hidden_kernel,
        grid=(total // rows,),
        in_specs=[tile(width), tile(width), fixed(w_gate), fixed(w_up), fixed(w_down)],
        out_specs=[
            pl.BlockSpec((width, rows), lambda i: (0, i)),
            tile(units),
            pl.BlockSpec((units, rows), lambda i: (0, i)),
            tile(units),
            tile(units),
        ],
        out_shape=(
            jax.ShapeDtypeStruct((width, total), BF16),
            jax.ShapeDtypeStruct((total, units), BF16),
            jax.ShapeDtypeStruct((units, total), BF16),
            jax.ShapeDtypeStruct((total, units), BF16),
            jax.ShapeDtypeStruct((total, units), BF16),
        ),
        cost_estimate=pl.CostEstimate(
            flops=6 * total * width * units, bytes_accessed=8 * total * width, transcendentals=0
        ),
        name="hidden_units",
    )(tokens, grads, w_gate, w_up, w_down)


def rotate_kernel(turned_heads, splits, sign, pre_ref, bias_ref, cos_ref, sin_ref, *outs):
    cosine, sine = cos_ref[...], sin_ref[...] * sign
    for head in range(pre_ref.shape[1] // HEAD_WIDTH):
        cols = slice(head * HEAD_WIDTH, (head + 1) * HEAD_WIDTH)
        part = pre_ref[:, cols] + bias_ref[:, cols]
        if head in turned_heads:
            part = part * cosine + pltpu.roll(part, HEAD_WIDTH // 2, 1) * sine
        part = part.astype(BF16)
        for (top, height, left, wide), out in zip(splits, outs):
            if left <= head * HEAD_WIDTH < left + wide:
                at = head * HEAD_WIDTH - left
                out[:, at : at + HEAD_WIDTH] = part[top : top + height]


def rotate(pre, bias, cosine, sine, turned_heads, splits, sign):
    return pl.pallas_call(
        functools.partial(rotate_kernel, tuple(turned_heads), splits, sign),
        out_shape=tuple(
            jax.ShapeDtypeStruct((height, wide), BF16) for _, height, _, wide in splits
        ),
        cost_estimate=pl.CostEstimate(flops=0, bytes_accessed=8 * pre.size, transcendentals=0),
        name="rotate",
    )(pre, bias, cosine, sine)


def cut_kernel(far, whole, *refs):
    count = len(refs) // 2
    for source, out in zip(refs[:count], refs[count:]):
        small = (out if whole else source).shape[1] // (8 * far)
        for h in range(far):
            for g in range(8):
                left, right = (h * 8 + g) * small, h * small
                if whole:
                    out[:, left : left + small] = source[g, :, right : right + small].astype(F32)
                else:
                    out[g, :, right : right + small] = source[:, left : left + small]


def cut_columns(far, whole, arrays):
    shapes = []
    for array in arrays:
        if whole:
            shapes.append(jax.ShapeDtypeStruct((array.shape[1], 8 * array.shape[2]), F32))
        else:
            shape = (8, array.shape[0], array.shape[1] // 8)
            shapes.append(jax.ShapeDtypeStruct(shape, array.dtype))
    return pl.pallas_call(
        functools.partial(cut_kernel, far, whole),
        out_shape=tuple(shapes),
        name="join_columns" if whole else "cut_columns",
    )(*arrays)


MESH = pl.DeviceIdType.MESH
PARTS = {"pair": 4, "pair8": 8}
COST = 1024
ANY = pl.BlockSpec(memory_space=pl.ANY)


class Local:
    def __init__(self, source, buffer, target, sems):
        self.load = pltpu.make_async_copy(source, buffer, sems.at[0])
        self.store = pltpu.make_async_copy(buffer, target, sems.at[1])

    def start(self):
        self.load.start()

    def turn(self):
        self.load.wait()
        self.store.start()

    def wait(self):
        self.store.wait()


class Copies:
    def __init__(self, send_sems, recv_sems):
        self.send_sems, self.recv_sems, self.started = send_sems, recv_sems, []

    def start(self, source, target, device):
        number = len(self.started)
        copy = pltpu.make_async_remote_copy(
            src_ref=source,
            dst_ref=target,
            send_sem=self.send_sems.at[number],
            recv_sem=self.recv_sems.at[number],
            device_id=device,
            device_id_type=MESH,
        )
        copy.start()
        self.started.append(copy)
        return copy


def greet(devices):
    barrier = pltpu.get_barrier_semaphore()
    for device in devices:
        pl.semaphore_signal(barrier, inc=1, device_id=device, device_id_type=MESH)
    pl.semaphore_wait(barrier, len(devices))


def other_h(far, k):
    return {"h": lax.rem(lax.axis_index("h") + k, far)}


def flip(*axes):
    return {axis: 1 - lax.axis_index(axis) for axis in axes}


def corners():
    return [flip("p", "y"), flip("p", "c"), flip("y", "c"), flip("p", "y", "c")]


def gather_steps(kind, far, copies, source, out, local):
    ih, ip, iy, ic, ix = (lax.axis_index(name) for name in ("h", "p", "y", "c", "x"))
    every = kind in ("all", "all_y")

    def block(h, p, y=iy, x=ix):
        return out.at[h, p, y, ic, x] if every else out.at[h, p, y, ic]

    local.start()
    pieces = [(lax.rem(ih - k + far, far), p) for p in (ip, 1 - ip) for k in range(far)]
    count = len(pieces)
    arrivals, plane, cross, core = [None] * count, [None] * count, [None] * count, [None] * count
    columns = source.shape[-1]
    half = columns // 2 if columns % 256 == 0 and kind == "all" else columns

    def cut(ref, first):
        if half == columns:
            return ref
        return ref.at[:, pl.ds(0 if first else half, half)]

    for k in range(1, far):
        arrivals[k] = copies.start(source, block(ih, ip), other_h(far, k))
    for step in range(count + 3):
        if step < count:
            if arrivals[step] is not None:
                arrivals[step].wait_recv()
            h, p = pieces[step]
            held = source if step == 0 else block(h, p)
            if step < far:
                arrivals[far + step] = copies.start(held, block(h, p), flip("p"))
            plane[step] = [copies.start(held, block(h, p), flip("y"))]
            if every:
                plane[step].append(copies.start(held, block(h, p), flip("x")))
        if 0 <= step - 1 < count:
            h, p = pieces[step - 1]
            for copy in plane[step - 1]:
                copy.wait_recv()
            cross[step - 1] = []
            if every:
                ref = cut(block(h, p, x=1 - ix), True)
                cross[step - 1].append(copies.start(ref, ref, flip("y")))
                if half < columns:
                    ref = cut(block(h, p, y=1 - iy), False)
                    cross[step - 1].append(copies.start(ref, ref, flip("x")))
        if 0 <= step - 2 < count:
            h, p = pieces[step - 2]
            for copy in cross[step - 2]:
                copy.wait_recv()
            if step == 2:
                local.wait()
            ref = out.at[h, p, :, ic]
            core[step - 2] = copies.start(ref, ref, flip("c"))
        if 0 <= step - 3 < count:
            core[step - 3].wait_recv()
        yield


def group_steps(far, copies, source, out, local, delay):
    ip, iy, ic = (lax.axis_index(name) for name in ("p", "y", "c"))
    half = source.shape[0] // 2
    top, low = pl.ds(0, half), pl.ds(half, half)

    def rows(p, y, part):
        return out.at[p, y, ic, part]

    def forward(ref, axis):
        return copies.start(ref, ref, flip(axis))

    local.start()
    for _ in range(delay):
        yield
    first = [
        copies.start(source.at[top], rows(ip, iy, top), flip("y")),
        copies.start(source.at[low], rows(ip, iy, low), flip("p")),
    ]
    second = [
        copies.start(source.at[top], rows(ip, iy, top), flip("p")),
        copies.start(source.at[low], rows(ip, iy, low), flip("y")),
    ]
    core = [copies.start(source, out.at[ip, iy, ic], flip("c"))]
    yield
    first[0].wait_recv()
    second.append(forward(rows(ip, 1 - iy, top), "p"))
    core.append(forward(rows(ip, 1 - iy, top), "c"))
    first[1].wait_recv()
    second.append(forward(rows(1 - ip, iy, low), "y"))
    core.append(forward(rows(1 - ip, iy, low), "c"))
    yield
    for copy, p, y, part in (
        (second[0], 1 - ip, iy, top),
        (second[1], ip, 1 - iy, low),
        (second[2], 1 - ip, 1 - iy, top),
        (second[3], 1 - ip, 1 - iy, low),
    ):
        copy.wait_recv()
        core.append(forward(rows(p, y, part), "c"))
    yield
    for copy in core:
        copy.wait_recv()
    local.wait()


def pair_steps(far, copies, parts, place, local, delay):
    ih, ix = lax.axis_index("h"), lax.axis_index("x")
    local.start()
    for _ in range(delay):
        yield
    arrived, sent = [], []

    def send(i):
        if i < len(parts):
            target = place(ih, ix, i)
            arrived.append([copies.start(parts[i], target, other_h(far, k)) for k in range(1, far)])
            sent.append(copies.start(parts[i], target, flip("x")))

    ahead = len(parts) // 2
    for i in range(ahead):
        send(i)
    for i in range(len(parts)):
        yield
        send(i + ahead)
        for k in range(1, far):
            arrived[i][k - 1].wait_recv()
            ref = place(lax.rem(ih - k + far, far), ix, i)
            sent.append(copies.start(ref, ref, flip("x")))
    yield
    for copy in sent:
        copy.wait_recv()
    local.wait()


def spread_steps(far, copies, source, out, local, delay):
    ip, iy, ic = (lax.axis_index(name) for name in ("p", "y", "c"))
    me = (ip * 2 + iy) * 2 + ic
    local.start()
    for _ in range(delay):
        yield
    started = []
    for j in (1, 2, 4, 3, 5, 6, 7):
        p = 1 - ip if j & 4 else ip
        y = 1 - iy if j & 2 else iy
        c = 1 - ic if j & 1 else ic
        started.append(
            copies.start(source.at[(p * 2 + y) * 2 + c], out.at[me], {"p": p, "y": y, "c": c})
        )
    for _ in range(2 * far + 2):
        yield
    for copy in started:
        copy.wait_recv()
    local.wait()
    yield


def move_kernel(kinds, far, *refs):
    count = len(kinds)
    sources, outs = refs[:count], refs[count : 2 * count]
    buffers = refs[2 * count : 3 * count]
    send_sems, recv_sems, local_sems = refs[3 * count :]
    locals_ = []

    def local_copy(i, source, target):
        locals_.append(Local(source, buffers[i], target, local_sems.at[i]))
        return locals_[-1]

    ih, ip, iy, ic, ix = (lax.axis_index(name) for name in ("h", "p", "y", "c", "x"))
    partners = [flip("p"), flip("y"), flip("c")]
    if set(kinds) - {"spread", "group"}:
        partners += [other_h(far, k) for k in range(1, far)]
    if set(kinds) - {"seq", "group", "spread"}:
        partners.append(flip("x"))
    if "spread" in kinds:
        partners += corners()
    greet(partners)
    copies = Copies(send_sems, recv_sems)
    running = []
    for i, kind in enumerate(kinds):
        if kind == "spread":
            me = (ip * 2 + iy) * 2 + ic
            local = local_copy(i, sources[i].at[me], outs[i].at[me])
            running.append(spread_steps(far, copies, sources[i], outs[i], local, 0))
        elif kind == "group":
            place = outs[i].at[ip, iy, ic]
            local = local_copy(i, sources[i], place)
            delay = 3 if count > 1 else 0
            running.append(group_steps(far, copies, sources[i], outs[i], local, delay))
        elif kind in ("pair", "pair8"):
            local = outs[i].at[ih, :, ix] if kind == "pair8" else outs[i].at[ih, ix]
            local = local_copy(i, sources[i], local)
            step = (8 if kind == "pair8" else sources[i].shape[1]) // PARTS[kind]
            cuts = [pl.ds(part * step, step) for part in range(PARTS[kind])]
            if kind == "pair8":
                parts = [sources[i].at[c] for c in cuts]
            else:
                parts = [sources[i].at[:, c] for c in cuts]

            def place(h, x, part, out=outs[i], cuts=cuts, wide=kind == "pair8"):
                return out.at[h, cuts[part], x] if wide else out.at[h, x, :, cuts[part]]

            wait = (PARTS[kind] // 2 + 1) * kinds[:i].count("pair8")
            running.append(pair_steps(far, copies, parts, place, local, wait))
        else:
            place = (ih, ip, iy, ic) if kind == "seq" else (ih, ip, iy, ic, ix)
            local = local_copy(i, sources[i], outs[i].at[place])
            running.append(gather_steps(kind, far, copies, sources[i], outs[i], local))
    running = [job for job in running if next(job, "end") != "end"]
    for local in locals_:
        local.turn()
    while running:
        running = [job for job in running if next(job, "end") != "end"]
    for copy in copies.started:
        copy.wait_send()


def move(name, number, far, fsdp, kinds, arrays):
    shapes, total = [], 0
    pieces = 2 * far
    for kind, array in zip(kinds, arrays):
        if kind in ("all", "all_y"):
            lead, total = (far, 2, 2, 2, fsdp), total + (far - 1) + far + 5 * pieces
        elif kind == "seq":
            lead, total = (far, 2, 2, 2), total + (far - 1) + far + 2 * pieces
        elif kind == "group":
            lead, total = (2, 2, 2), total + 13
        elif kind == "pair":
            lead, total = (far, fsdp), total + PARTS[kind] * (2 * far - 1)
        elif kind == "pair8":
            lead, total = (far, 8, fsdp), total + PARTS[kind] * (2 * far - 1)
        else:
            lead, total = (), total + 7
        tail = array.shape[1:] if kind == "pair8" else array.shape
        shapes.append(jax.ShapeDtypeStruct(lead + tail, array.dtype))
    return pl.pallas_call(
        functools.partial(move_kernel, kinds, far),
        out_shape=tuple(shapes),
        in_specs=[ANY] * len(arrays),
        out_specs=tuple([ANY] * len(arrays)),
        scratch_shapes=[
            pltpu.VMEM(a.shape[1:] if kind == "spread" else a.shape, a.dtype)
            for kind, a in zip(kinds, arrays)
        ]
        + [
            pltpu.SemaphoreType.DMA((total,)),
            pltpu.SemaphoreType.DMA((total,)),
            pltpu.SemaphoreType.DMA((len(arrays), 2)),
        ],
        compiler_params=pltpu.CompilerParams(collective_id=number, has_side_effects=True),
        cost_estimate=pl.CostEstimate(flops=0, bytes_accessed=COST, transcendentals=0),
        name=name,
    )(*arrays)


def reduce_plan(kind, far, fsdp, tail):
    rows, columns = tail
    if kind == "group":
        step = rows // 4
        return ("p", "y"), [
            ((pl.ds(i * step, step), slice(None)), (step, columns), ("yp", "py")[i % 2])
            for i in range(4)
        ]
    if kind in ("seq", "seq_turned"):
        order = ("y", "p", "h") if kind == "seq" else ("p", "y", "h")
        return ("h", "p", "y"), [((slice(None), slice(None)), tail, order)]
    names = ("h", "p", "y", "x")
    if columns % 256:
        return names, [((slice(None), slice(None)), tail, ("x", "y", "p", "h"))]
    count = 4 if columns % 512 == 0 else 2
    step = columns // count
    orders = (("x", "y", "p", "h"), ("y", "x", "p", "h")) if kind == "all" else (("x", "y", "p", "h"),) * 2
    return names, [
        ((slice(None), pl.ds(i * step, step)), (rows, step), orders[i % 2]) for i in range(count)
    ]


def reduce_shapes(kind, far, fsdp, tail, dtype):
    length = {"h": far, "p": 2, "y": 2, "x": fsdp}
    names, parts = reduce_plan(kind, far, fsdp, tail)
    shapes = []
    for _, small, order in parts:
        left = list(names)
        full = tuple(length[n] for n in left) + small
        shapes += [full, full]
        for axis in order:
            left.remove(axis)
            lead = tuple(length[n] for n in left) + small
            shapes.append((far - 1,) + lead if axis == "h" else lead)
    return shapes


def reduce_steps(kind, far, fsdp, copies, source, out, scratch, local_sem):
    place = {name: lax.axis_index(name) for name in ("h", "p", "y", "x")}
    ic = lax.axis_index("c")
    length = {"h": far, "p": 2, "y": 2, "x": fsdp}
    core_dim = 2 if kind == "group" else 3
    names, parts = reduce_plan(kind, far, fsdp, out.shape)
    jobs, position = [], 0
    for cut, small, order in parts:
        count = 2 + len(order)
        jobs.append((cut, small, order, scratch[position : position + count]))
        position += count

    def view(c, cut):
        lead = [slice(None)] * core_dim + [c] + [slice(None)] * (len(names) - core_dim)
        return source.at[tuple(lead) + cut]

    def add(sums, brought, fixed, left, target=None, also=()):
        sizes = [1 if n in also else length[n] for n in left]
        total = 1
        for size in sizes:
            total *= size

        def one(number, _):
            index, rest = {}, number
            for n, size in reversed(list(zip(left, sizes))):
                index[n] = also[n] if n in also else rest % size
                rest = rest // size
            whole = tuple(fixed[n] if n in fixed else index[n] for n in names)
            value = sums[whole].astype(F32) + brought[tuple(index[n] for n in left)].astype(F32)
            if target is None:
                sums[whole] = value.astype(sums.dtype)
            else:
                target(value)
            return 0

        if total == 1:
            one(0, 0)
        else:
            lax.fori_loop(0, total, one, 0)

    loads, sent = [], []
    for i, (cut, small, order, refs) in enumerate(jobs):
        loads.append(pltpu.make_async_copy(view(ic, cut), refs[0], local_sem.at[i]))
        loads[i].start()
        sent.append(copies.start(view(1 - ic, cut), refs[1], flip("c")))
    yield
    for stage in range(len(jobs[0][2]) + 1):
        for i, (cut, small, order, refs) in enumerate(jobs):
            sums, brought = refs[0], refs[1 + stage]
            done = order[:stage]
            left = tuple(n for n in names if n not in done)
            fixed = {n: place[n] for n in done}
            if stage == 0:
                loads[i].wait()
            if stage > 0 and order[stage - 1] == "h":
                for copy in sent[i]:
                    copy.wait_recv()
            else:
                sent[i].wait_recv()
            if stage == len(order):
                if order[-1] == "h":
                    whole = tuple(place[n] for n in names)
                    value = sums[whole].astype(F32)
                    for k in range(far - 1):
                        value = value + brought[k].astype(F32)
                    out[cut] = value
                else:

                    def put(value, cut=cut):
                        out[cut] = value

                    add(sums, brought, fixed, left, put)
                continue
            axis = order[stage]
            if axis == "h":
                add(sums, brought, fixed, left)
                sent[i] = []
                for k in range(1, far):
                    goal = lax.rem(place["h"] + k, far)
                    whole = tuple(goal if n == "h" else place[n] for n in names)
                    sent[i].append(
                        copies.start(sums.at[whole], refs[2 + stage].at[k - 1], other_h(far, k))
                    )
            else:
                add(sums, brought, fixed, left, also={axis: 1 - place[axis]})
                index = tuple(
                    1 - place[n] if n == axis else fixed.get(n, slice(None)) for n in names
                )
                sent[i] = copies.start(sums.at[index], refs[2 + stage], flip(axis))
                add(sums, brought, fixed, left, also={axis: place[axis]})
        yield


def reduce_kernel(kinds, far, fsdp, counts, *refs):
    n = len(kinds)
    sources, outs = refs[:n], refs[n : 2 * n]
    scratch = refs[2 * n : -3]
    send_sems, recv_sems, local_sems = refs[-3:]
    partners = [flip("p"), flip("y"), flip("c")]
    if set(kinds) - {"group", "spread"}:
        partners += [other_h(far, k) for k in range(1, far)]
    if "all" in kinds or "all_x" in kinds:
        partners.append(flip("x"))
    if "spread" in kinds:
        partners += corners()
    greet(partners)
    copies = Copies(send_sems, recv_sems)
    running, position = [], 0
    for i, kind in enumerate(kinds):
        if kind == "spread":
            me = (lax.axis_index("p") * 2 + lax.axis_index("y")) * 2 + lax.axis_index("c")
            local = pltpu.make_async_copy(
                sources[i].at[me], outs[i].at[me], local_sems.at[i, 0]
            )
            running.append(spread_steps(far, copies, sources[i], outs[i], local, 1))
            continue
        part = scratch[position : position + counts[i]]
        position += counts[i]
        running.append(
            reduce_steps(
                kind, far, fsdp, copies, sources[i], outs[i], part, local_sems.at[i]
            )
        )
    while running:
        running = [job for job in running if next(job, "end") != "end"]
    for copy in copies.started:
        copy.wait_send()


def reduce(name, number, far, fsdp, kinds, arrays):
    shapes, scratch, counts, total = [], [], [], 0
    for kind, array in zip(kinds, arrays):
        if kind == "spread":
            shapes.append(jax.ShapeDtypeStruct(array.shape, array.dtype))
            counts.append(0)
            total += 7
            continue
        tail = array.shape[-2:]
        parts = reduce_plan(kind, far, fsdp, tail)[1]
        own = reduce_shapes(kind, far, fsdp, tail, array.dtype)
        counts.append(len(own))
        scratch += [pltpu.VMEM(shape, array.dtype) for shape in own]
        shapes.append(jax.ShapeDtypeStruct(tail, F32))
        total += sum(1 + len(order) + (far - 2 if "h" in order else 0) for _, _, order in parts)
    return pl.pallas_call(
        functools.partial(reduce_kernel, kinds, far, fsdp, tuple(counts)),
        out_shape=tuple(shapes),
        in_specs=[ANY] * len(arrays),
        out_specs=tuple(
            ANY if kind == "spread" else pl.BlockSpec(memory_space=pltpu.VMEM) for kind in kinds
        ),
        scratch_shapes=scratch
        + [
            pltpu.SemaphoreType.DMA((total,)),
            pltpu.SemaphoreType.DMA((total,)),
            pltpu.SemaphoreType.DMA((len(arrays), 4)),
        ],
        compiler_params=pltpu.CompilerParams(collective_id=number, has_side_effects=True),
        cost_estimate=pl.CostEstimate(flops=0, bytes_accessed=COST, transcendentals=0),
        name=name,
    )(*arrays)


def body(
    sizes,
    inputs,
    lengths,
    attn_gain,
    query_weight,
    query_bias,
    key_matrix,
    key_bias_vector,
    value_matrix,
    value_bias_vector,
    output_weight,
    mlp_gain,
    gate_weight,
    up_weight,
    down_weight,
    cotangent,
):
    far, fsdp = sizes
    micro, token_rows, width = inputs.shape[1:]
    shard = query_weight.shape[0]
    kv_width = key_matrix.shape[1]
    hidden_width = gate_weight.shape[1]
    devices = far * 8 * fsdp
    seq = far * 8
    ih, ip, iy, ic, ix = (lax.axis_index(name) for name in ("h", "p", "y", "c", "x"))
    me8 = (ip * 2 + iy) * 2 + ic
    me_seq = ih * 8 + me8

    def hop(array, axis, shift=1):
        if axis == "h":
            return lax.ppermute(array, "h", [(i, (i + shift) % far) for i in range(far)])
        return lax.ppermute(array, axis, SWAP)

    def pick(array, index, axis):
        return lax.dynamic_index_in_dim(array, index, axis, keepdims=False)

    slice_width = hidden_width // 8

    gate_cut, up_cut = cut_columns(far, False, (gate_weight, up_weight))

    vectors = jnp.concatenate(
        [attn_gain, query_bias, key_bias_vector, value_bias_vector, mlp_gain]
    ).astype(F32)
    vectors = jnp.pad(vectors, (0, 1024 - vectors.shape[0])).reshape(8, 128)
    w_qkv, vectors, gate_parts, up_parts, w_down = move(
        "gather_first",
        0,
        far,
        fsdp,
        ("all_y", "all", "spread", "spread", "pair"),
        (
            jnp.concatenate([query_weight, key_matrix, value_matrix], axis=1),
            vectors,
            gate_cut,
            up_cut,
            down_weight,
        ),
    )
    w_down = w_down.reshape(slice_width, width)
    w_qkv = w_qkv.reshape(width, -1)
    vectors = vectors.reshape(devices, 1024)
    cuts = [0]
    for part in (attn_gain, query_bias, key_bias_vector, value_bias_vector, mlp_gain):
        cuts.append(cuts[-1] + part.shape[0])
    gain_attn, b_query, b_key, b_value, gain_mlp = (
        vectors[:, cuts[i] : cuts[i + 1]].reshape(-1) for i in range(5)
    )
    rows = inputs[0].astype(F32).reshape(micro * token_rows, width)
    upstream_low = cotangent[0].reshape(micro * token_rows, width)
    positions_at = me_seq * token_rows + jnp.arange(token_rows, dtype=jnp.int32)
    tables, spans, metas = [], [], []
    for number in range(micro):
        offsets, first = locate(lengths[0, number], positions_at)
        tables.append(rotary_tables(offsets, HEAD_WIDTH))
        spans.append(
            jnp.concatenate(
                [
                    jnp.tile(first, GROUP)[None],
                    jnp.tile(positions_at, GROUP)[None],
                    jnp.zeros((6, GROUP * token_rows), jnp.int32),
                ],
                axis=0,
            )
        )
        low = jnp.maximum(first[0] // token_rows, me_seq - seq // 2)
        metas.append(jnp.stack([low, me_seq]).astype(jnp.int32))
    cosine_table = jnp.concatenate([t[0] for t in tables], axis=0)
    sine_table = jnp.concatenate([t[1] for t in tables], axis=0)

    normed, recip_one = rms_forward(rows, gain_attn)
    normed_low = normed.astype(BF16)
    pre = mat_dot(normed_low, w_qkv)
    heads = range(QUERY_HEADS + KEY_VALUE_HEADS)
    splits = ((0, micro * token_rows, 0, width),) + tuple(
        (m * token_rows, token_rows, width, 2 * kv_width) for m in range(micro)
    )
    biases = jnp.concatenate([b_query, b_key, b_value])[None]
    query_rotated, *own_kv = rotate(pre, biases, cosine_table, sine_table, heads, splits, 1.0)
    moved = move(
        "gather_second",
        1,
        far,
        fsdp,
        ("seq",) * micro + ("all_y", "pair8", "pair8", "group"),
        tuple(own_kv) + (output_weight, gate_parts, up_parts, upstream_low),
    )
    stacks = [part.reshape(seq, token_rows, 2 * kv_width) for part in moved[:micro]]
    w_output = moved[micro].reshape(width, width)
    w_gate, w_up = (part.reshape(width, slice_width) for part in moved[micro + 1 : micro + 3])
    upstream_all = moved[micro + 3].reshape(-1, width)
    attended, lses = [], []
    for m in range(micro):
        result, lse = attend_forward(m, metas[m], query_rotated, stacks[m], spans[m])
        attended.append(result)
        lses.append(lse)
    attended = jnp.concatenate(attended, axis=0)
    middle = rows + mat_dot(attended, w_output)
    normed_two, recip_two = rms_forward(middle, gain_mlp)
    (tokens,) = move("gather_tokens", 2, far, fsdp, ("group",), (normed_two.astype(BF16),))
    tokens = tokens.reshape(-1, width)

    tokens_turned, hidden, hidden_turned, grad_gate, grad_up = hidden_units(
        micro * token_rows, tokens, upstream_all, w_gate, w_up, w_down
    )
    group = (2, 2, 2, micro * token_rows, width)

    def over_x(grad, axis, other):
        grad = grad.astype(BF16)
        sent, other = lax.optimization_barrier((pick(grad, 1 - ix, axis), other))
        kept = pick(grad, ix, axis).astype(F32) + hop(sent, "x").astype(F32)
        return kept.astype(BF16), other

    def over_h(kept):
        total = pick(kept, ih, 0).astype(F32)
        for k in range(1, far):
            total = total + hop(pick(kept, (ih + k) % far, 0), "h", k).astype(F32)
        return total

    eight = (far, 8, fsdp, shard, slice_width)
    turned = tokens_turned.reshape(far, 8, fsdp, shard, -1)
    gate_sum, grad_up_last = over_x(dot(turned, grad_gate, ((4,), (0,))), 2, grad_up)
    up_sum, _ = over_x(dot(turned, grad_up_last, ((4,), (0,))), 2, ())
    grad_two = (cols_dot(grad_gate, w_gate) + cols_dot(grad_up, w_up)).astype(BF16)

    (grad_two,) = reduce("reduce_tokens", 3, far, fsdp, ("group",), (grad_two.reshape(group),))
    grad_norm, gain_mlp_sum = rms_backward(middle, recip_two, gain_mlp, grad_two)
    grad_middle = upstream_low.astype(F32) + grad_norm
    grad_branch = grad_middle.astype(BF16)
    grad_branch, gate_sum, up_sum = lax.optimization_barrier((grad_branch, gate_sum, up_sum))
    gate_sum = over_h(gate_sum).astype(BF16)
    grad_attended = cols_dot(grad_branch, w_output).astype(BF16)
    grad_kvs, grad_query = [], []
    for m in range(micro):
        query_part, grad_kv = attend_backward(
            m,
            metas[m],
            query_rotated,
            grad_attended,
            stacks[m],
            spans[m],
            lses[m],
            cosine_table,
            sine_table,
        )
        grad_kvs.append(grad_kv.reshape(far, 2, 2, 2, token_rows, 2 * kv_width))
        grad_query.append(query_part)

    blocks = (far, 2, 2, 2, fsdp, shard)
    grad_kvs, gate_sum, up_sum, hidden, hidden_turned = lax.optimization_barrier(
        (grad_kvs, gate_sum, up_sum, hidden, hidden_turned)
    )
    up_sum = over_h(up_sum).astype(BF16)
    down_part, _ = over_x(
        mat_dot(hidden_turned, upstream_all).reshape(far, fsdp, -1, width), 1, ()
    )
    final = mat_dot(hidden, w_down).astype(BF16)
    g_output = rows_dot(attended, grad_branch).astype(BF16)
    reduced = reduce(
        "reduce_second",
        4,
        far,
        fsdp,
        ("group", "all_x") + tuple("seq_turned" if m % 2 else "seq" for m in range(micro)),
        (final.reshape(group), g_output.reshape(blocks + (width,))) + tuple(grad_kvs),
    )
    grad_kvs, output_part = list(reduced[2:]), reduced[1]
    grad_kvs[0], down_part = lax.optimization_barrier((grad_kvs[0], down_part))
    down_part = over_h(down_part)
    results = (middle + reduced[0]).astype(BF16)
    grad_query = jnp.concatenate(grad_query, axis=0)
    grad_kv = jnp.concatenate(grad_kvs, axis=0)
    (grad_kv,) = rotate(
        grad_kv,
        jnp.zeros((1, 2 * kv_width), F32),
        cosine_table,
        sine_table,
        range(KEY_VALUE_HEADS),
        ((0, micro * token_rows, 0, 2 * kv_width),),
        -1.0,
    )
    grad_pre = jnp.concatenate([grad_query, grad_kv], axis=1)
    grad_normed = cols_dot(grad_pre, w_qkv)
    grad_rows, gain_attn_sum = rms_backward(rows, recip_one, gain_attn, grad_normed)
    input_grad = grad_middle + grad_rows
    g_qkv = rows_dot(normed_low, grad_pre).astype(BF16)
    bias_sum = jnp.sum(grad_pre.astype(F32), axis=0)
    vector_sums = jnp.concatenate(
        [
            v.reshape(devices, -1)
            for v in (
                gain_attn_sum,
                bias_sum[:width],
                bias_sum[width : width + kv_width],
                bias_sum[width + kv_width :],
                gain_mlp_sum,
            )
        ],
        axis=1,
    )
    vector_sums = jnp.pad(vector_sums, ((0, 0), (0, 1024 - vector_sums.shape[1])))
    qkv_part, vector_part, gate_sum, up_sum = reduce(
        "reduce_last",
        5,
        far,
        fsdp,
        ("all", "all", "spread", "spread"),
        (
            g_qkv.reshape(blocks + (-1,)),
            vector_sums.reshape(far, 2, 2, 2, fsdp, 8, 128),
            gate_sum,
            up_sum,
        ),
    )
    vector_part = vector_part.reshape(-1)

    gate_grad, up_grad = cut_columns(far, True, (gate_sum, up_sum))

    return (
        results.reshape(1, micro, token_rows, width),
        input_grad.reshape(1, micro, token_rows, width),
        vector_part[cuts[0] : cuts[1]],
        qkv_part[:, :width],
        vector_part[cuts[1] : cuts[2]],
        qkv_part[:, width : width + kv_width],
        vector_part[cuts[2] : cuts[3]],
        qkv_part[:, width + kv_width :],
        vector_part[cuts[3] : cuts[4]],
        output_part,
        vector_part[cuts[4] : cuts[5]],
        gate_grad,
        up_grad,
        down_part,
    )


def solution(mesh):
    fsdp = mesh.shape["fsdp"]
    far = mesh.shape["seq"] // 8
    inner = Mesh(mesh.devices.reshape(far, 2, 2, 2, fsdp), ("h", "p", "y", "c", "x"))
    seq = ("h", "p", "y", "c")
    every = seq + ("x",)
    tokens = P("x", None, seq, None)
    matrix, vector = P(every, None), P(every)
    in_specs = (
        tokens,
        P("x", None, None),
        vector,
        matrix,
        vector,
        matrix,
        vector,
        matrix,
        vector,
        matrix,
        vector,
        matrix,
        matrix,
        matrix,
        tokens,
    )
    out_specs = (
        tokens,
        tokens,
        vector,
        matrix,
        vector,
        matrix,
        vector,
        matrix,
        vector,
        matrix,
        vector,
        matrix,
        matrix,
        matrix,
    )
    return jax.shard_map(
        functools.partial(body, (far, fsdp)),
        mesh=inner,
        in_specs=in_specs,
        out_specs=out_specs,
        check_vma=False,
    )
```

```python
import functools

import jax
import jax.numpy as jnp
from jax import lax
from jax.experimental import pallas as pl
from jax.experimental.pallas import tpu as pltpu
from jax.sharding import Mesh, PartitionSpec as P

QUERY_HEADS = 12
KEY_VALUE_HEADS = 2
HEAD_WIDTH = 128
EPSILON = 1e-06
THETA = 10000.0
GROUP = QUERY_HEADS // KEY_VALUE_HEADS
SCALE = HEAD_WIDTH ** (-0.5)
F32 = jnp.float32
BF16 = jnp.bfloat16
SWAP = [(0, 1), (1, 0)]


def locate(item_lengths, positions_at):
    ends = jnp.cumsum(item_lengths)
    starts = ends - item_lengths
    segment_ids = jnp.sum((ends[None, :] <= positions_at[:, None]).astype(jnp.int32), axis=1)
    onehot = segment_ids[:, None] == jnp.arange(item_lengths.shape[0], dtype=jnp.int32)[None, :]
    first = jnp.sum(jnp.where(onehot, starts[None, :], 0), axis=1)
    return (positions_at - first, first)


def rotary_tables(offsets, head_size):
    freqs = 1.0 / THETA ** (jnp.arange(0, head_size, 2, dtype=F32) / head_size)
    angles = offsets.astype(F32)[:, None] * freqs[None, :]
    cosine, sine = jnp.cos(angles), jnp.sin(angles)
    return (jnp.concatenate([cosine, cosine], axis=1), jnp.concatenate([-sine, sine], axis=1))


def rms_forward(rows, gain):
    recip = lax.rsqrt(jnp.mean(rows * rows, axis=-1, keepdims=True) + EPSILON)
    return (rows * recip * gain, recip)


def rms_backward(rows, recip, gain, upstream):
    weighted = upstream * gain
    grad_rows = recip * weighted - rows * (recip * recip * recip) * jnp.mean(
        rows * weighted, axis=-1, keepdims=True
    )
    gain_grad = jnp.sum(upstream * rows * recip, axis=0)
    return (grad_rows, gain_grad)


def dot(left, right, dims, out=F32):
    return lax.dot_general(left, right, ((dims[0], dims[1]), ((), ())), preferred_element_type=out)


def rows_dot(left, right):
    return dot(left, right, ((0,), (0,)))


def cols_dot(left, right):
    return dot(left, right, ((1,), (1,)))


def mat_dot(left, right):
    return dot(left, right, ((1,), (0,)))


def attend_forward_kernel(meta, q_ref, k_ref, v_ref, span_ref, o_ref, lse_ref):
    rows = q_ref.shape[0]
    queries = jnp.concatenate(
        [q_ref[:, h * HEAD_WIDTH : (h + 1) * HEAD_WIDTH] for h in range(GROUP)], axis=0
    )
    first, last = span_ref[0:1, :], span_ref[1:2, :]
    wide = GROUP * rows
    local = lax.broadcasted_iota(jnp.int32, (rows, 1), 0)

    def step(block, carry):
        top, total, accum = carry
        keys, values = k_ref[block], v_ref[block]
        scores = dot(keys, queries, ((1,), (1,))) * SCALE
        index = block * rows + local
        scores = jnp.where((index >= first) & (index <= last), scores, -1e30)
        new_top = jnp.maximum(top, jnp.max(scores, axis=0, keepdims=True))
        fade = jnp.exp(top - new_top)
        probs = jnp.exp(scores - new_top)
        total = total * fade + jnp.sum(probs, axis=0, keepdims=True)
        accum = accum * fade + dot(values, probs.astype(BF16), ((0,), (0,)))
        return (new_top, total, accum)

    top, total, accum = lax.fori_loop(
        meta[0],
        meta[1] + 1,
        step,
        (
            jnp.full((1, wide), -1e30, F32),
            jnp.zeros((1, wide), F32),
            jnp.zeros((HEAD_WIDTH, wide), F32),
        ),
    )
    attended = (accum / total).T.astype(BF16)
    for h in range(GROUP):
        o_ref[:, h * HEAD_WIDTH : (h + 1) * HEAD_WIDTH] = attended[h * rows : (h + 1) * rows]
    lse_ref[0] = top + jnp.log(total)


def attend_forward(number, meta, queries, stack, span):
    pieces, rows, _ = stack.shape
    width = queries.shape[1]
    part = width // KEY_VALUE_HEADS
    spec = pltpu.PrefetchScalarGridSpec(
        num_scalar_prefetch=1,
        grid=(KEY_VALUE_HEADS,),
        in_specs=[
            pl.BlockSpec((rows, part), lambda g, m: (number, g)),
            pl.BlockSpec((pieces, rows, HEAD_WIDTH), lambda g, m: (0, 0, g)),
            pl.BlockSpec((pieces, rows, HEAD_WIDTH), lambda g, m: (0, 0, KEY_VALUE_HEADS + g)),
            pl.BlockSpec((8, GROUP * rows), lambda g, m: (0, 0)),
        ],
        out_specs=[
            pl.BlockSpec((rows, part), lambda g, m: (0, g)),
            pl.BlockSpec((1, 1, GROUP * rows), lambda g, m: (g, 0, 0)),
        ],
    )
    return pl.pallas_call(
        attend_forward_kernel,
        grid_spec=spec,
        out_shape=(
            jax.ShapeDtypeStruct((rows, width), BF16),
            jax.ShapeDtypeStruct((KEY_VALUE_HEADS, 1, GROUP * rows), F32),
        ),
        cost_estimate=pl.CostEstimate(
            flops=4 * rows * rows * 6 * width, bytes_accessed=stack.size * 2, transcendentals=0
        ),
        name="attend_forward",
    )(meta, queries, stack, stack, span)


def attend_backward_kernel(
    meta, q_ref, do_ref, kv_ref, span_ref, lse_ref, cos_ref, sin_ref, dq_ref, dkv_ref, p_ref, dp_ref
):
    rows = q_ref.shape[0]
    wide = GROUP * rows
    first, last = span_ref[0:1, :], span_ref[1:2, :]
    local = lax.broadcasted_iota(jnp.int32, (rows, 1), 0)
    low = meta[0]
    cosine, sine = cos_ref[...], sin_ref[...]
    dkv_ref[...] = jnp.zeros_like(dkv_ref)
    for group in range(KEY_VALUE_HEADS):
        heads = range(group * GROUP, (group + 1) * GROUP)
        cols = [slice(h * HEAD_WIDTH, (h + 1) * HEAD_WIDTH) for h in heads]
        key_cols = slice(group * HEAD_WIDTH, (group + 1) * HEAD_WIDTH)
        start = (KEY_VALUE_HEADS + group) * HEAD_WIDTH
        value_cols = slice(start, start + HEAD_WIDTH)
        queries = jnp.concatenate([q_ref[:, c] for c in cols], axis=0)
        grads = jnp.concatenate([do_ref[:, c] for c in cols], axis=0)
        lse = lse_ref[group]

        def collect(block, delta):
            scores = dot(kv_ref[block, :, key_cols], queries, ((1,), (1,))) * SCALE
            index = block * rows + local
            probs = jnp.where((index >= first) & (index <= last), jnp.exp(scores - lse), 0.0)
            grad_probs = dot(kv_ref[block, :, value_cols], grads, ((1,), (1,)))
            p_ref[block - low] = probs
            dp_ref[block - low] = grad_probs
            return delta + jnp.sum(probs * grad_probs, axis=0, keepdims=True)

        delta = lax.fori_loop(low, meta[1] + 1, collect, jnp.zeros((1, wide), F32))

        def spread(block, accum):
            probs = p_ref[block - low]
            grad_scores = (probs * (dp_ref[block - low] - delta)).astype(BF16)
            dkv_ref[block, :, key_cols] = (mat_dot(grad_scores, queries) * SCALE).astype(BF16)
            dkv_ref[block, :, value_cols] = mat_dot(probs.astype(BF16), grads).astype(BF16)
            return accum + dot(kv_ref[block, :, key_cols], grad_scores, ((0,), (0,)))

        accum = lax.fori_loop(low, meta[1] + 1, spread, jnp.zeros((HEAD_WIDTH, wide), F32))
        grad_queries = (accum * SCALE).T
        for h in range(GROUP):
            part = grad_queries[h * rows : (h + 1) * rows]
            turned = pltpu.roll(part, HEAD_WIDTH // 2, 1)
            dq_ref[:, cols[h]] = (part * cosine - turned * sine).astype(BF16)


def attend_backward(number, meta, queries, grads, stack, span, lse, cosine, sine):
    pieces, rows, wide = stack.shape
    width = queries.shape[1]
    most = pieces // 2 + 1

    def own(columns):
        return pl.BlockSpec((rows, columns), lambda i, m: (number, 0))

    def whole(shape):
        return pl.BlockSpec(shape, lambda i, m: (0,) * len(shape))

    spec = pltpu.PrefetchScalarGridSpec(
        num_scalar_prefetch=1,
        grid=(1,),
        in_specs=[
            own(width),
            own(width),
            whole(stack.shape),
            whole(span.shape),
            whole(lse.shape),
            own(HEAD_WIDTH),
            own(HEAD_WIDTH),
        ],
        out_specs=[whole((rows, width)), whole(stack.shape)],
        scratch_shapes=[
            pltpu.VMEM((most, rows, GROUP * rows), F32),
            pltpu.VMEM((most, rows, GROUP * rows), F32),
        ],
    )
    return pl.pallas_call(
        attend_backward_kernel,
        grid_spec=spec,
        out_shape=(
            jax.ShapeDtypeStruct((rows, width), BF16),
            jax.ShapeDtypeStruct(stack.shape, BF16),
        ),
        cost_estimate=pl.CostEstimate(
            flops=0, bytes_accessed=COST, transcendentals=0
        ),
        name="attend_backward",
    )(meta, queries, grads, stack, span, lse, cosine, sine)


def hidden_kernel(
    token_ref,
    grad_ref,
    gate_ref,
    up_ref,
    down_ref,
    token_turned_ref,
    hidden_ref,
    turned_ref,
    dgate_ref,
    dup_ref,
):
    tokens = token_ref[...]
    token_turned_ref[...] = tokens.T
    gate_pre = mat_dot(tokens, gate_ref[...])
    up_pre = mat_dot(tokens, up_ref[...])
    grad_hidden = cols_dot(grad_ref[...], down_ref[...])
    sigma = jax.nn.sigmoid(gate_pre)
    activated = gate_pre * sigma
    hidden = activated * up_pre
    hidden_ref[...] = hidden.astype(BF16)
    turned_ref[...] = hidden.T.astype(BF16)
    dgate_ref[...] = (grad_hidden * up_pre * sigma * (1.0 + gate_pre * (1.0 - sigma))).astype(BF16)
    dup_ref[...] = (grad_hidden * activated).astype(BF16)


def hidden_units(rows, tokens, grads, w_gate, w_up, w_down):
    total, width = tokens.shape
    units = w_gate.shape[1]

    def tile(columns):
        return pl.BlockSpec((rows, columns), lambda i: (i, 0))

    def fixed(array):
        return pl.BlockSpec(array.shape, lambda i: (0, 0))

    return pl.pallas_call(
        hidden_kernel,
        grid=(total // rows,),
        in_specs=[tile(width), tile(width), fixed(w_gate), fixed(w_up), fixed(w_down)],
        out_specs=[
            pl.BlockSpec((width, rows), lambda i: (0, i)),
            tile(units),
            pl.BlockSpec((units, rows), lambda i: (0, i)),
            tile(units),
            tile(units),
        ],
        out_shape=(
            jax.ShapeDtypeStruct((width, total), BF16),
            jax.ShapeDtypeStruct((total, units), BF16),
            jax.ShapeDtypeStruct((units, total), BF16),
            jax.ShapeDtypeStruct((total, units), BF16),
            jax.ShapeDtypeStruct((total, units), BF16),
        ),
        cost_estimate=pl.CostEstimate(
            flops=6 * total * width * units, bytes_accessed=8 * total * width, transcendentals=0
        ),
        name="hidden_units",
    )(tokens, grads, w_gate, w_up, w_down)


def rotate_kernel(turned_heads, splits, sign, pre_ref, bias_ref, cos_ref, sin_ref, *outs):
    cosine, sine = cos_ref[...], sin_ref[...] * sign
    for head in range(pre_ref.shape[1] // HEAD_WIDTH):
        cols = slice(head * HEAD_WIDTH, (head + 1) * HEAD_WIDTH)
        part = pre_ref[:, cols] + bias_ref[:, cols]
        if head in turned_heads:
            part = part * cosine + pltpu.roll(part, HEAD_WIDTH // 2, 1) * sine
        part = part.astype(BF16)
        for (top, height, left, wide), out in zip(splits, outs):
            if left <= head * HEAD_WIDTH < left + wide:
                at = head * HEAD_WIDTH - left
                out[:, at : at + HEAD_WIDTH] = part[top : top + height]


def rotate(pre, bias, cosine, sine, turned_heads, splits, sign):
    return pl.pallas_call(
        functools.partial(rotate_kernel, tuple(turned_heads), splits, sign),
        out_shape=tuple(
            jax.ShapeDtypeStruct((height, wide), BF16) for _, height, _, wide in splits
        ),
        cost_estimate=pl.CostEstimate(flops=0, bytes_accessed=8 * pre.size, transcendentals=0),
        name="rotate",
    )(pre, bias, cosine, sine)


def cut_kernel(far, whole, *refs):
    count = len(refs) // 2
    for source, out in zip(refs[:count], refs[count:]):
        small = (out if whole else source).shape[1] // (8 * far)
        for h in range(far):
            for g in range(8):
                left, right = (h * 8 + g) * small, h * small
                if whole:
                    out[:, left : left + small] = source[g, :, right : right + small].astype(F32)
                else:
                    out[g, :, right : right + small] = source[:, left : left + small]


def cut_columns(far, whole, arrays):
    shapes = []
    for array in arrays:
        if whole:
            shapes.append(jax.ShapeDtypeStruct((array.shape[1], 8 * array.shape[2]), F32))
        else:
            shape = (8, array.shape[0], array.shape[1] // 8)
            shapes.append(jax.ShapeDtypeStruct(shape, array.dtype))
    return pl.pallas_call(
        functools.partial(cut_kernel, far, whole),
        out_shape=tuple(shapes),
        name="join_columns" if whole else "cut_columns",
    )(*arrays)


MESH = pl.DeviceIdType.MESH
PARTS = 4
COST = 1024
ANY = pl.BlockSpec(memory_space=pl.ANY)


class Local:
    def __init__(self, source, buffer, target, sems):
        self.load = pltpu.make_async_copy(source, buffer, sems.at[0])
        self.store = pltpu.make_async_copy(buffer, target, sems.at[1])

    def start(self):
        self.load.start()

    def turn(self):
        self.load.wait()
        self.store.start()

    def wait(self):
        self.store.wait()


class Copies:
    def __init__(self, send_sems, recv_sems):
        self.send_sems, self.recv_sems, self.started = send_sems, recv_sems, []

    def start(self, source, target, device):
        number = len(self.started)
        copy = pltpu.make_async_remote_copy(
            src_ref=source,
            dst_ref=target,
            send_sem=self.send_sems.at[number],
            recv_sem=self.recv_sems.at[number],
            device_id=device,
            device_id_type=MESH,
        )
        copy.start()
        self.started.append(copy)
        return copy


def greet(devices):
    barrier = pltpu.get_barrier_semaphore()
    for device in devices:
        pl.semaphore_signal(barrier, inc=1, device_id=device, device_id_type=MESH)
    pl.semaphore_wait(barrier, len(devices))


def other_h(far, k):
    return {"h": lax.rem(lax.axis_index("h") + k, far)}


def flip(*axes):
    return {axis: 1 - lax.axis_index(axis) for axis in axes}


def corners():
    return [flip("p", "y"), flip("p", "c"), flip("y", "c"), flip("p", "y", "c")]


def gather_steps(kind, far, copies, source, out, local):
    ih, ip, iy, ic, ix = (lax.axis_index(name) for name in ("h", "p", "y", "c", "x"))
    every = kind in ("all", "all_y")

    def block(h, p, y=iy, x=ix):
        return out.at[h, p, y, ic, x] if every else out.at[h, p, y, ic]

    local.start()
    pieces = [(lax.rem(ih - k + far, far), p) for p in (ip, 1 - ip) for k in range(far)]
    count = len(pieces)
    arrivals, plane, cross, core = [None] * count, [None] * count, [None] * count, [None] * count
    columns = source.shape[-1]
    half = columns // 2 if columns % 256 == 0 and kind == "all" else columns

    def cut(ref, first):
        if half == columns:
            return ref
        return ref.at[:, pl.ds(0 if first else half, half)]

    for k in range(1, far):
        arrivals[k] = copies.start(source, block(ih, ip), other_h(far, k))
    for step in range(count + 3):
        if step < count:
            if arrivals[step] is not None:
                arrivals[step].wait_recv()
            h, p = pieces[step]
            held = source if step == 0 else block(h, p)
            if step < far:
                arrivals[far + step] = copies.start(held, block(h, p), flip("p"))
            plane[step] = [copies.start(held, block(h, p), flip("y"))]
            if every:
                plane[step].append(copies.start(held, block(h, p), flip("x")))
        if 0 <= step - 1 < count:
            h, p = pieces[step - 1]
            for copy in plane[step - 1]:
                copy.wait_recv()
            cross[step - 1] = []
            if every:
                ref = cut(block(h, p, x=1 - ix), True)
                cross[step - 1].append(copies.start(ref, ref, flip("y")))
                if half < columns:
                    ref = cut(block(h, p, y=1 - iy), False)
                    cross[step - 1].append(copies.start(ref, ref, flip("x")))
        if 0 <= step - 2 < count:
            h, p = pieces[step - 2]
            for copy in cross[step - 2]:
                copy.wait_recv()
            if step == 2:
                local.wait()
            ref = out.at[h, p, :, ic]
            core[step - 2] = copies.start(ref, ref, flip("c"))
        if 0 <= step - 3 < count:
            core[step - 3].wait_recv()
        yield


def group_steps(far, copies, source, out, local, delay):
    ip, iy, ic = (lax.axis_index(name) for name in ("p", "y", "c"))
    half = source.shape[0] // 2
    top, low = pl.ds(0, half), pl.ds(half, half)

    def rows(p, y, part):
        return out.at[p, y, ic, part]

    def forward(ref, axis):
        return copies.start(ref, ref, flip(axis))

    local.start()
    for _ in range(delay):
        yield
    first = [
        copies.start(source.at[top], rows(ip, iy, top), flip("y")),
        copies.start(source.at[low], rows(ip, iy, low), flip("p")),
    ]
    second = [
        copies.start(source.at[top], rows(ip, iy, top), flip("p")),
        copies.start(source.at[low], rows(ip, iy, low), flip("y")),
    ]
    core = [copies.start(source, out.at[ip, iy, ic], flip("c"))]
    yield
    first[0].wait_recv()
    second.append(forward(rows(ip, 1 - iy, top), "p"))
    core.append(forward(rows(ip, 1 - iy, top), "c"))
    first[1].wait_recv()
    second.append(forward(rows(1 - ip, iy, low), "y"))
    core.append(forward(rows(1 - ip, iy, low), "c"))
    yield
    for copy, p, y, part in (
        (second[0], 1 - ip, iy, top),
        (second[1], ip, 1 - iy, low),
        (second[2], 1 - ip, 1 - iy, top),
        (second[3], 1 - ip, 1 - iy, low),
    ):
        copy.wait_recv()
        core.append(forward(rows(p, y, part), "c"))
    yield
    for copy in core:
        copy.wait_recv()
    local.wait()


def pair_steps(far, copies, parts, place, local, number):
    ih, ix = lax.axis_index("h"), lax.axis_index("x")
    local.start()
    count = len(parts)
    sent = [copies.start(parts[i], place(ih, ix, i), flip("x")) for i in range(count)]
    for _ in range(1 + number):
        yield
    arrived = [
        [copies.start(parts[i], place(ih, ix, i), other_h(far, k)) for k in range(1, far)]
        for i in range(count)
    ]
    for _ in range((count - 1) * number):
        yield
    for i in range(count):
        yield
        for k in range(1, far):
            arrived[i][k - 1].wait_recv()
            ref = place(lax.rem(ih - k + far, far), ix, i)
            sent.append(copies.start(ref, ref, flip("x")))
    yield
    for copy in sent:
        copy.wait_recv()
    local.wait()


def spread_steps(far, copies, source, out, local, delay):
    ip, iy, ic = (lax.axis_index(name) for name in ("p", "y", "c"))
    me = (ip * 2 + iy) * 2 + ic
    local.start()
    for _ in range(delay):
        yield
    started = []
    for j in (1, 2, 4, 3, 5, 6, 7):
        p = 1 - ip if j & 4 else ip
        y = 1 - iy if j & 2 else iy
        c = 1 - ic if j & 1 else ic
        started.append(
            copies.start(source.at[(p * 2 + y) * 2 + c], out.at[me], {"p": p, "y": y, "c": c})
        )
    for _ in range(2 * far + 2):
        yield
    for copy in started:
        copy.wait_recv()
    local.wait()
    yield


def move_kernel(kinds, far, *refs):
    count = len(kinds)
    sources, outs = refs[:count], refs[count : 2 * count]
    buffers = refs[2 * count : 3 * count]
    send_sems, recv_sems, local_sems = refs[3 * count :]
    locals_ = []

    def local_copy(i, source, target):
        locals_.append(Local(source, buffers[i], target, local_sems.at[i]))
        return locals_[-1]

    ih, ip, iy, ic, ix = (lax.axis_index(name) for name in ("h", "p", "y", "c", "x"))
    partners = [flip("p"), flip("y"), flip("c")]
    if set(kinds) - {"spread", "group"}:
        partners += [other_h(far, k) for k in range(1, far)]
    if set(kinds) - {"seq", "group", "spread"}:
        partners.append(flip("x"))
    if "spread" in kinds:
        partners += corners()
    greet(partners)
    copies = Copies(send_sems, recv_sems)
    running = []
    for i, kind in enumerate(kinds):
        if kind == "spread":
            me = (ip * 2 + iy) * 2 + ic
            local = local_copy(i, sources[i].at[me], outs[i].at[me])
            running.append(spread_steps(far, copies, sources[i], outs[i], local, 0))
        elif kind == "group":
            place = outs[i].at[ip, iy, ic]
            local = local_copy(i, sources[i], place)
            running.append(group_steps(far, copies, sources[i], outs[i], local, 0))
        elif kind in ("pair", "pair8"):
            local = outs[i].at[ih, :, ix] if kind == "pair8" else outs[i].at[ih, ix]
            local = local_copy(i, sources[i], local)
            step = (8 if kind == "pair8" else sources[i].shape[1]) // PARTS
            cuts = [pl.ds(part * step, step) for part in range(PARTS)]
            if kind == "pair8":
                parts = [sources[i].at[c] for c in cuts]
            else:
                parts = [sources[i].at[:, c] for c in cuts]

            def place(h, x, part, out=outs[i], cuts=cuts, wide=kind == "pair8"):
                return out.at[h, cuts[part], x] if wide else out.at[h, x, :, cuts[part]]

            number = kinds[:i].count("pair8")
            running.append(pair_steps(far, copies, parts, place, local, number))
        else:
            place = (ih, ip, iy, ic) if kind == "seq" else (ih, ip, iy, ic, ix)
            local = local_copy(i, sources[i], outs[i].at[place])
            running.append(gather_steps(kind, far, copies, sources[i], outs[i], local))
    running = [job for job in running if next(job, "end") != "end"]
    for local in locals_:
        local.turn()
    while running:
        running = [job for job in running if next(job, "end") != "end"]
    for copy in copies.started:
        copy.wait_send()


def move(name, number, far, fsdp, kinds, arrays):
    shapes, total = [], 0
    pieces = 2 * far
    for kind, array in zip(kinds, arrays):
        if kind in ("all", "all_y"):
            lead, total = (far, 2, 2, 2, fsdp), total + (far - 1) + far + 5 * pieces
        elif kind == "seq":
            lead, total = (far, 2, 2, 2), total + (far - 1) + far + 2 * pieces
        elif kind == "group":
            lead, total = (2, 2, 2), total + 13
        elif kind == "pair":
            lead, total = (far, fsdp), total + PARTS * (2 * far - 1)
        elif kind == "pair8":
            lead, total = (far, 8, fsdp), total + PARTS * (2 * far - 1)
        else:
            lead, total = (), total + 7
        tail = array.shape[1:] if kind == "pair8" else array.shape
        shapes.append(jax.ShapeDtypeStruct(lead + tail, array.dtype))
    return pl.pallas_call(
        functools.partial(move_kernel, kinds, far),
        out_shape=tuple(shapes),
        in_specs=[ANY] * len(arrays),
        out_specs=tuple([ANY] * len(arrays)),
        scratch_shapes=[
            pltpu.VMEM(a.shape[1:] if kind == "spread" else a.shape, a.dtype)
            for kind, a in zip(kinds, arrays)
        ]
        + [
            pltpu.SemaphoreType.DMA((total,)),
            pltpu.SemaphoreType.DMA((total,)),
            pltpu.SemaphoreType.DMA((len(arrays), 2)),
        ],
        compiler_params=pltpu.CompilerParams(collective_id=number, has_side_effects=True),
        cost_estimate=pl.CostEstimate(flops=0, bytes_accessed=COST, transcendentals=0),
        name=name,
    )(*arrays)


def reduce_plan(kind, far, fsdp, tail):
    rows, columns = tail
    if kind == "group":
        step = rows // 4
        return ("p", "y"), [
            ((pl.ds(i * step, step), slice(None)), (step, columns), ("yp", "py")[i % 2])
            for i in range(4)
        ]
    if kind in ("seq", "seq_turned"):
        order = ("y", "p", "h") if kind == "seq" else ("p", "y", "h")
        return ("h", "p", "y"), [((slice(None), slice(None)), tail, order)]
    names = ("h", "p", "y", "x")
    if columns % 256:
        return names, [((slice(None), slice(None)), tail, ("x", "y", "p", "h"))]
    count = 4 if columns % 512 == 0 else 2
    step = columns // count
    orders = (("x", "y", "p", "h"), ("y", "x", "p", "h")) if kind == "all" else (("x", "y", "p", "h"),) * 2
    return names, [
        ((slice(None), pl.ds(i * step, step)), (rows, step), orders[i % 2]) for i in range(count)
    ]


def reduce_shapes(kind, far, fsdp, tail, dtype):
    length = {"h": far, "p": 2, "y": 2, "x": fsdp}
    names, parts = reduce_plan(kind, far, fsdp, tail)
    shapes = []
    for _, small, order in parts:
        left = list(names)
        full = tuple(length[n] for n in left) + small
        shapes += [full, full]
        for axis in order:
            left.remove(axis)
            lead = tuple(length[n] for n in left) + small
            shapes.append((far - 1,) + lead if axis == "h" else lead)
    return shapes


def reduce_steps(kind, far, fsdp, copies, source, out, scratch, local_sem):
    place = {name: lax.axis_index(name) for name in ("h", "p", "y", "x")}
    ic = lax.axis_index("c")
    length = {"h": far, "p": 2, "y": 2, "x": fsdp}
    core_dim = 2 if kind == "group" else 3
    names, parts = reduce_plan(kind, far, fsdp, out.shape)
    jobs, position = [], 0
    for cut, small, order in parts:
        count = 2 + len(order)
        jobs.append((cut, small, order, scratch[position : position + count]))
        position += count

    def view(c, cut):
        lead = [slice(None)] * core_dim + [c] + [slice(None)] * (len(names) - core_dim)
        return source.at[tuple(lead) + cut]

    def add(sums, brought, fixed, left, target=None, also=()):
        sizes = [1 if n in also else length[n] for n in left]
        total = 1
        for size in sizes:
            total *= size

        def one(number, _):
            index, rest = {}, number
            for n, size in reversed(list(zip(left, sizes))):
                index[n] = also[n] if n in also else rest % size
                rest = rest // size
            whole = tuple(fixed[n] if n in fixed else index[n] for n in names)
            value = sums[whole].astype(F32) + brought[tuple(index[n] for n in left)].astype(F32)
            if target is None:
                sums[whole] = value.astype(sums.dtype)
            else:
                target(value)
            return 0

        if total == 1:
            one(0, 0)
        else:
            lax.fori_loop(0, total, one, 0)

    loads, sent = [], []
    for i, (cut, small, order, refs) in enumerate(jobs):
        loads.append(pltpu.make_async_copy(view(ic, cut), refs[0], local_sem.at[i]))
        loads[i].start()
        sent.append(copies.start(view(1 - ic, cut), refs[1], flip("c")))
    yield
    for stage in range(len(jobs[0][2]) + 1):
        for i, (cut, small, order, refs) in enumerate(jobs):
            sums, brought = refs[0], refs[1 + stage]
            done = order[:stage]
            left = tuple(n for n in names if n not in done)
            fixed = {n: place[n] for n in done}
            if stage == 0:
                loads[i].wait()
            if stage > 0 and order[stage - 1] == "h":
                for copy in sent[i]:
                    copy.wait_recv()
            else:
                sent[i].wait_recv()
            if stage == len(order):
                if order[-1] == "h":
                    whole = tuple(place[n] for n in names)
                    value = sums[whole].astype(F32)
                    for k in range(far - 1):
                        value = value + brought[k].astype(F32)
                    out[cut] = value
                else:

                    def put(value, cut=cut):
                        out[cut] = value

                    add(sums, brought, fixed, left, put)
                continue
            axis = order[stage]
            if axis == "h":
                add(sums, brought, fixed, left)
                sent[i] = []
                for k in range(1, far):
                    goal = lax.rem(place["h"] + k, far)
                    whole = tuple(goal if n == "h" else place[n] for n in names)
                    sent[i].append(
                        copies.start(sums.at[whole], refs[2 + stage].at[k - 1], other_h(far, k))
                    )
            else:
                add(sums, brought, fixed, left, also={axis: 1 - place[axis]})
                index = tuple(
                    1 - place[n] if n == axis else fixed.get(n, slice(None)) for n in names
                )
                sent[i] = copies.start(sums.at[index], refs[2 + stage], flip(axis))
                add(sums, brought, fixed, left, also={axis: place[axis]})
        yield


def reduce_kernel(kinds, far, fsdp, counts, *refs):
    n = len(kinds)
    sources, outs = refs[:n], refs[n : 2 * n]
    scratch = refs[2 * n : -3]
    send_sems, recv_sems, local_sems = refs[-3:]
    partners = [flip("p"), flip("y"), flip("c")]
    if set(kinds) - {"group", "spread"}:
        partners += [other_h(far, k) for k in range(1, far)]
    if "all" in kinds or "all_x" in kinds:
        partners.append(flip("x"))
    if "spread" in kinds:
        partners += corners()
    greet(partners)
    copies = Copies(send_sems, recv_sems)
    running, position = [], 0
    for i, kind in enumerate(kinds):
        if kind == "spread":
            me = (lax.axis_index("p") * 2 + lax.axis_index("y")) * 2 + lax.axis_index("c")
            local = pltpu.make_async_copy(
                sources[i].at[me], outs[i].at[me], local_sems.at[i, 0]
            )
            running.append(spread_steps(far, copies, sources[i], outs[i], local, 1))
            continue
        part = scratch[position : position + counts[i]]
        position += counts[i]
        running.append(
            reduce_steps(
                kind, far, fsdp, copies, sources[i], outs[i], part, local_sems.at[i]
            )
        )
    while running:
        running = [job for job in running if next(job, "end") != "end"]
    for copy in copies.started:
        copy.wait_send()


def reduce(name, number, far, fsdp, kinds, arrays):
    shapes, scratch, counts, total = [], [], [], 0
    for kind, array in zip(kinds, arrays):
        if kind == "spread":
            shapes.append(jax.ShapeDtypeStruct(array.shape, array.dtype))
            counts.append(0)
            total += 7
            continue
        tail = array.shape[-2:]
        parts = reduce_plan(kind, far, fsdp, tail)[1]
        own = reduce_shapes(kind, far, fsdp, tail, array.dtype)
        counts.append(len(own))
        scratch += [pltpu.VMEM(shape, array.dtype) for shape in own]
        shapes.append(jax.ShapeDtypeStruct(tail, F32))
        total += sum(1 + len(order) + (far - 2 if "h" in order else 0) for _, _, order in parts)
    return pl.pallas_call(
        functools.partial(reduce_kernel, kinds, far, fsdp, tuple(counts)),
        out_shape=tuple(shapes),
        in_specs=[ANY] * len(arrays),
        out_specs=tuple(
            ANY if kind == "spread" else pl.BlockSpec(memory_space=pltpu.VMEM) for kind in kinds
        ),
        scratch_shapes=scratch
        + [
            pltpu.SemaphoreType.DMA((total,)),
            pltpu.SemaphoreType.DMA((total,)),
            pltpu.SemaphoreType.DMA((len(arrays), 4)),
        ],
        compiler_params=pltpu.CompilerParams(collective_id=number, has_side_effects=True),
        cost_estimate=pl.CostEstimate(flops=0, bytes_accessed=COST, transcendentals=0),
        name=name,
    )(*arrays)


def body(
    sizes,
    inputs,
    lengths,
    attn_gain,
    query_weight,
    query_bias,
    key_matrix,
    key_bias_vector,
    value_matrix,
    value_bias_vector,
    output_weight,
    mlp_gain,
    gate_weight,
    up_weight,
    down_weight,
    cotangent,
):
    far, fsdp = sizes
    micro, token_rows, width = inputs.shape[1:]
    shard = query_weight.shape[0]
    kv_width = key_matrix.shape[1]
    hidden_width = gate_weight.shape[1]
    devices = far * 8 * fsdp
    seq = far * 8
    ih, ip, iy, ic, ix = (lax.axis_index(name) for name in ("h", "p", "y", "c", "x"))
    me8 = (ip * 2 + iy) * 2 + ic
    me_seq = ih * 8 + me8

    def hop(array, axis, shift=1):
        if axis == "h":
            return lax.ppermute(array, "h", [(i, (i + shift) % far) for i in range(far)])
        return lax.ppermute(array, axis, SWAP)

    def pick(array, index, axis):
        return lax.dynamic_index_in_dim(array, index, axis, keepdims=False)

    slice_width = hidden_width // 8

    gate_cut, up_cut = cut_columns(far, False, (gate_weight, up_weight))

    vectors = jnp.concatenate(
        [attn_gain, query_bias, key_bias_vector, value_bias_vector, mlp_gain]
    ).astype(F32)
    vectors = jnp.pad(vectors, (0, 1024 - vectors.shape[0])).reshape(8, 128)
    w_qkv, vectors, gate_parts, up_parts, w_down = move(
        "gather_first",
        0,
        far,
        fsdp,
        ("all_y", "all", "spread", "spread", "pair"),
        (
            jnp.concatenate([query_weight, key_matrix, value_matrix], axis=1),
            vectors,
            gate_cut,
            up_cut,
            down_weight,
        ),
    )
    w_down = w_down.reshape(slice_width, width)
    w_qkv = w_qkv.reshape(width, -1)
    vectors = vectors.reshape(devices, 1024)
    cuts = [0]
    for part in (attn_gain, query_bias, key_bias_vector, value_bias_vector, mlp_gain):
        cuts.append(cuts[-1] + part.shape[0])
    gain_attn, b_query, b_key, b_value, gain_mlp = (
        vectors[:, cuts[i] : cuts[i + 1]].reshape(-1) for i in range(5)
    )
    rows = inputs[0].astype(F32).reshape(micro * token_rows, width)
    upstream_low = cotangent[0].reshape(micro * token_rows, width)
    positions_at = me_seq * token_rows + jnp.arange(token_rows, dtype=jnp.int32)
    tables, spans, metas = [], [], []
    for number in range(micro):
        offsets, first = locate(lengths[0, number], positions_at)
        tables.append(rotary_tables(offsets, HEAD_WIDTH))
        spans.append(
            jnp.concatenate(
                [
                    jnp.tile(first, GROUP)[None],
                    jnp.tile(positions_at, GROUP)[None],
                    jnp.zeros((6, GROUP * token_rows), jnp.int32),
                ],
                axis=0,
            )
        )
        low = jnp.maximum(first[0] // token_rows, me_seq - seq // 2)
        metas.append(jnp.stack([low, me_seq]).astype(jnp.int32))
    cosine_table = jnp.concatenate([t[0] for t in tables], axis=0)
    sine_table = jnp.concatenate([t[1] for t in tables], axis=0)

    normed, recip_one = rms_forward(rows, gain_attn)
    normed_low = normed.astype(BF16)
    pre = mat_dot(normed_low, w_qkv)
    heads = range(QUERY_HEADS + KEY_VALUE_HEADS)
    splits = ((0, micro * token_rows, 0, width),) + tuple(
        (m * token_rows, token_rows, width, 2 * kv_width) for m in range(micro)
    )
    biases = jnp.concatenate([b_query, b_key, b_value])[None]
    query_rotated, *own_kv = rotate(pre, biases, cosine_table, sine_table, heads, splits, 1.0)
    moved = move(
        "gather_second",
        1,
        far,
        fsdp,
        ("seq",) * micro + ("all_y", "pair8", "pair8", "group"),
        tuple(own_kv) + (output_weight, gate_parts, up_parts, upstream_low),
    )
    stacks = [part.reshape(seq, token_rows, 2 * kv_width) for part in moved[:micro]]
    w_output = moved[micro].reshape(width, width)
    w_gate, w_up = (part.reshape(width, slice_width) for part in moved[micro + 1 : micro + 3])
    upstream_all = moved[micro + 3].reshape(-1, width)
    attended, lses = [], []
    for m in range(micro):
        result, lse = attend_forward(m, metas[m], query_rotated, stacks[m], spans[m])
        attended.append(result)
        lses.append(lse)
    attended = jnp.concatenate(attended, axis=0)
    middle = rows + mat_dot(attended, w_output)
    normed_two, recip_two = rms_forward(middle, gain_mlp)
    (tokens,) = move("gather_tokens", 2, far, fsdp, ("group",), (normed_two.astype(BF16),))
    tokens = tokens.reshape(-1, width)

    tokens_turned, hidden, hidden_turned, grad_gate, grad_up = hidden_units(
        micro * token_rows, tokens, upstream_all, w_gate, w_up, w_down
    )
    group = (2, 2, 2, micro * token_rows, width)

    def over_x(grad, axis, other):
        grad = grad.astype(BF16)
        sent, other = lax.optimization_barrier((pick(grad, 1 - ix, axis), other))
        kept = pick(grad, ix, axis).astype(F32) + hop(sent, "x").astype(F32)
        return kept.astype(BF16), other

    def over_h(kept):
        total = pick(kept, ih, 0).astype(F32)
        for k in range(1, far):
            total = total + hop(pick(kept, (ih + k) % far, 0), "h", k).astype(F32)
        return total

    eight = (far, 8, fsdp, shard, slice_width)
    turned = tokens_turned.reshape(far, 8, fsdp, shard, -1)
    gate_sum, grad_up_last = over_x(dot(turned, grad_gate, ((4,), (0,))), 2, grad_up)
    up_sum, _ = over_x(dot(turned, grad_up_last, ((4,), (0,))), 2, ())
    grad_two = (cols_dot(grad_gate, w_gate) + cols_dot(grad_up, w_up)).astype(BF16)

    (grad_two,) = reduce("reduce_tokens", 3, far, fsdp, ("group",), (grad_two.reshape(group),))
    grad_norm, gain_mlp_sum = rms_backward(middle, recip_two, gain_mlp, grad_two)
    grad_middle = upstream_low.astype(F32) + grad_norm
    grad_branch = grad_middle.astype(BF16)
    grad_branch, gate_sum, up_sum = lax.optimization_barrier((grad_branch, gate_sum, up_sum))
    gate_sum = over_h(gate_sum).astype(BF16)
    grad_attended = cols_dot(grad_branch, w_output).astype(BF16)
    grad_kvs, grad_query = [], []
    for m in range(micro):
        query_part, grad_kv = attend_backward(
            m,
            metas[m],
            query_rotated,
            grad_attended,
            stacks[m],
            spans[m],
            lses[m],
            cosine_table,
            sine_table,
        )
        grad_kvs.append(grad_kv.reshape(far, 2, 2, 2, token_rows, 2 * kv_width))
        grad_query.append(query_part)

    blocks = (far, 2, 2, 2, fsdp, shard)
    grad_kvs, gate_sum, hidden, hidden_turned = lax.optimization_barrier(
        (grad_kvs, gate_sum, hidden, hidden_turned)
    )
    down_part, _ = over_x(
        mat_dot(hidden_turned, upstream_all).reshape(far, fsdp, -1, width), 1, ()
    )
    final = mat_dot(hidden, w_down).astype(BF16)
    g_output = rows_dot(attended, grad_branch).astype(BF16)
    reduced = reduce(
        "reduce_second",
        4,
        far,
        fsdp,
        ("group", "all_x") + tuple("seq_turned" if m % 2 else "seq" for m in range(micro)),
        (final.reshape(group), g_output.reshape(blocks + (width,))) + tuple(grad_kvs),
    )
    grad_kvs, output_part = list(reduced[2:]), reduced[1]
    grad_kvs[0], up_sum = lax.optimization_barrier((grad_kvs[0], up_sum))
    up_sum = over_h(up_sum).astype(BF16)
    results = (middle + reduced[0]).astype(BF16)
    grad_query = jnp.concatenate(grad_query, axis=0)
    grad_kv = jnp.concatenate(grad_kvs, axis=0)
    (grad_kv,) = rotate(
        grad_kv,
        jnp.zeros((1, 2 * kv_width), F32),
        cosine_table,
        sine_table,
        range(KEY_VALUE_HEADS),
        ((0, micro * token_rows, 0, 2 * kv_width),),
        -1.0,
    )
    grad_pre = jnp.concatenate([grad_query, grad_kv], axis=1)
    grad_normed = cols_dot(grad_pre, w_qkv)
    grad_rows, gain_attn_sum = rms_backward(rows, recip_one, gain_attn, grad_normed)
    input_grad = grad_middle + grad_rows
    g_qkv = rows_dot(normed_low, grad_pre).astype(BF16)
    g_qkv, up_sum, down_part = lax.optimization_barrier((g_qkv, up_sum, down_part))
    down_part = over_h(down_part)
    bias_sum = jnp.sum(grad_pre.astype(F32), axis=0)
    vector_sums = jnp.concatenate(
        [
            v.reshape(devices, -1)
            for v in (
                gain_attn_sum,
                bias_sum[:width],
                bias_sum[width : width + kv_width],
                bias_sum[width + kv_width :],
                gain_mlp_sum,
            )
        ],
        axis=1,
    )
    vector_sums = jnp.pad(vector_sums, ((0, 0), (0, 1024 - vector_sums.shape[1])))
    qkv_part, vector_part, gate_sum, up_sum = reduce(
        "reduce_last",
        5,
        far,
        fsdp,
        ("all", "all", "spread", "spread"),
        (
            g_qkv.reshape(blocks + (-1,)),
            vector_sums.reshape(far, 2, 2, 2, fsdp, 8, 128),
            gate_sum,
            up_sum,
        ),
    )
    vector_part = vector_part.reshape(-1)

    gate_grad, up_grad = cut_columns(far, True, (gate_sum, up_sum))

    return (
        results.reshape(1, micro, token_rows, width),
        input_grad.reshape(1, micro, token_rows, width),
        vector_part[cuts[0] : cuts[1]],
        qkv_part[:, :width],
        vector_part[cuts[1] : cuts[2]],
        qkv_part[:, width : width + kv_width],
        vector_part[cuts[2] : cuts[3]],
        qkv_part[:, width + kv_width :],
        vector_part[cuts[3] : cuts[4]],
        output_part,
        vector_part[cuts[4] : cuts[5]],
        gate_grad,
        up_grad,
        down_part,
    )


def solution(mesh):
    fsdp = mesh.shape["fsdp"]
    far = mesh.shape["seq"] // 8
    inner = Mesh(mesh.devices.reshape(far, 2, 2, 2, fsdp), ("h", "p", "y", "c", "x"))
    seq = ("h", "p", "y", "c")
    every = seq + ("x",)
    tokens = P("x", None, seq, None)
    matrix, vector = P(every, None), P(every)
    in_specs = (
        tokens,
        P("x", None, None),
        vector,
        matrix,
        vector,
        matrix,
        vector,
        matrix,
        vector,
        matrix,
        vector,
        matrix,
        matrix,
        matrix,
        tokens,
    )
    out_specs = (
        tokens,
        tokens,
        vector,
        matrix,
        vector,
        matrix,
        vector,
        matrix,
        vector,
        matrix,
        vector,
        matrix,
        matrix,
        matrix,
    )
    return jax.shard_map(
        functools.partial(body, (far, fsdp)),
        mesh=inner,
        in_specs=in_specs,
        out_specs=out_specs,
        check_vma=False,
    )
```

```python
import functools

import jax
import jax.numpy as jnp
from jax import lax
from jax.experimental import pallas as pl
from jax.experimental.pallas import tpu as pltpu
from jax.sharding import Mesh, PartitionSpec as P

QUERY_HEADS = 12
KEY_VALUE_HEADS = 2
HEAD_WIDTH = 128
EPSILON = 1e-06
THETA = 10000.0
GROUP = QUERY_HEADS // KEY_VALUE_HEADS
SCALE = HEAD_WIDTH ** (-0.5)
F32 = jnp.float32
BF16 = jnp.bfloat16
SWAP = [(0, 1), (1, 0)]


def locate(item_lengths, positions_at):
    ends = jnp.cumsum(item_lengths)
    starts = ends - item_lengths
    segment_ids = jnp.sum((ends[None, :] <= positions_at[:, None]).astype(jnp.int32), axis=1)
    onehot = segment_ids[:, None] == jnp.arange(item_lengths.shape[0], dtype=jnp.int32)[None, :]
    first = jnp.sum(jnp.where(onehot, starts[None, :], 0), axis=1)
    return (positions_at - first, first)


def rotary_tables(offsets, head_size):
    freqs = 1.0 / THETA ** (jnp.arange(0, head_size, 2, dtype=F32) / head_size)
    angles = offsets.astype(F32)[:, None] * freqs[None, :]
    cosine, sine = jnp.cos(angles), jnp.sin(angles)
    return (jnp.concatenate([cosine, cosine], axis=1), jnp.concatenate([-sine, sine], axis=1))


def rms_forward(rows, gain):
    recip = lax.rsqrt(jnp.mean(rows * rows, axis=-1, keepdims=True) + EPSILON)
    return (rows * recip * gain, recip)


def rms_backward(rows, recip, gain, upstream):
    weighted = upstream * gain
    grad_rows = recip * weighted - rows * (recip * recip * recip) * jnp.mean(
        rows * weighted, axis=-1, keepdims=True
    )
    gain_grad = jnp.sum(upstream * rows * recip, axis=0)
    return (grad_rows, gain_grad)


def dot(left, right, dims, out=F32):
    return lax.dot_general(left, right, ((dims[0], dims[1]), ((), ())), preferred_element_type=out)


def rows_dot(left, right):
    return dot(left, right, ((0,), (0,)))


def cols_dot(left, right):
    return dot(left, right, ((1,), (1,)))


def mat_dot(left, right):
    return dot(left, right, ((1,), (0,)))


def attend_forward_kernel(meta, q_ref, k_ref, v_ref, span_ref, o_ref, lse_ref):
    rows = q_ref.shape[0]
    queries = jnp.concatenate(
        [q_ref[:, h * HEAD_WIDTH : (h + 1) * HEAD_WIDTH] for h in range(GROUP)], axis=0
    )
    first, last = span_ref[0:1, :], span_ref[1:2, :]
    wide = GROUP * rows
    local = lax.broadcasted_iota(jnp.int32, (rows, 1), 0)

    def step(block, carry):
        top, total, accum = carry
        keys, values = k_ref[block], v_ref[block]
        scores = dot(keys, queries, ((1,), (1,))) * SCALE
        index = block * rows + local
        scores = jnp.where((index >= first) & (index <= last), scores, -1e30)
        new_top = jnp.maximum(top, jnp.max(scores, axis=0, keepdims=True))
        fade = jnp.exp(top - new_top)
        probs = jnp.exp(scores - new_top)
        total = total * fade + jnp.sum(probs, axis=0, keepdims=True)
        accum = accum * fade + dot(values, probs.astype(BF16), ((0,), (0,)))
        return (new_top, total, accum)

    top, total, accum = lax.fori_loop(
        meta[0],
        meta[1] + 1,
        step,
        (
            jnp.full((1, wide), -1e30, F32),
            jnp.zeros((1, wide), F32),
            jnp.zeros((HEAD_WIDTH, wide), F32),
        ),
    )
    attended = (accum / total).T.astype(BF16)
    for h in range(GROUP):
        o_ref[:, h * HEAD_WIDTH : (h + 1) * HEAD_WIDTH] = attended[h * rows : (h + 1) * rows]
    lse_ref[0] = top + jnp.log(total)


def attend_forward(number, meta, queries, stack, span):
    pieces, rows, _ = stack.shape
    width = queries.shape[1]
    part = width // KEY_VALUE_HEADS
    spec = pltpu.PrefetchScalarGridSpec(
        num_scalar_prefetch=1,
        grid=(KEY_VALUE_HEADS,),
        in_specs=[
            pl.BlockSpec((rows, part), lambda g, m: (number, g)),
            pl.BlockSpec((pieces, rows, HEAD_WIDTH), lambda g, m: (0, 0, g)),
            pl.BlockSpec((pieces, rows, HEAD_WIDTH), lambda g, m: (0, 0, KEY_VALUE_HEADS + g)),
            pl.BlockSpec((8, GROUP * rows), lambda g, m: (0, 0)),
        ],
        out_specs=[
            pl.BlockSpec((rows, part), lambda g, m: (0, g)),
            pl.BlockSpec((1, 1, GROUP * rows), lambda g, m: (g, 0, 0)),
        ],
    )
    return pl.pallas_call(
        attend_forward_kernel,
        grid_spec=spec,
        out_shape=(
            jax.ShapeDtypeStruct((rows, width), BF16),
            jax.ShapeDtypeStruct((KEY_VALUE_HEADS, 1, GROUP * rows), F32),
        ),
        cost_estimate=pl.CostEstimate(
            flops=4 * rows * rows * 6 * width, bytes_accessed=stack.size * 2, transcendentals=0
        ),
        name="attend_forward",
    )(meta, queries, stack, stack, span)


def attend_backward_kernel(
    meta, q_ref, do_ref, kv_ref, span_ref, lse_ref, cos_ref, sin_ref, dq_ref, dkv_ref, p_ref, dp_ref
):
    rows = q_ref.shape[0]
    wide = GROUP * rows
    first, last = span_ref[0:1, :], span_ref[1:2, :]
    local = lax.broadcasted_iota(jnp.int32, (rows, 1), 0)
    low = meta[0]
    cosine, sine = cos_ref[...], sin_ref[...]
    dkv_ref[...] = jnp.zeros_like(dkv_ref)
    for group in range(KEY_VALUE_HEADS):
        heads = range(group * GROUP, (group + 1) * GROUP)
        cols = [slice(h * HEAD_WIDTH, (h + 1) * HEAD_WIDTH) for h in heads]
        key_cols = slice(group * HEAD_WIDTH, (group + 1) * HEAD_WIDTH)
        start = (KEY_VALUE_HEADS + group) * HEAD_WIDTH
        value_cols = slice(start, start + HEAD_WIDTH)
        queries = jnp.concatenate([q_ref[:, c] for c in cols], axis=0)
        grads = jnp.concatenate([do_ref[:, c] for c in cols], axis=0)
        lse = lse_ref[group]

        def collect(block, delta):
            scores = dot(kv_ref[block, :, key_cols], queries, ((1,), (1,))) * SCALE
            index = block * rows + local
            probs = jnp.where((index >= first) & (index <= last), jnp.exp(scores - lse), 0.0)
            grad_probs = dot(kv_ref[block, :, value_cols], grads, ((1,), (1,)))
            p_ref[block - low] = probs
            dp_ref[block - low] = grad_probs
            return delta + jnp.sum(probs * grad_probs, axis=0, keepdims=True)

        delta = lax.fori_loop(low, meta[1] + 1, collect, jnp.zeros((1, wide), F32))

        def spread(block, accum):
            probs = p_ref[block - low]
            grad_scores = (probs * (dp_ref[block - low] - delta)).astype(BF16)
            dkv_ref[block, :, key_cols] = (mat_dot(grad_scores, queries) * SCALE).astype(BF16)
            dkv_ref[block, :, value_cols] = mat_dot(probs.astype(BF16), grads).astype(BF16)
            return accum + dot(kv_ref[block, :, key_cols], grad_scores, ((0,), (0,)))

        accum = lax.fori_loop(low, meta[1] + 1, spread, jnp.zeros((HEAD_WIDTH, wide), F32))
        grad_queries = (accum * SCALE).T
        for h in range(GROUP):
            part = grad_queries[h * rows : (h + 1) * rows]
            turned = pltpu.roll(part, HEAD_WIDTH // 2, 1)
            dq_ref[:, cols[h]] = (part * cosine - turned * sine).astype(BF16)


def attend_backward(number, meta, queries, grads, stack, span, lse, cosine, sine):
    pieces, rows, wide = stack.shape
    width = queries.shape[1]
    most = pieces // 2 + 1

    def own(columns):
        return pl.BlockSpec((rows, columns), lambda i, m: (number, 0))

    def whole(shape):
        return pl.BlockSpec(shape, lambda i, m: (0,) * len(shape))

    spec = pltpu.PrefetchScalarGridSpec(
        num_scalar_prefetch=1,
        grid=(1,),
        in_specs=[
            own(width),
            own(width),
            whole(stack.shape),
            whole(span.shape),
            whole(lse.shape),
            own(HEAD_WIDTH),
            own(HEAD_WIDTH),
        ],
        out_specs=[whole((rows, width)), whole(stack.shape)],
        scratch_shapes=[
            pltpu.VMEM((most, rows, GROUP * rows), F32),
            pltpu.VMEM((most, rows, GROUP * rows), F32),
        ],
    )
    return pl.pallas_call(
        attend_backward_kernel,
        grid_spec=spec,
        out_shape=(
            jax.ShapeDtypeStruct((rows, width), BF16),
            jax.ShapeDtypeStruct(stack.shape, BF16),
        ),
        cost_estimate=pl.CostEstimate(
            flops=0, bytes_accessed=COST, transcendentals=0
        ),
        name="attend_backward",
    )(meta, queries, grads, stack, span, lse, cosine, sine)


def hidden_kernel(
    token_ref,
    grad_ref,
    gate_ref,
    up_ref,
    down_ref,
    token_turned_ref,
    hidden_ref,
    turned_ref,
    dgate_ref,
    dup_ref,
):
    tokens = token_ref[...]
    token_turned_ref[...] = tokens.T
    gate_pre = mat_dot(tokens, gate_ref[...])
    up_pre = mat_dot(tokens, up_ref[...])
    grad_hidden = cols_dot(grad_ref[...], down_ref[...])
    sigma = jax.nn.sigmoid(gate_pre)
    activated = gate_pre * sigma
    hidden = activated * up_pre
    hidden_ref[...] = hidden.astype(BF16)
    turned_ref[...] = hidden.T.astype(BF16)
    dgate_ref[...] = (grad_hidden * up_pre * sigma * (1.0 + gate_pre * (1.0 - sigma))).astype(BF16)
    dup_ref[...] = (grad_hidden * activated).astype(BF16)


def hidden_units(rows, tokens, grads, w_gate, w_up, w_down):
    total, width = tokens.shape
    units = w_gate.shape[1]

    def tile(columns):
        return pl.BlockSpec((rows, columns), lambda i: (i, 0))

    def fixed(array):
        return pl.BlockSpec(array.shape, lambda i: (0, 0))

    return pl.pallas_call(
        hidden_kernel,
        grid=(total // rows,),
        in_specs=[tile(width), tile(width), fixed(w_gate), fixed(w_up), fixed(w_down)],
        out_specs=[
            pl.BlockSpec((width, rows), lambda i: (0, i)),
            tile(units),
            pl.BlockSpec((units, rows), lambda i: (0, i)),
            tile(units),
            tile(units),
        ],
        out_shape=(
            jax.ShapeDtypeStruct((width, total), BF16),
            jax.ShapeDtypeStruct((total, units), BF16),
            jax.ShapeDtypeStruct((units, total), BF16),
            jax.ShapeDtypeStruct((total, units), BF16),
            jax.ShapeDtypeStruct((total, units), BF16),
        ),
        cost_estimate=pl.CostEstimate(
            flops=6 * total * width * units, bytes_accessed=8 * total * width, transcendentals=0
        ),
        name="hidden_units",
    )(tokens, grads, w_gate, w_up, w_down)


def rotate_kernel(turned_heads, splits, sign, pre_ref, bias_ref, cos_ref, sin_ref, *outs):
    cosine, sine = cos_ref[...], sin_ref[...] * sign
    for head in range(pre_ref.shape[1] // HEAD_WIDTH):
        cols = slice(head * HEAD_WIDTH, (head + 1) * HEAD_WIDTH)
        part = pre_ref[:, cols] + bias_ref[:, cols]
        if head in turned_heads:
            part = part * cosine + pltpu.roll(part, HEAD_WIDTH // 2, 1) * sine
        part = part.astype(BF16)
        for (top, height, left, wide), out in zip(splits, outs):
            if left <= head * HEAD_WIDTH < left + wide:
                at = head * HEAD_WIDTH - left
                out[:, at : at + HEAD_WIDTH] = part[top : top + height]


def rotate(pre, bias, cosine, sine, turned_heads, splits, sign):
    return pl.pallas_call(
        functools.partial(rotate_kernel, tuple(turned_heads), splits, sign),
        out_shape=tuple(
            jax.ShapeDtypeStruct((height, wide), BF16) for _, height, _, wide in splits
        ),
        cost_estimate=pl.CostEstimate(flops=0, bytes_accessed=8 * pre.size, transcendentals=0),
        name="rotate",
    )(pre, bias, cosine, sine)


def cut_kernel(far, whole, *refs):
    count = len(refs) // 2
    for source, out in zip(refs[:count], refs[count:]):
        small = (out if whole else source).shape[1] // (8 * far)
        for h in range(far):
            for g in range(8):
                left, right = (h * 8 + g) * small, h * small
                if whole:
                    out[:, left : left + small] = source[g, :, right : right + small].astype(F32)
                else:
                    out[g, :, right : right + small] = source[:, left : left + small]


def cut_columns(far, whole, arrays):
    shapes = []
    for array in arrays:
        if whole:
            shapes.append(jax.ShapeDtypeStruct((array.shape[1], 8 * array.shape[2]), F32))
        else:
            shape = (8, array.shape[0], array.shape[1] // 8)
            shapes.append(jax.ShapeDtypeStruct(shape, array.dtype))
    return pl.pallas_call(
        functools.partial(cut_kernel, far, whole),
        out_shape=tuple(shapes),
        name="join_columns" if whole else "cut_columns",
    )(*arrays)


MESH = pl.DeviceIdType.MESH
PARTS, AHEAD = 4, 2
COST = 1024
ANY = pl.BlockSpec(memory_space=pl.ANY)


class Local:
    def __init__(self, source, buffer, target, sems):
        self.load = pltpu.make_async_copy(source, buffer, sems.at[0])
        self.store = pltpu.make_async_copy(buffer, target, sems.at[1])

    def start(self):
        self.load.start()

    def turn(self):
        self.load.wait()
        self.store.start()

    def wait(self):
        self.store.wait()


class Copies:
    def __init__(self, send_sems, recv_sems):
        self.send_sems, self.recv_sems, self.started = send_sems, recv_sems, []

    def start(self, source, target, device):
        number = len(self.started)
        copy = pltpu.make_async_remote_copy(
            src_ref=source,
            dst_ref=target,
            send_sem=self.send_sems.at[number],
            recv_sem=self.recv_sems.at[number],
            device_id=device,
            device_id_type=MESH,
        )
        copy.start()
        self.started.append(copy)
        return copy


def greet(devices):
    barrier = pltpu.get_barrier_semaphore()
    for device in devices:
        pl.semaphore_signal(barrier, inc=1, device_id=device, device_id_type=MESH)
    pl.semaphore_wait(barrier, len(devices))


def other_h(far, k):
    return {"h": lax.rem(lax.axis_index("h") + k, far)}


def flip(*axes):
    return {axis: 1 - lax.axis_index(axis) for axis in axes}


def corners():
    return [flip("p", "y"), flip("p", "c"), flip("y", "c"), flip("p", "y", "c")]


def gather_steps(kind, far, copies, source, out, local):
    ih, ip, iy, ic, ix = (lax.axis_index(name) for name in ("h", "p", "y", "c", "x"))
    every = kind in ("all", "all_y")

    def block(h, p, y=iy, x=ix):
        return out.at[h, p, y, ic, x] if every else out.at[h, p, y, ic]

    local.start()
    pieces = [(lax.rem(ih - k + far, far), p) for p in (ip, 1 - ip) for k in range(far)]
    count = len(pieces)
    arrivals, plane, cross, core = [None] * count, [None] * count, [None] * count, [None] * count
    columns = source.shape[-1]
    half = columns // 2 if columns % 256 == 0 and kind == "all" else columns

    def cut(ref, first):
        if half == columns:
            return ref
        return ref.at[:, pl.ds(0 if first else half, half)]

    for k in range(1, far):
        arrivals[k] = copies.start(source, block(ih, ip), other_h(far, k))
    for step in range(count + 3):
        if step < count:
            if arrivals[step] is not None:
                arrivals[step].wait_recv()
            h, p = pieces[step]
            held = source if step == 0 else block(h, p)
            if step < far:
                arrivals[far + step] = copies.start(held, block(h, p), flip("p"))
            plane[step] = [copies.start(held, block(h, p), flip("y"))]
            if every:
                plane[step].append(copies.start(held, block(h, p), flip("x")))
        if 0 <= step - 1 < count:
            h, p = pieces[step - 1]
            for copy in plane[step - 1]:
                copy.wait_recv()
            cross[step - 1] = []
            if every:
                ref = cut(block(h, p, x=1 - ix), True)
                cross[step - 1].append(copies.start(ref, ref, flip("y")))
                if half < columns:
                    ref = cut(block(h, p, y=1 - iy), False)
                    cross[step - 1].append(copies.start(ref, ref, flip("x")))
        if 0 <= step - 2 < count:
            h, p = pieces[step - 2]
            for copy in cross[step - 2]:
                copy.wait_recv()
            if step == 2:
                local.wait()
            ref = out.at[h, p, :, ic]
            core[step - 2] = copies.start(ref, ref, flip("c"))
        if 0 <= step - 3 < count:
            core[step - 3].wait_recv()
        yield


def group_steps(far, copies, source, out, local, delay):
    ip, iy, ic = (lax.axis_index(name) for name in ("p", "y", "c"))
    half = source.shape[0] // 2
    top, low = pl.ds(0, half), pl.ds(half, half)

    def rows(p, y, part):
        return out.at[p, y, ic, part]

    def forward(ref, axis):
        return copies.start(ref, ref, flip(axis))

    local.start()
    for _ in range(delay):
        yield
    first = [
        copies.start(source.at[top], rows(ip, iy, top), flip("y")),
        copies.start(source.at[low], rows(ip, iy, low), flip("p")),
    ]
    second = [
        copies.start(source.at[top], rows(ip, iy, top), flip("p")),
        copies.start(source.at[low], rows(ip, iy, low), flip("y")),
    ]
    core = [copies.start(source, out.at[ip, iy, ic], flip("c"))]
    yield
    first[0].wait_recv()
    second.append(forward(rows(ip, 1 - iy, top), "p"))
    core.append(forward(rows(ip, 1 - iy, top), "c"))
    first[1].wait_recv()
    second.append(forward(rows(1 - ip, iy, low), "y"))
    core.append(forward(rows(1 - ip, iy, low), "c"))
    yield
    for copy, p, y, part in (
        (second[0], 1 - ip, iy, top),
        (second[1], ip, 1 - iy, low),
        (second[2], 1 - ip, 1 - iy, top),
        (second[3], 1 - ip, 1 - iy, low),
    ):
        copy.wait_recv()
        core.append(forward(rows(p, y, part), "c"))
    yield
    for copy in core:
        copy.wait_recv()
    local.wait()


def pair_steps(far, copies, parts, place, local, delay):
    ih, ix = lax.axis_index("h"), lax.axis_index("x")
    local.start()
    for _ in range(delay):
        yield
    arrived, sent = [], []

    def send(i):
        if i < len(parts):
            target = place(ih, ix, i)
            arrived.append([copies.start(parts[i], target, other_h(far, k)) for k in range(1, far)])
            sent.append(copies.start(parts[i], target, flip("x")))

    for i in range(AHEAD):
        send(i)
    for i in range(len(parts)):
        yield
        send(i + AHEAD)
        for k in range(1, far):
            arrived[i][k - 1].wait_recv()
            ref = place(lax.rem(ih - k + far, far), ix, i)
            sent.append(copies.start(ref, ref, flip("x")))
    yield
    for copy in sent:
        copy.wait_recv()
    local.wait()


def spread_steps(far, copies, source, out, local, delay):
    ip, iy, ic = (lax.axis_index(name) for name in ("p", "y", "c"))
    me = (ip * 2 + iy) * 2 + ic
    local.start()
    for _ in range(delay):
        yield
    started = []
    for j in (1, 2, 4, 3, 5, 6, 7):
        p = 1 - ip if j & 4 else ip
        y = 1 - iy if j & 2 else iy
        c = 1 - ic if j & 1 else ic
        started.append(
            copies.start(source.at[(p * 2 + y) * 2 + c], out.at[me], {"p": p, "y": y, "c": c})
        )
    for _ in range(2 * far + 2):
        yield
    for copy in started:
        copy.wait_recv()
    local.wait()
    yield


def move_kernel(kinds, far, *refs):
    count = len(kinds)
    sources, outs = refs[:count], refs[count : 2 * count]
    buffers = refs[2 * count : 3 * count]
    send_sems, recv_sems, local_sems = refs[3 * count :]
    locals_ = []

    def local_copy(i, source, target):
        locals_.append(Local(source, buffers[i], target, local_sems.at[i]))
        return locals_[-1]

    ih, ip, iy, ic, ix = (lax.axis_index(name) for name in ("h", "p", "y", "c", "x"))
    partners = [flip("p"), flip("y"), flip("c")]
    if set(kinds) - {"spread", "group"}:
        partners += [other_h(far, k) for k in range(1, far)]
    if set(kinds) - {"seq", "group", "spread"}:
        partners.append(flip("x"))
    if "spread" in kinds:
        partners += corners()
    greet(partners)
    copies = Copies(send_sems, recv_sems)
    running = []
    for i, kind in enumerate(kinds):
        if kind == "spread":
            me = (ip * 2 + iy) * 2 + ic
            local = local_copy(i, sources[i].at[me], outs[i].at[me])
            running.append(spread_steps(far, copies, sources[i], outs[i], local, 0))
        elif kind == "group":
            place = outs[i].at[ip, iy, ic]
            local = local_copy(i, sources[i], place)
            delay = 3 if count > 1 else 0
            running.append(group_steps(far, copies, sources[i], outs[i], local, delay))
        elif kind in ("pair", "pair8"):
            local = outs[i].at[ih, :, ix] if kind == "pair8" else outs[i].at[ih, ix]
            local = local_copy(i, sources[i], local)
            step = (8 if kind == "pair8" else sources[i].shape[1]) // PARTS
            cuts = [pl.ds(part * step, step) for part in range(PARTS)]
            if kind == "pair8":
                parts = [sources[i].at[c] for c in cuts]
            else:
                parts = [sources[i].at[:, c] for c in cuts]

            def place(h, x, part, out=outs[i], cuts=cuts, wide=kind == "pair8"):
                return out.at[h, cuts[part], x] if wide else out.at[h, x, :, cuts[part]]

            wait = (PARTS - AHEAD + 1) * kinds[:i].count("pair8")
            running.append(pair_steps(far, copies, parts, place, local, wait))
        else:
            place = (ih, ip, iy, ic) if kind == "seq" else (ih, ip, iy, ic, ix)
            local = local_copy(i, sources[i], outs[i].at[place])
            running.append(gather_steps(kind, far, copies, sources[i], outs[i], local))
    running = [job for job in running if next(job, "end") != "end"]
    for local in locals_:
        local.turn()
    while running:
        running = [job for job in running if next(job, "end") != "end"]
    for copy in copies.started:
        copy.wait_send()


def move(name, number, far, fsdp, kinds, arrays):
    shapes, total = [], 0
    pieces = 2 * far
    for kind, array in zip(kinds, arrays):
        if kind in ("all", "all_y"):
            lead, total = (far, 2, 2, 2, fsdp), total + (far - 1) + far + 5 * pieces
        elif kind == "seq":
            lead, total = (far, 2, 2, 2), total + (far - 1) + far + 2 * pieces
        elif kind == "group":
            lead, total = (2, 2, 2), total + 13
        elif kind == "pair":
            lead, total = (far, fsdp), total + PARTS * (2 * far - 1)
        elif kind == "pair8":
            lead, total = (far, 8, fsdp), total + PARTS * (2 * far - 1)
        else:
            lead, total = (), total + 7
        tail = array.shape[1:] if kind == "pair8" else array.shape
        shapes.append(jax.ShapeDtypeStruct(lead + tail, array.dtype))
    return pl.pallas_call(
        functools.partial(move_kernel, kinds, far),
        out_shape=tuple(shapes),
        in_specs=[ANY] * len(arrays),
        out_specs=tuple([ANY] * len(arrays)),
        scratch_shapes=[
            pltpu.VMEM(a.shape[1:] if kind == "spread" else a.shape, a.dtype)
            for kind, a in zip(kinds, arrays)
        ]
        + [
            pltpu.SemaphoreType.DMA((total,)),
            pltpu.SemaphoreType.DMA((total,)),
            pltpu.SemaphoreType.DMA((len(arrays), 2)),
        ],
        compiler_params=pltpu.CompilerParams(collective_id=number, has_side_effects=True),
        cost_estimate=pl.CostEstimate(flops=0, bytes_accessed=COST, transcendentals=0),
        name=name,
    )(*arrays)


def reduce_plan(kind, far, fsdp, tail):
    rows, columns = tail
    if kind == "group":
        step = rows // 4
        return ("p", "y"), [
            ((pl.ds(i * step, step), slice(None)), (step, columns), ("yp", "py")[i % 2])
            for i in range(4)
        ]
    if kind in ("seq", "seq_turned"):
        order = ("y", "p", "h") if kind == "seq" else ("p", "y", "h")
        return ("h", "p", "y"), [((slice(None), slice(None)), tail, order)]
    names = ("h", "p", "y", "x")
    if columns % 256:
        return names, [((slice(None), slice(None)), tail, ("x", "y", "p", "h"))]
    count = 4 if columns % 512 == 0 else 2
    step = columns // count
    orders = (("x", "y", "p", "h"), ("y", "x", "p", "h")) if kind == "all" else (("x", "y", "p", "h"),) * 2
    return names, [
        ((slice(None), pl.ds(i * step, step)), (rows, step), orders[i % 2]) for i in range(count)
    ]


def reduce_shapes(kind, far, fsdp, tail, dtype):
    length = {"h": far, "p": 2, "y": 2, "x": fsdp}
    names, parts = reduce_plan(kind, far, fsdp, tail)
    shapes = []
    for _, small, order in parts:
        left = list(names)
        full = tuple(length[n] for n in left) + small
        shapes += [full, full]
        for axis in order:
            left.remove(axis)
            lead = tuple(length[n] for n in left) + small
            shapes.append((far - 1,) + lead if axis == "h" else lead)
    return shapes


def reduce_steps(kind, far, fsdp, copies, source, out, scratch, local_sem):
    place = {name: lax.axis_index(name) for name in ("h", "p", "y", "x")}
    ic = lax.axis_index("c")
    length = {"h": far, "p": 2, "y": 2, "x": fsdp}
    core_dim = 2 if kind == "group" else 3
    names, parts = reduce_plan(kind, far, fsdp, out.shape)
    jobs, position = [], 0
    for cut, small, order in parts:
        count = 2 + len(order)
        jobs.append((cut, small, order, scratch[position : position + count]))
        position += count

    def view(c, cut):
        lead = [slice(None)] * core_dim + [c] + [slice(None)] * (len(names) - core_dim)
        return source.at[tuple(lead) + cut]

    def add(sums, brought, fixed, left, target=None, also=()):
        sizes = [1 if n in also else length[n] for n in left]
        total = 1
        for size in sizes:
            total *= size

        def one(number, _):
            index, rest = {}, number
            for n, size in reversed(list(zip(left, sizes))):
                index[n] = also[n] if n in also else rest % size
                rest = rest // size
            whole = tuple(fixed[n] if n in fixed else index[n] for n in names)
            value = sums[whole].astype(F32) + brought[tuple(index[n] for n in left)].astype(F32)
            if target is None:
                sums[whole] = value.astype(sums.dtype)
            else:
                target(value)
            return 0

        if total == 1:
            one(0, 0)
        else:
            lax.fori_loop(0, total, one, 0)

    loads, sent = [], []
    for i, (cut, small, order, refs) in enumerate(jobs):
        loads.append(pltpu.make_async_copy(view(ic, cut), refs[0], local_sem.at[i]))
        loads[i].start()
        sent.append(copies.start(view(1 - ic, cut), refs[1], flip("c")))
    yield
    for stage in range(len(jobs[0][2]) + 1):
        for i, (cut, small, order, refs) in enumerate(jobs):
            sums, brought = refs[0], refs[1 + stage]
            done = order[:stage]
            left = tuple(n for n in names if n not in done)
            fixed = {n: place[n] for n in done}
            if stage == 0:
                loads[i].wait()
            if stage > 0 and order[stage - 1] == "h":
                for copy in sent[i]:
                    copy.wait_recv()
            else:
                sent[i].wait_recv()
            if stage == len(order):
                if order[-1] == "h":
                    whole = tuple(place[n] for n in names)
                    value = sums[whole].astype(F32)
                    for k in range(far - 1):
                        value = value + brought[k].astype(F32)
                    out[cut] = value
                else:

                    def put(value, cut=cut):
                        out[cut] = value

                    add(sums, brought, fixed, left, put)
                continue
            axis = order[stage]
            if axis == "h":
                add(sums, brought, fixed, left)
                sent[i] = []
                for k in range(1, far):
                    goal = lax.rem(place["h"] + k, far)
                    whole = tuple(goal if n == "h" else place[n] for n in names)
                    sent[i].append(
                        copies.start(sums.at[whole], refs[2 + stage].at[k - 1], other_h(far, k))
                    )
            else:
                add(sums, brought, fixed, left, also={axis: 1 - place[axis]})
                index = tuple(
                    1 - place[n] if n == axis else fixed.get(n, slice(None)) for n in names
                )
                sent[i] = copies.start(sums.at[index], refs[2 + stage], flip(axis))
                add(sums, brought, fixed, left, also={axis: place[axis]})
        yield


def reduce_kernel(kinds, far, fsdp, counts, *refs):
    n = len(kinds)
    sources, outs = refs[:n], refs[n : 2 * n]
    scratch = refs[2 * n : -3]
    send_sems, recv_sems, local_sems = refs[-3:]
    partners = [flip("p"), flip("y"), flip("c")]
    if set(kinds) - {"group", "spread"}:
        partners += [other_h(far, k) for k in range(1, far)]
    if "all" in kinds or "all_x" in kinds:
        partners.append(flip("x"))
    if "spread" in kinds:
        partners += corners()
    greet(partners)
    copies = Copies(send_sems, recv_sems)
    running, position = [], 0
    for i, kind in enumerate(kinds):
        if kind == "spread":
            me = (lax.axis_index("p") * 2 + lax.axis_index("y")) * 2 + lax.axis_index("c")
            local = pltpu.make_async_copy(
                sources[i].at[me], outs[i].at[me], local_sems.at[i, 0]
            )
            running.append(spread_steps(far, copies, sources[i], outs[i], local, 1))
            continue
        part = scratch[position : position + counts[i]]
        position += counts[i]
        running.append(
            reduce_steps(
                kind, far, fsdp, copies, sources[i], outs[i], part, local_sems.at[i]
            )
        )
    while running:
        running = [job for job in running if next(job, "end") != "end"]
    for copy in copies.started:
        copy.wait_send()


def reduce(name, number, far, fsdp, kinds, arrays):
    shapes, scratch, counts, total = [], [], [], 0
    for kind, array in zip(kinds, arrays):
        if kind == "spread":
            shapes.append(jax.ShapeDtypeStruct(array.shape, array.dtype))
            counts.append(0)
            total += 7
            continue
        tail = array.shape[-2:]
        parts = reduce_plan(kind, far, fsdp, tail)[1]
        own = reduce_shapes(kind, far, fsdp, tail, array.dtype)
        counts.append(len(own))
        scratch += [pltpu.VMEM(shape, array.dtype) for shape in own]
        shapes.append(jax.ShapeDtypeStruct(tail, F32))
        total += sum(1 + len(order) + (far - 2 if "h" in order else 0) for _, _, order in parts)
    return pl.pallas_call(
        functools.partial(reduce_kernel, kinds, far, fsdp, tuple(counts)),
        out_shape=tuple(shapes),
        in_specs=[ANY] * len(arrays),
        out_specs=tuple(
            ANY if kind == "spread" else pl.BlockSpec(memory_space=pltpu.VMEM) for kind in kinds
        ),
        scratch_shapes=scratch
        + [
            pltpu.SemaphoreType.DMA((total,)),
            pltpu.SemaphoreType.DMA((total,)),
            pltpu.SemaphoreType.DMA((len(arrays), 4)),
        ],
        compiler_params=pltpu.CompilerParams(collective_id=number, has_side_effects=True),
        cost_estimate=pl.CostEstimate(flops=0, bytes_accessed=COST, transcendentals=0),
        name=name,
    )(*arrays)


def body(
    sizes,
    inputs,
    lengths,
    attn_gain,
    query_weight,
    query_bias,
    key_matrix,
    key_bias_vector,
    value_matrix,
    value_bias_vector,
    output_weight,
    mlp_gain,
    gate_weight,
    up_weight,
    down_weight,
    cotangent,
):
    far, fsdp = sizes
    micro, token_rows, width = inputs.shape[1:]
    shard = query_weight.shape[0]
    kv_width = key_matrix.shape[1]
    hidden_width = gate_weight.shape[1]
    devices = far * 8 * fsdp
    seq = far * 8
    ih, ip, iy, ic, ix = (lax.axis_index(name) for name in ("h", "p", "y", "c", "x"))
    me8 = (ip * 2 + iy) * 2 + ic
    me_seq = ih * 8 + me8

    def hop(array, axis, shift=1):
        if axis == "h":
            return lax.ppermute(array, "h", [(i, (i + shift) % far) for i in range(far)])
        return lax.ppermute(array, axis, SWAP)

    def pick(array, index, axis):
        return lax.dynamic_index_in_dim(array, index, axis, keepdims=False)

    slice_width = hidden_width // 8

    gate_cut, up_cut = cut_columns(far, False, (gate_weight, up_weight))

    vectors = jnp.concatenate(
        [attn_gain, query_bias, key_bias_vector, value_bias_vector, mlp_gain]
    ).astype(F32)
    vectors = jnp.pad(vectors, (0, 1024 - vectors.shape[0])).reshape(8, 128)
    w_qkv, vectors, gate_parts, up_parts, w_down = move(
        "gather_first",
        0,
        far,
        fsdp,
        ("all_y", "all", "spread", "spread", "pair"),
        (
            jnp.concatenate([query_weight, key_matrix, value_matrix], axis=1),
            vectors,
            gate_cut,
            up_cut,
            down_weight,
        ),
    )
    w_down = w_down.reshape(slice_width, width)
    w_qkv = w_qkv.reshape(width, -1)
    vectors = vectors.reshape(devices, 1024)
    cuts = [0]
    for part in (attn_gain, query_bias, key_bias_vector, value_bias_vector, mlp_gain):
        cuts.append(cuts[-1] + part.shape[0])
    gain_attn, b_query, b_key, b_value, gain_mlp = (
        vectors[:, cuts[i] : cuts[i + 1]].reshape(-1) for i in range(5)
    )
    rows = inputs[0].astype(F32).reshape(micro * token_rows, width)
    upstream_low = cotangent[0].reshape(micro * token_rows, width)
    positions_at = me_seq * token_rows + jnp.arange(token_rows, dtype=jnp.int32)
    tables, spans, metas = [], [], []
    for number in range(micro):
        offsets, first = locate(lengths[0, number], positions_at)
        tables.append(rotary_tables(offsets, HEAD_WIDTH))
        spans.append(
            jnp.concatenate(
                [
                    jnp.tile(first, GROUP)[None],
                    jnp.tile(positions_at, GROUP)[None],
                    jnp.zeros((6, GROUP * token_rows), jnp.int32),
                ],
                axis=0,
            )
        )
        low = jnp.maximum(first[0] // token_rows, me_seq - seq // 2)
        metas.append(jnp.stack([low, me_seq]).astype(jnp.int32))
    cosine_table = jnp.concatenate([t[0] for t in tables], axis=0)
    sine_table = jnp.concatenate([t[1] for t in tables], axis=0)

    normed, recip_one = rms_forward(rows, gain_attn)
    normed_low = normed.astype(BF16)
    pre = mat_dot(normed_low, w_qkv)
    heads = range(QUERY_HEADS + KEY_VALUE_HEADS)
    splits = ((0, micro * token_rows, 0, width),) + tuple(
        (m * token_rows, token_rows, width, 2 * kv_width) for m in range(micro)
    )
    biases = jnp.concatenate([b_query, b_key, b_value])[None]
    query_rotated, *own_kv = rotate(pre, biases, cosine_table, sine_table, heads, splits, 1.0)
    moved = move(
        "gather_second",
        1,
        far,
        fsdp,
        ("seq",) * micro + ("all_y", "pair8", "pair8", "group"),
        tuple(own_kv) + (output_weight, gate_parts, up_parts, upstream_low),
    )
    stacks = [part.reshape(seq, token_rows, 2 * kv_width) for part in moved[:micro]]
    w_output = moved[micro].reshape(width, width)
    w_gate, w_up = (part.reshape(width, slice_width) for part in moved[micro + 1 : micro + 3])
    upstream_all = moved[micro + 3].reshape(-1, width)
    attended, lses = [], []
    for m in range(micro):
        result, lse = attend_forward(m, metas[m], query_rotated, stacks[m], spans[m])
        attended.append(result)
        lses.append(lse)
    attended = jnp.concatenate(attended, axis=0)
    middle = rows + mat_dot(attended, w_output)
    normed_two, recip_two = rms_forward(middle, gain_mlp)
    (tokens,) = move("gather_tokens", 2, far, fsdp, ("group",), (normed_two.astype(BF16),))
    tokens = tokens.reshape(-1, width)

    tokens_turned, hidden, hidden_turned, grad_gate, grad_up = hidden_units(
        micro * token_rows, tokens, upstream_all, w_gate, w_up, w_down
    )
    group = (2, 2, 2, micro * token_rows, width)

    def over_x(grad, axis, other):
        grad = grad.astype(BF16)
        sent, other = lax.optimization_barrier((pick(grad, 1 - ix, axis), other))
        kept = pick(grad, ix, axis).astype(F32) + hop(sent, "x").astype(F32)
        return kept.astype(BF16), other

    def over_h(kept):
        total = pick(kept, ih, 0).astype(F32)
        for k in range(1, far):
            total = total + hop(pick(kept, (ih + k) % far, 0), "h", k).astype(F32)
        return total

    eight = (far, 8, fsdp, shard, slice_width)
    turned = tokens_turned.reshape(far, 8, fsdp, shard, -1)
    gate_sum, grad_up_last = over_x(dot(turned, grad_gate, ((4,), (0,))), 2, grad_up)
    up_sum, _ = over_x(dot(turned, grad_up_last, ((4,), (0,))), 2, ())
    grad_two = (cols_dot(grad_gate, w_gate) + cols_dot(grad_up, w_up)).astype(BF16)

    (grad_two,) = reduce("reduce_tokens", 3, far, fsdp, ("group",), (grad_two.reshape(group),))
    grad_norm, gain_mlp_sum = rms_backward(middle, recip_two, gain_mlp, grad_two)
    grad_middle = upstream_low.astype(F32) + grad_norm
    grad_branch = grad_middle.astype(BF16)
    grad_branch, gate_sum, up_sum = lax.optimization_barrier((grad_branch, gate_sum, up_sum))
    gate_sum = over_h(gate_sum).astype(BF16)
    grad_attended = cols_dot(grad_branch, w_output).astype(BF16)
    grad_kvs, grad_query = [], []
    for m in range(micro):
        query_part, grad_kv = attend_backward(
            m,
            metas[m],
            query_rotated,
            grad_attended,
            stacks[m],
            spans[m],
            lses[m],
            cosine_table,
            sine_table,
        )
        grad_kvs.append(grad_kv.reshape(far, 2, 2, 2, token_rows, 2 * kv_width))
        grad_query.append(query_part)

    blocks = (far, 2, 2, 2, fsdp, shard)
    grad_kvs, gate_sum, up_sum, hidden, hidden_turned = lax.optimization_barrier(
        (grad_kvs, gate_sum, up_sum, hidden, hidden_turned)
    )
    up_sum = over_h(up_sum).astype(BF16)
    down_part, _ = over_x(
        mat_dot(hidden_turned, upstream_all).reshape(far, fsdp, -1, width), 1, ()
    )
    final = mat_dot(hidden, w_down).astype(BF16)
    g_output = rows_dot(attended, grad_branch).astype(BF16)
    reduced = reduce(
        "reduce_second",
        4,
        far,
        fsdp,
        tuple("seq_turned" if m % 2 else "seq" for m in range(micro)) + ("all_x", "group"),
        tuple(grad_kvs) + (g_output.reshape(blocks + (width,)), final.reshape(group)),
    )
    grad_kvs, output_part = list(reduced[:micro]), reduced[micro]
    grad_kvs[0], down_part = lax.optimization_barrier((grad_kvs[0], down_part))
    down_part = over_h(down_part)
    results = (middle + reduced[micro + 1]).astype(BF16)
    grad_query = jnp.concatenate(grad_query, axis=0)
    grad_kv = jnp.concatenate(grad_kvs, axis=0)
    (grad_kv,) = rotate(
        grad_kv,
        jnp.zeros((1, 2 * kv_width), F32),
        cosine_table,
        sine_table,
        range(KEY_VALUE_HEADS),
        ((0, micro * token_rows, 0, 2 * kv_width),),
        -1.0,
    )
    grad_pre = jnp.concatenate([grad_query, grad_kv], axis=1)
    grad_normed = cols_dot(grad_pre, w_qkv)
    grad_rows, gain_attn_sum = rms_backward(rows, recip_one, gain_attn, grad_normed)
    input_grad = grad_middle + grad_rows
    g_qkv = rows_dot(normed_low, grad_pre).astype(BF16)
    bias_sum = jnp.sum(grad_pre.astype(F32), axis=0)
    vector_sums = jnp.concatenate(
        [
            v.reshape(devices, -1)
            for v in (
                gain_attn_sum,
                bias_sum[:width],
                bias_sum[width : width + kv_width],
                bias_sum[width + kv_width :],
                gain_mlp_sum,
            )
        ],
        axis=1,
    )
    vector_sums = jnp.pad(vector_sums, ((0, 0), (0, 1024 - vector_sums.shape[1])))
    qkv_part, vector_part, gate_sum, up_sum = reduce(
        "reduce_last",
        5,
        far,
        fsdp,
        ("all", "all", "spread", "spread"),
        (
            g_qkv.reshape(blocks + (-1,)),
            vector_sums.reshape(far, 2, 2, 2, fsdp, 8, 128),
            gate_sum,
            up_sum,
        ),
    )
    vector_part = vector_part.reshape(-1)

    gate_grad, up_grad = cut_columns(far, True, (gate_sum, up_sum))

    return (
        results.reshape(1, micro, token_rows, width),
        input_grad.reshape(1, micro, token_rows, width),
        vector_part[cuts[0] : cuts[1]],
        qkv_part[:, :width],
        vector_part[cuts[1] : cuts[2]],
        qkv_part[:, width : width + kv_width],
        vector_part[cuts[2] : cuts[3]],
        qkv_part[:, width + kv_width :],
        vector_part[cuts[3] : cuts[4]],
        output_part,
        vector_part[cuts[4] : cuts[5]],
        gate_grad,
        up_grad,
        down_part,
    )


def solution(mesh):
    fsdp = mesh.shape["fsdp"]
    far = mesh.shape["seq"] // 8
    inner = Mesh(mesh.devices.reshape(far, 2, 2, 2, fsdp), ("h", "p", "y", "c", "x"))
    seq = ("h", "p", "y", "c")
    every = seq + ("x",)
    tokens = P("x", None, seq, None)
    matrix, vector = P(every, None), P(every)
    in_specs = (
        tokens,
        P("x", None, None),
        vector,
        matrix,
        vector,
        matrix,
        vector,
        matrix,
        vector,
        matrix,
        vector,
        matrix,
        matrix,
        matrix,
        tokens,
    )
    out_specs = (
        tokens,
        tokens,
        vector,
        matrix,
        vector,
        matrix,
        vector,
        matrix,
        vector,
        matrix,
        vector,
        matrix,
        matrix,
        matrix,
    )
    return jax.shard_map(
        functools.partial(body, (far, fsdp)),
        mesh=inner,
        in_specs=in_specs,
        out_specs=out_specs,
        check_vma=False,
    )
```

```python
import functools

import jax
import jax.numpy as jnp
from jax import lax
from jax.experimental import pallas as pl
from jax.experimental.pallas import tpu as pltpu
from jax.sharding import Mesh, PartitionSpec as P

QUERY_HEADS = 12
KEY_VALUE_HEADS = 2
HEAD_WIDTH = 128
EPSILON = 1e-06
THETA = 10000.0
GROUP = QUERY_HEADS // KEY_VALUE_HEADS
SCALE = HEAD_WIDTH ** (-0.5)
F32 = jnp.float32
BF16 = jnp.bfloat16
SWAP = [(0, 1), (1, 0)]


def locate(item_lengths, positions_at):
    ends = jnp.cumsum(item_lengths)
    starts = ends - item_lengths
    segment_ids = jnp.sum((ends[None, :] <= positions_at[:, None]).astype(jnp.int32), axis=1)
    onehot = segment_ids[:, None] == jnp.arange(item_lengths.shape[0], dtype=jnp.int32)[None, :]
    first = jnp.sum(jnp.where(onehot, starts[None, :], 0), axis=1)
    return (positions_at - first, first)


def rotary_tables(offsets, head_size):
    freqs = 1.0 / THETA ** (jnp.arange(0, head_size, 2, dtype=F32) / head_size)
    angles = offsets.astype(F32)[:, None] * freqs[None, :]
    cosine, sine = jnp.cos(angles), jnp.sin(angles)
    return (jnp.concatenate([cosine, cosine], axis=1), jnp.concatenate([-sine, sine], axis=1))


def rms_forward(rows, gain):
    recip = lax.rsqrt(jnp.mean(rows * rows, axis=-1, keepdims=True) + EPSILON)
    return (rows * recip * gain, recip)


def rms_backward(rows, recip, gain, upstream):
    weighted = upstream * gain
    grad_rows = recip * weighted - rows * (recip * recip * recip) * jnp.mean(
        rows * weighted, axis=-1, keepdims=True
    )
    gain_grad = jnp.sum(upstream * rows * recip, axis=0)
    return (grad_rows, gain_grad)


def dot(left, right, dims, out=F32):
    return lax.dot_general(left, right, ((dims[0], dims[1]), ((), ())), preferred_element_type=out)


def rows_dot(left, right):
    return dot(left, right, ((0,), (0,)))


def cols_dot(left, right):
    return dot(left, right, ((1,), (1,)))


def mat_dot(left, right):
    return dot(left, right, ((1,), (0,)))


def attend_forward_kernel(meta, q_ref, k_ref, v_ref, span_ref, o_ref, lse_ref):
    rows = q_ref.shape[0]
    queries = jnp.concatenate(
        [q_ref[:, h * HEAD_WIDTH : (h + 1) * HEAD_WIDTH] for h in range(GROUP)], axis=0
    )
    first, last = span_ref[0:1, :], span_ref[1:2, :]
    wide = GROUP * rows
    local = lax.broadcasted_iota(jnp.int32, (rows, 1), 0)

    def step(block, carry):
        top, total, accum = carry
        keys, values = k_ref[block], v_ref[block]
        scores = dot(keys, queries, ((1,), (1,))) * SCALE
        index = block * rows + local
        scores = jnp.where((index >= first) & (index <= last), scores, -1e30)
        new_top = jnp.maximum(top, jnp.max(scores, axis=0, keepdims=True))
        fade = jnp.exp(top - new_top)
        probs = jnp.exp(scores - new_top)
        total = total * fade + jnp.sum(probs, axis=0, keepdims=True)
        accum = accum * fade + dot(values, probs.astype(BF16), ((0,), (0,)))
        return (new_top, total, accum)

    top, total, accum = lax.fori_loop(
        meta[0],
        meta[1] + 1,
        step,
        (
            jnp.full((1, wide), -1e30, F32),
            jnp.zeros((1, wide), F32),
            jnp.zeros((HEAD_WIDTH, wide), F32),
        ),
    )
    attended = (accum / total).T.astype(BF16)
    for h in range(GROUP):
        o_ref[:, h * HEAD_WIDTH : (h + 1) * HEAD_WIDTH] = attended[h * rows : (h + 1) * rows]
    lse_ref[0] = top + jnp.log(total)


def attend_forward(number, meta, queries, stack, span):
    pieces, rows, _ = stack.shape
    width = queries.shape[1]
    part = width // KEY_VALUE_HEADS
    spec = pltpu.PrefetchScalarGridSpec(
        num_scalar_prefetch=1,
        grid=(KEY_VALUE_HEADS,),
        in_specs=[
            pl.BlockSpec((rows, part), lambda g, m: (number, g)),
            pl.BlockSpec((pieces, rows, HEAD_WIDTH), lambda g, m: (0, 0, g)),
            pl.BlockSpec((pieces, rows, HEAD_WIDTH), lambda g, m: (0, 0, KEY_VALUE_HEADS + g)),
            pl.BlockSpec((8, GROUP * rows), lambda g, m: (0, 0)),
        ],
        out_specs=[
            pl.BlockSpec((rows, part), lambda g, m: (0, g)),
            pl.BlockSpec((1, 1, GROUP * rows), lambda g, m: (g, 0, 0)),
        ],
    )
    return pl.pallas_call(
        attend_forward_kernel,
        grid_spec=spec,
        out_shape=(
            jax.ShapeDtypeStruct((rows, width), BF16),
            jax.ShapeDtypeStruct((KEY_VALUE_HEADS, 1, GROUP * rows), F32),
        ),
        cost_estimate=pl.CostEstimate(
            flops=4 * rows * rows * 6 * width, bytes_accessed=stack.size * 2, transcendentals=0
        ),
        name="attend_forward",
    )(meta, queries, stack, stack, span)


def attend_backward_kernel(
    meta, q_ref, do_ref, kv_ref, span_ref, lse_ref, cos_ref, sin_ref, dq_ref, dkv_ref, p_ref, dp_ref
):
    rows = q_ref.shape[0]
    wide = GROUP * rows
    first, last = span_ref[0:1, :], span_ref[1:2, :]
    local = lax.broadcasted_iota(jnp.int32, (rows, 1), 0)
    low = meta[0]
    cosine, sine = cos_ref[...], sin_ref[...]
    dkv_ref[...] = jnp.zeros_like(dkv_ref)
    for group in range(KEY_VALUE_HEADS):
        heads = range(group * GROUP, (group + 1) * GROUP)
        cols = [slice(h * HEAD_WIDTH, (h + 1) * HEAD_WIDTH) for h in heads]
        key_cols = slice(group * HEAD_WIDTH, (group + 1) * HEAD_WIDTH)
        start = (KEY_VALUE_HEADS + group) * HEAD_WIDTH
        value_cols = slice(start, start + HEAD_WIDTH)
        queries = jnp.concatenate([q_ref[:, c] for c in cols], axis=0)
        grads = jnp.concatenate([do_ref[:, c] for c in cols], axis=0)
        lse = lse_ref[group]

        def collect(block, delta):
            scores = dot(kv_ref[block, :, key_cols], queries, ((1,), (1,))) * SCALE
            index = block * rows + local
            probs = jnp.where((index >= first) & (index <= last), jnp.exp(scores - lse), 0.0)
            grad_probs = dot(kv_ref[block, :, value_cols], grads, ((1,), (1,)))
            p_ref[block - low] = probs
            dp_ref[block - low] = grad_probs
            return delta + jnp.sum(probs * grad_probs, axis=0, keepdims=True)

        delta = lax.fori_loop(low, meta[1] + 1, collect, jnp.zeros((1, wide), F32))

        def spread(block, accum):
            probs = p_ref[block - low]
            grad_scores = (probs * (dp_ref[block - low] - delta)).astype(BF16)
            dkv_ref[block, :, key_cols] = (mat_dot(grad_scores, queries) * SCALE).astype(BF16)
            dkv_ref[block, :, value_cols] = mat_dot(probs.astype(BF16), grads).astype(BF16)
            return accum + dot(kv_ref[block, :, key_cols], grad_scores, ((0,), (0,)))

        accum = lax.fori_loop(low, meta[1] + 1, spread, jnp.zeros((HEAD_WIDTH, wide), F32))
        grad_queries = (accum * SCALE).T
        for h in range(GROUP):
            part = grad_queries[h * rows : (h + 1) * rows]
            turned = pltpu.roll(part, HEAD_WIDTH // 2, 1)
            dq_ref[:, cols[h]] = (part * cosine - turned * sine).astype(BF16)


def attend_backward(number, meta, queries, grads, stack, span, lse, cosine, sine):
    pieces, rows, wide = stack.shape
    width = queries.shape[1]
    most = pieces // 2 + 1

    def own(columns):
        return pl.BlockSpec((rows, columns), lambda i, m: (number, 0))

    def whole(shape):
        return pl.BlockSpec(shape, lambda i, m: (0,) * len(shape))

    spec = pltpu.PrefetchScalarGridSpec(
        num_scalar_prefetch=1,
        grid=(1,),
        in_specs=[
            own(width),
            own(width),
            whole(stack.shape),
            whole(span.shape),
            whole(lse.shape),
            own(HEAD_WIDTH),
            own(HEAD_WIDTH),
        ],
        out_specs=[whole((rows, width)), whole(stack.shape)],
        scratch_shapes=[
            pltpu.VMEM((most, rows, GROUP * rows), F32),
            pltpu.VMEM((most, rows, GROUP * rows), F32),
        ],
    )
    return pl.pallas_call(
        attend_backward_kernel,
        grid_spec=spec,
        out_shape=(
            jax.ShapeDtypeStruct((rows, width), BF16),
            jax.ShapeDtypeStruct(stack.shape, BF16),
        ),
        cost_estimate=pl.CostEstimate(
            flops=0, bytes_accessed=COST, transcendentals=0
        ),
        name="attend_backward",
    )(meta, queries, grads, stack, span, lse, cosine, sine)


def hidden_kernel(
    token_ref,
    grad_ref,
    gate_ref,
    up_ref,
    down_ref,
    token_turned_ref,
    hidden_ref,
    turned_ref,
    dgate_ref,
    dup_ref,
):
    tokens = token_ref[...]
    token_turned_ref[...] = tokens.T
    gate_pre = mat_dot(tokens, gate_ref[...])
    up_pre = mat_dot(tokens, up_ref[...])
    grad_hidden = cols_dot(grad_ref[...], down_ref[...])
    sigma = jax.nn.sigmoid(gate_pre)
    activated = gate_pre * sigma
    hidden = activated * up_pre
    hidden_ref[...] = hidden.astype(BF16)
    turned_ref[...] = hidden.T.astype(BF16)
    dgate_ref[...] = (grad_hidden * up_pre * sigma * (1.0 + gate_pre * (1.0 - sigma))).astype(BF16)
    dup_ref[...] = (grad_hidden * activated).astype(BF16)


def hidden_units(rows, tokens, grads, w_gate, w_up, w_down):
    total, width = tokens.shape
    units = w_gate.shape[1]

    def tile(columns):
        return pl.BlockSpec((rows, columns), lambda i: (i, 0))

    def fixed(array):
        return pl.BlockSpec(array.shape, lambda i: (0, 0))

    return pl.pallas_call(
        hidden_kernel,
        grid=(total // rows,),
        in_specs=[tile(width), tile(width), fixed(w_gate), fixed(w_up), fixed(w_down)],
        out_specs=[
            pl.BlockSpec((width, rows), lambda i: (0, i)),
            tile(units),
            pl.BlockSpec((units, rows), lambda i: (0, i)),
            tile(units),
            tile(units),
        ],
        out_shape=(
            jax.ShapeDtypeStruct((width, total), BF16),
            jax.ShapeDtypeStruct((total, units), BF16),
            jax.ShapeDtypeStruct((units, total), BF16),
            jax.ShapeDtypeStruct((total, units), BF16),
            jax.ShapeDtypeStruct((total, units), BF16),
        ),
        cost_estimate=pl.CostEstimate(
            flops=6 * total * width * units, bytes_accessed=8 * total * width, transcendentals=0
        ),
        name="hidden_units",
    )(tokens, grads, w_gate, w_up, w_down)


def rotate_kernel(turned_heads, splits, sign, pre_ref, bias_ref, cos_ref, sin_ref, *outs):
    cosine, sine = cos_ref[...], sin_ref[...] * sign
    for head in range(pre_ref.shape[1] // HEAD_WIDTH):
        cols = slice(head * HEAD_WIDTH, (head + 1) * HEAD_WIDTH)
        part = pre_ref[:, cols] + bias_ref[:, cols]
        if head in turned_heads:
            part = part * cosine + pltpu.roll(part, HEAD_WIDTH // 2, 1) * sine
        part = part.astype(BF16)
        for (top, height, left, wide), out in zip(splits, outs):
            if left <= head * HEAD_WIDTH < left + wide:
                at = head * HEAD_WIDTH - left
                out[:, at : at + HEAD_WIDTH] = part[top : top + height]


def rotate(pre, bias, cosine, sine, turned_heads, splits, sign):
    return pl.pallas_call(
        functools.partial(rotate_kernel, tuple(turned_heads), splits, sign),
        out_shape=tuple(
            jax.ShapeDtypeStruct((height, wide), BF16) for _, height, _, wide in splits
        ),
        cost_estimate=pl.CostEstimate(flops=0, bytes_accessed=8 * pre.size, transcendentals=0),
        name="rotate",
    )(pre, bias, cosine, sine)


def cut_kernel(far, whole, *refs):
    count = len(refs) // 2
    for source, out in zip(refs[:count], refs[count:]):
        small = (out if whole else source).shape[1] // (8 * far)
        for h in range(far):
            for g in range(8):
                left, right = (h * 8 + g) * small, h * small
                if whole:
                    out[:, left : left + small] = source[g, :, right : right + small].astype(F32)
                else:
                    out[g, :, right : right + small] = source[:, left : left + small]


def cut_columns(far, whole, arrays):
    shapes = []
    for array in arrays:
        if whole:
            shapes.append(jax.ShapeDtypeStruct((array.shape[1], 8 * array.shape[2]), F32))
        else:
            shape = (8, array.shape[0], array.shape[1] // 8)
            shapes.append(jax.ShapeDtypeStruct(shape, array.dtype))
    return pl.pallas_call(
        functools.partial(cut_kernel, far, whole),
        out_shape=tuple(shapes),
        name="join_columns" if whole else "cut_columns",
    )(*arrays)


MESH = pl.DeviceIdType.MESH
PARTS, AHEAD = {"pair": 4, "pair8": 8}, 2
COST = 1024
ANY = pl.BlockSpec(memory_space=pl.ANY)


class Local:
    def __init__(self, source, buffer, target, sems):
        self.load = pltpu.make_async_copy(source, buffer, sems.at[0])
        self.store = pltpu.make_async_copy(buffer, target, sems.at[1])

    def start(self):
        self.load.start()

    def turn(self):
        self.load.wait()
        self.store.start()

    def wait(self):
        self.store.wait()


class Copies:
    def __init__(self, send_sems, recv_sems):
        self.send_sems, self.recv_sems, self.started = send_sems, recv_sems, []

    def start(self, source, target, device):
        number = len(self.started)
        copy = pltpu.make_async_remote_copy(
            src_ref=source,
            dst_ref=target,
            send_sem=self.send_sems.at[number],
            recv_sem=self.recv_sems.at[number],
            device_id=device,
            device_id_type=MESH,
        )
        copy.start()
        self.started.append(copy)
        return copy


def greet(devices):
    barrier = pltpu.get_barrier_semaphore()
    for device in devices:
        pl.semaphore_signal(barrier, inc=1, device_id=device, device_id_type=MESH)
    pl.semaphore_wait(barrier, len(devices))


def other_h(far, k):
    return {"h": lax.rem(lax.axis_index("h") + k, far)}


def flip(*axes):
    return {axis: 1 - lax.axis_index(axis) for axis in axes}


def corners():
    return [flip("p", "y"), flip("p", "c"), flip("y", "c"), flip("p", "y", "c")]


def gather_steps(kind, far, copies, source, out, local):
    ih, ip, iy, ic, ix = (lax.axis_index(name) for name in ("h", "p", "y", "c", "x"))
    every = kind in ("all", "all_y")

    def block(h, p, y=iy, x=ix):
        return out.at[h, p, y, ic, x] if every else out.at[h, p, y, ic]

    local.start()
    pieces = [(lax.rem(ih - k + far, far), p) for p in (ip, 1 - ip) for k in range(far)]
    count = len(pieces)
    arrivals, plane, cross, core = [None] * count, [None] * count, [None] * count, [None] * count
    columns = source.shape[-1]
    half = columns // 2 if columns % 256 == 0 and kind == "all" else columns

    def cut(ref, first):
        if half == columns:
            return ref
        return ref.at[:, pl.ds(0 if first else half, half)]

    for k in range(1, far):
        arrivals[k] = copies.start(source, block(ih, ip), other_h(far, k))
    for step in range(count + 3):
        if step < count:
            if arrivals[step] is not None:
                arrivals[step].wait_recv()
            h, p = pieces[step]
            held = source if step == 0 else block(h, p)
            if step < far:
                arrivals[far + step] = copies.start(held, block(h, p), flip("p"))
            plane[step] = [copies.start(held, block(h, p), flip("y"))]
            if every:
                plane[step].append(copies.start(held, block(h, p), flip("x")))
        if 0 <= step - 1 < count:
            h, p = pieces[step - 1]
            for copy in plane[step - 1]:
                copy.wait_recv()
            cross[step - 1] = []
            if every:
                ref = cut(block(h, p, x=1 - ix), True)
                cross[step - 1].append(copies.start(ref, ref, flip("y")))
                if half < columns:
                    ref = cut(block(h, p, y=1 - iy), False)
                    cross[step - 1].append(copies.start(ref, ref, flip("x")))
        if 0 <= step - 2 < count:
            h, p = pieces[step - 2]
            for copy in cross[step - 2]:
                copy.wait_recv()
            if step == 2:
                local.wait()
            ref = out.at[h, p, :, ic]
            core[step - 2] = copies.start(ref, ref, flip("c"))
        if 0 <= step - 3 < count:
            core[step - 3].wait_recv()
        yield


def group_steps(far, copies, source, out, local, delay):
    ip, iy, ic = (lax.axis_index(name) for name in ("p", "y", "c"))
    half = source.shape[0] // 2
    top, low = pl.ds(0, half), pl.ds(half, half)

    def rows(p, y, part):
        return out.at[p, y, ic, part]

    def forward(ref, axis):
        return copies.start(ref, ref, flip(axis))

    local.start()
    for _ in range(delay):
        yield
    first = [
        copies.start(source.at[top], rows(ip, iy, top), flip("y")),
        copies.start(source.at[low], rows(ip, iy, low), flip("p")),
    ]
    second = [
        copies.start(source.at[top], rows(ip, iy, top), flip("p")),
        copies.start(source.at[low], rows(ip, iy, low), flip("y")),
    ]
    core = [copies.start(source, out.at[ip, iy, ic], flip("c"))]
    yield
    first[0].wait_recv()
    second.append(forward(rows(ip, 1 - iy, top), "p"))
    core.append(forward(rows(ip, 1 - iy, top), "c"))
    first[1].wait_recv()
    second.append(forward(rows(1 - ip, iy, low), "y"))
    core.append(forward(rows(1 - ip, iy, low), "c"))
    yield
    for copy, p, y, part in (
        (second[0], 1 - ip, iy, top),
        (second[1], ip, 1 - iy, low),
        (second[2], 1 - ip, 1 - iy, top),
        (second[3], 1 - ip, 1 - iy, low),
    ):
        copy.wait_recv()
        core.append(forward(rows(p, y, part), "c"))
    yield
    for copy in core:
        copy.wait_recv()
    local.wait()


def pair_steps(far, copies, parts, place, local, delay):
    ih, ix = lax.axis_index("h"), lax.axis_index("x")
    local.start()
    for _ in range(delay):
        yield
    arrived, sent = [], []

    def send(i):
        if i < len(parts):
            target = place(ih, ix, i)
            arrived.append([copies.start(parts[i], target, other_h(far, k)) for k in range(1, far)])
            sent.append(copies.start(parts[i], target, flip("x")))

    for i in range(AHEAD):
        send(i)
    for i in range(len(parts)):
        yield
        send(i + AHEAD)
        for k in range(1, far):
            arrived[i][k - 1].wait_recv()
            ref = place(lax.rem(ih - k + far, far), ix, i)
            sent.append(copies.start(ref, ref, flip("x")))
    yield
    for copy in sent:
        copy.wait_recv()
    local.wait()


def spread_steps(far, copies, source, out, local, delay):
    ip, iy, ic = (lax.axis_index(name) for name in ("p", "y", "c"))
    me = (ip * 2 + iy) * 2 + ic
    local.start()
    for _ in range(delay):
        yield
    started = []
    for j in (1, 2, 4, 3, 5, 6, 7):
        p = 1 - ip if j & 4 else ip
        y = 1 - iy if j & 2 else iy
        c = 1 - ic if j & 1 else ic
        started.append(
            copies.start(source.at[(p * 2 + y) * 2 + c], out.at[me], {"p": p, "y": y, "c": c})
        )
    for _ in range(2 * far + 2):
        yield
    for copy in started:
        copy.wait_recv()
    local.wait()
    yield


def move_kernel(kinds, far, *refs):
    count = len(kinds)
    sources, outs = refs[:count], refs[count : 2 * count]
    buffers = refs[2 * count : 3 * count]
    send_sems, recv_sems, local_sems = refs[3 * count :]
    locals_ = []

    def local_copy(i, source, target):
        locals_.append(Local(source, buffers[i], target, local_sems.at[i]))
        return locals_[-1]

    ih, ip, iy, ic, ix = (lax.axis_index(name) for name in ("h", "p", "y", "c", "x"))
    partners = [flip("p"), flip("y"), flip("c")]
    if set(kinds) - {"spread", "group"}:
        partners += [other_h(far, k) for k in range(1, far)]
    if set(kinds) - {"seq", "group", "spread"}:
        partners.append(flip("x"))
    if "spread" in kinds:
        partners += corners()
    greet(partners)
    copies = Copies(send_sems, recv_sems)
    running = []
    for i, kind in enumerate(kinds):
        if kind == "spread":
            me = (ip * 2 + iy) * 2 + ic
            local = local_copy(i, sources[i].at[me], outs[i].at[me])
            running.append(spread_steps(far, copies, sources[i], outs[i], local, 0))
        elif kind == "group":
            place = outs[i].at[ip, iy, ic]
            local = local_copy(i, sources[i], place)
            delay = 3 if count > 1 else 0
            running.append(group_steps(far, copies, sources[i], outs[i], local, delay))
        elif kind in ("pair", "pair8"):
            local = outs[i].at[ih, :, ix] if kind == "pair8" else outs[i].at[ih, ix]
            local = local_copy(i, sources[i], local)
            step = (8 if kind == "pair8" else sources[i].shape[1]) // PARTS[kind]
            cuts = [pl.ds(part * step, step) for part in range(PARTS[kind])]
            if kind == "pair8":
                parts = [sources[i].at[c] for c in cuts]
            else:
                parts = [sources[i].at[:, c] for c in cuts]

            def place(h, x, part, out=outs[i], cuts=cuts, wide=kind == "pair8"):
                return out.at[h, cuts[part], x] if wide else out.at[h, x, :, cuts[part]]

            wait = (PARTS[kind] - AHEAD + 1) * kinds[:i].count("pair8")
            running.append(pair_steps(far, copies, parts, place, local, wait))
        else:
            place = (ih, ip, iy, ic) if kind == "seq" else (ih, ip, iy, ic, ix)
            local = local_copy(i, sources[i], outs[i].at[place])
            running.append(gather_steps(kind, far, copies, sources[i], outs[i], local))
    running = [job for job in running if next(job, "end") != "end"]
    for local in locals_:
        local.turn()
    while running:
        running = [job for job in running if next(job, "end") != "end"]
    for copy in copies.started:
        copy.wait_send()


def move(name, number, far, fsdp, kinds, arrays):
    shapes, total = [], 0
    pieces = 2 * far
    for kind, array in zip(kinds, arrays):
        if kind in ("all", "all_y"):
            lead, total = (far, 2, 2, 2, fsdp), total + (far - 1) + far + 5 * pieces
        elif kind == "seq":
            lead, total = (far, 2, 2, 2), total + (far - 1) + far + 2 * pieces
        elif kind == "group":
            lead, total = (2, 2, 2), total + 13
        elif kind == "pair":
            lead, total = (far, fsdp), total + PARTS[kind] * (2 * far - 1)
        elif kind == "pair8":
            lead, total = (far, 8, fsdp), total + PARTS[kind] * (2 * far - 1)
        else:
            lead, total = (), total + 7
        tail = array.shape[1:] if kind == "pair8" else array.shape
        shapes.append(jax.ShapeDtypeStruct(lead + tail, array.dtype))
    return pl.pallas_call(
        functools.partial(move_kernel, kinds, far),
        out_shape=tuple(shapes),
        in_specs=[ANY] * len(arrays),
        out_specs=tuple([ANY] * len(arrays)),
        scratch_shapes=[
            pltpu.VMEM(a.shape[1:] if kind == "spread" else a.shape, a.dtype)
            for kind, a in zip(kinds, arrays)
        ]
        + [
            pltpu.SemaphoreType.DMA((total,)),
            pltpu.SemaphoreType.DMA((total,)),
            pltpu.SemaphoreType.DMA((len(arrays), 2)),
        ],
        compiler_params=pltpu.CompilerParams(collective_id=number, has_side_effects=True),
        cost_estimate=pl.CostEstimate(flops=0, bytes_accessed=COST, transcendentals=0),
        name=name,
    )(*arrays)


def reduce_plan(kind, far, fsdp, tail):
    rows, columns = tail
    if kind == "group":
        step = rows // 4
        return ("p", "y"), [
            ((pl.ds(i * step, step), slice(None)), (step, columns), ("yp", "py")[i % 2])
            for i in range(4)
        ]
    if kind in ("seq", "seq_turned"):
        order = ("y", "p", "h") if kind == "seq" else ("p", "y", "h")
        return ("h", "p", "y"), [((slice(None), slice(None)), tail, order)]
    names = ("h", "p", "y", "x")
    if columns % 256:
        return names, [((slice(None), slice(None)), tail, ("x", "y", "p", "h"))]
    count = 4 if columns % 512 == 0 else 2
    step = columns // count
    orders = (("x", "y", "p", "h"), ("y", "x", "p", "h")) if kind == "all" else (("x", "y", "p", "h"),) * 2
    return names, [
        ((slice(None), pl.ds(i * step, step)), (rows, step), orders[i % 2]) for i in range(count)
    ]


def reduce_shapes(kind, far, fsdp, tail, dtype):
    length = {"h": far, "p": 2, "y": 2, "x": fsdp}
    names, parts = reduce_plan(kind, far, fsdp, tail)
    shapes = []
    for _, small, order in parts:
        left = list(names)
        full = tuple(length[n] for n in left) + small
        shapes += [full, full]
        for axis in order:
            left.remove(axis)
            lead = tuple(length[n] for n in left) + small
            shapes.append((far - 1,) + lead if axis == "h" else lead)
    return shapes


def reduce_steps(kind, far, fsdp, copies, source, out, scratch, local_sem):
    place = {name: lax.axis_index(name) for name in ("h", "p", "y", "x")}
    ic = lax.axis_index("c")
    length = {"h": far, "p": 2, "y": 2, "x": fsdp}
    core_dim = 2 if kind == "group" else 3
    names, parts = reduce_plan(kind, far, fsdp, out.shape)
    jobs, position = [], 0
    for cut, small, order in parts:
        count = 2 + len(order)
        jobs.append((cut, small, order, scratch[position : position + count]))
        position += count

    def view(c, cut):
        lead = [slice(None)] * core_dim + [c] + [slice(None)] * (len(names) - core_dim)
        return source.at[tuple(lead) + cut]

    def add(sums, brought, fixed, left, target=None, also=()):
        sizes = [1 if n in also else length[n] for n in left]
        total = 1
        for size in sizes:
            total *= size

        def one(number, _):
            index, rest = {}, number
            for n, size in reversed(list(zip(left, sizes))):
                index[n] = also[n] if n in also else rest % size
                rest = rest // size
            whole = tuple(fixed[n] if n in fixed else index[n] for n in names)
            value = sums[whole].astype(F32) + brought[tuple(index[n] for n in left)].astype(F32)
            if target is None:
                sums[whole] = value.astype(sums.dtype)
            else:
                target(value)
            return 0

        if total == 1:
            one(0, 0)
        else:
            lax.fori_loop(0, total, one, 0)

    loads, sent = [], []
    for i, (cut, small, order, refs) in enumerate(jobs):
        loads.append(pltpu.make_async_copy(view(ic, cut), refs[0], local_sem.at[i]))
        loads[i].start()
        sent.append(copies.start(view(1 - ic, cut), refs[1], flip("c")))
    yield
    for stage in range(len(jobs[0][2]) + 1):
        for i, (cut, small, order, refs) in enumerate(jobs):
            sums, brought = refs[0], refs[1 + stage]
            done = order[:stage]
            left = tuple(n for n in names if n not in done)
            fixed = {n: place[n] for n in done}
            if stage == 0:
                loads[i].wait()
            if stage > 0 and order[stage - 1] == "h":
                for copy in sent[i]:
                    copy.wait_recv()
            else:
                sent[i].wait_recv()
            if stage == len(order):
                if order[-1] == "h":
                    whole = tuple(place[n] for n in names)
                    value = sums[whole].astype(F32)
                    for k in range(far - 1):
                        value = value + brought[k].astype(F32)
                    out[cut] = value
                else:

                    def put(value, cut=cut):
                        out[cut] = value

                    add(sums, brought, fixed, left, put)
                continue
            axis = order[stage]
            if axis == "h":
                add(sums, brought, fixed, left)
                sent[i] = []
                for k in range(1, far):
                    goal = lax.rem(place["h"] + k, far)
                    whole = tuple(goal if n == "h" else place[n] for n in names)
                    sent[i].append(
                        copies.start(sums.at[whole], refs[2 + stage].at[k - 1], other_h(far, k))
                    )
            else:
                add(sums, brought, fixed, left, also={axis: 1 - place[axis]})
                index = tuple(
                    1 - place[n] if n == axis else fixed.get(n, slice(None)) for n in names
                )
                sent[i] = copies.start(sums.at[index], refs[2 + stage], flip(axis))
                add(sums, brought, fixed, left, also={axis: place[axis]})
        yield


def reduce_kernel(kinds, far, fsdp, counts, *refs):
    n = len(kinds)
    sources, outs = refs[:n], refs[n : 2 * n]
    scratch = refs[2 * n : -3]
    send_sems, recv_sems, local_sems = refs[-3:]
    partners = [flip("p"), flip("y"), flip("c")]
    if set(kinds) - {"group", "spread"}:
        partners += [other_h(far, k) for k in range(1, far)]
    if "all" in kinds or "all_x" in kinds:
        partners.append(flip("x"))
    if "spread" in kinds:
        partners += corners()
    greet(partners)
    copies = Copies(send_sems, recv_sems)
    running, position = [], 0
    for i, kind in enumerate(kinds):
        if kind == "spread":
            me = (lax.axis_index("p") * 2 + lax.axis_index("y")) * 2 + lax.axis_index("c")
            local = pltpu.make_async_copy(
                sources[i].at[me], outs[i].at[me], local_sems.at[i, 0]
            )
            running.append(spread_steps(far, copies, sources[i], outs[i], local, 1))
            continue
        part = scratch[position : position + counts[i]]
        position += counts[i]
        running.append(
            reduce_steps(
                kind, far, fsdp, copies, sources[i], outs[i], part, local_sems.at[i]
            )
        )
    while running:
        running = [job for job in running if next(job, "end") != "end"]
    for copy in copies.started:
        copy.wait_send()


def reduce(name, number, far, fsdp, kinds, arrays):
    shapes, scratch, counts, total = [], [], [], 0
    for kind, array in zip(kinds, arrays):
        if kind == "spread":
            shapes.append(jax.ShapeDtypeStruct(array.shape, array.dtype))
            counts.append(0)
            total += 7
            continue
        tail = array.shape[-2:]
        parts = reduce_plan(kind, far, fsdp, tail)[1]
        own = reduce_shapes(kind, far, fsdp, tail, array.dtype)
        counts.append(len(own))
        scratch += [pltpu.VMEM(shape, array.dtype) for shape in own]
        shapes.append(jax.ShapeDtypeStruct(tail, F32))
        total += sum(1 + len(order) + (far - 2 if "h" in order else 0) for _, _, order in parts)
    return pl.pallas_call(
        functools.partial(reduce_kernel, kinds, far, fsdp, tuple(counts)),
        out_shape=tuple(shapes),
        in_specs=[ANY] * len(arrays),
        out_specs=tuple(
            ANY if kind == "spread" else pl.BlockSpec(memory_space=pltpu.VMEM) for kind in kinds
        ),
        scratch_shapes=scratch
        + [
            pltpu.SemaphoreType.DMA((total,)),
            pltpu.SemaphoreType.DMA((total,)),
            pltpu.SemaphoreType.DMA((len(arrays), 4)),
        ],
        compiler_params=pltpu.CompilerParams(collective_id=number, has_side_effects=True),
        cost_estimate=pl.CostEstimate(flops=0, bytes_accessed=COST, transcendentals=0),
        name=name,
    )(*arrays)


def body(
    sizes,
    inputs,
    lengths,
    attn_gain,
    query_weight,
    query_bias,
    key_matrix,
    key_bias_vector,
    value_matrix,
    value_bias_vector,
    output_weight,
    mlp_gain,
    gate_weight,
    up_weight,
    down_weight,
    cotangent,
):
    far, fsdp = sizes
    micro, token_rows, width = inputs.shape[1:]
    shard = query_weight.shape[0]
    kv_width = key_matrix.shape[1]
    hidden_width = gate_weight.shape[1]
    devices = far * 8 * fsdp
    seq = far * 8
    ih, ip, iy, ic, ix = (lax.axis_index(name) for name in ("h", "p", "y", "c", "x"))
    me8 = (ip * 2 + iy) * 2 + ic
    me_seq = ih * 8 + me8

    def hop(array, axis, shift=1):
        if axis == "h":
            return lax.ppermute(array, "h", [(i, (i + shift) % far) for i in range(far)])
        return lax.ppermute(array, axis, SWAP)

    def pick(array, index, axis):
        return lax.dynamic_index_in_dim(array, index, axis, keepdims=False)

    slice_width = hidden_width // 8

    gate_cut, up_cut = cut_columns(far, False, (gate_weight, up_weight))

    vectors = jnp.concatenate(
        [attn_gain, query_bias, key_bias_vector, value_bias_vector, mlp_gain]
    ).astype(F32)
    vectors = jnp.pad(vectors, (0, 1024 - vectors.shape[0])).reshape(8, 128)
    w_qkv, vectors, gate_parts, up_parts, w_down = move(
        "gather_first",
        0,
        far,
        fsdp,
        ("all_y", "all", "spread", "spread", "pair"),
        (
            jnp.concatenate([query_weight, key_matrix, value_matrix], axis=1),
            vectors,
            gate_cut,
            up_cut,
            down_weight,
        ),
    )
    w_down = w_down.reshape(slice_width, width)
    w_qkv = w_qkv.reshape(width, -1)
    vectors = vectors.reshape(devices, 1024)
    cuts = [0]
    for part in (attn_gain, query_bias, key_bias_vector, value_bias_vector, mlp_gain):
        cuts.append(cuts[-1] + part.shape[0])
    gain_attn, b_query, b_key, b_value, gain_mlp = (
        vectors[:, cuts[i] : cuts[i + 1]].reshape(-1) for i in range(5)
    )
    rows = inputs[0].astype(F32).reshape(micro * token_rows, width)
    upstream_low = cotangent[0].reshape(micro * token_rows, width)
    positions_at = me_seq * token_rows + jnp.arange(token_rows, dtype=jnp.int32)
    tables, spans, metas = [], [], []
    for number in range(micro):
        offsets, first = locate(lengths[0, number], positions_at)
        tables.append(rotary_tables(offsets, HEAD_WIDTH))
        spans.append(
            jnp.concatenate(
                [
                    jnp.tile(first, GROUP)[None],
                    jnp.tile(positions_at, GROUP)[None],
                    jnp.zeros((6, GROUP * token_rows), jnp.int32),
                ],
                axis=0,
            )
        )
        low = jnp.maximum(first[0] // token_rows, me_seq - seq // 2)
        metas.append(jnp.stack([low, me_seq]).astype(jnp.int32))
    cosine_table = jnp.concatenate([t[0] for t in tables], axis=0)
    sine_table = jnp.concatenate([t[1] for t in tables], axis=0)

    normed, recip_one = rms_forward(rows, gain_attn)
    normed_low = normed.astype(BF16)
    pre = mat_dot(normed_low, w_qkv)
    heads = range(QUERY_HEADS + KEY_VALUE_HEADS)
    splits = ((0, micro * token_rows, 0, width),) + tuple(
        (m * token_rows, token_rows, width, 2 * kv_width) for m in range(micro)
    )
    biases = jnp.concatenate([b_query, b_key, b_value])[None]
    query_rotated, *own_kv = rotate(pre, biases, cosine_table, sine_table, heads, splits, 1.0)
    moved = move(
        "gather_second",
        1,
        far,
        fsdp,
        ("seq",) * micro + ("all_y", "pair8", "pair8", "group"),
        tuple(own_kv) + (output_weight, gate_parts, up_parts, upstream_low),
    )
    stacks = [part.reshape(seq, token_rows, 2 * kv_width) for part in moved[:micro]]
    w_output = moved[micro].reshape(width, width)
    w_gate, w_up = (part.reshape(width, slice_width) for part in moved[micro + 1 : micro + 3])
    upstream_all = moved[micro + 3].reshape(-1, width)
    attended, lses = [], []
    for m in range(micro):
        result, lse = attend_forward(m, metas[m], query_rotated, stacks[m], spans[m])
        attended.append(result)
        lses.append(lse)
    attended = jnp.concatenate(attended, axis=0)
    middle = rows + mat_dot(attended, w_output)
    normed_two, recip_two = rms_forward(middle, gain_mlp)
    (tokens,) = move("gather_tokens", 2, far, fsdp, ("group",), (normed_two.astype(BF16),))
    tokens = tokens.reshape(-1, width)

    tokens_turned, hidden, hidden_turned, grad_gate, grad_up = hidden_units(
        micro * token_rows, tokens, upstream_all, w_gate, w_up, w_down
    )
    group = (2, 2, 2, micro * token_rows, width)

    def over_x(grad, axis, other):
        grad = grad.astype(BF16)
        sent, other = lax.optimization_barrier((pick(grad, 1 - ix, axis), other))
        kept = pick(grad, ix, axis).astype(F32) + hop(sent, "x").astype(F32)
        return kept.astype(BF16), other

    def over_h(kept):
        total = pick(kept, ih, 0).astype(F32)
        for k in range(1, far):
            total = total + hop(pick(kept, (ih + k) % far, 0), "h", k).astype(F32)
        return total

    eight = (far, 8, fsdp, shard, slice_width)
    turned = tokens_turned.reshape(far, 8, fsdp, shard, -1)
    gate_sum, grad_up_last = over_x(dot(turned, grad_gate, ((4,), (0,))), 2, grad_up)
    up_sum, _ = over_x(dot(turned, grad_up_last, ((4,), (0,))), 2, ())
    grad_two = (cols_dot(grad_gate, w_gate) + cols_dot(grad_up, w_up)).astype(BF16)

    (grad_two,) = reduce("reduce_tokens", 3, far, fsdp, ("group",), (grad_two.reshape(group),))
    grad_norm, gain_mlp_sum = rms_backward(middle, recip_two, gain_mlp, grad_two)
    grad_middle = upstream_low.astype(F32) + grad_norm
    grad_branch = grad_middle.astype(BF16)
    grad_branch, gate_sum, up_sum = lax.optimization_barrier((grad_branch, gate_sum, up_sum))
    gate_sum = over_h(gate_sum).astype(BF16)
    grad_attended = cols_dot(grad_branch, w_output).astype(BF16)
    grad_kvs, grad_query = [], []
    for m in range(micro):
        query_part, grad_kv = attend_backward(
            m,
            metas[m],
            query_rotated,
            grad_attended,
            stacks[m],
            spans[m],
            lses[m],
            cosine_table,
            sine_table,
        )
        grad_kvs.append(grad_kv.reshape(far, 2, 2, 2, token_rows, 2 * kv_width))
        grad_query.append(query_part)

    blocks = (far, 2, 2, 2, fsdp, shard)
    grad_kvs, gate_sum, up_sum, hidden, hidden_turned = lax.optimization_barrier(
        (grad_kvs, gate_sum, up_sum, hidden, hidden_turned)
    )
    up_sum = over_h(up_sum).astype(BF16)
    down_part, _ = over_x(
        mat_dot(hidden_turned, upstream_all).reshape(far, fsdp, -1, width), 1, ()
    )
    final = mat_dot(hidden, w_down).astype(BF16)
    g_output = rows_dot(attended, grad_branch).astype(BF16)
    reduced = reduce(
        "reduce_second",
        4,
        far,
        fsdp,
        tuple("seq_turned" if m % 2 else "seq" for m in range(micro)) + ("all_x", "group"),
        tuple(grad_kvs) + (g_output.reshape(blocks + (width,)), final.reshape(group)),
    )
    grad_kvs, output_part = list(reduced[:micro]), reduced[micro]
    grad_kvs[0], down_part = lax.optimization_barrier((grad_kvs[0], down_part))
    down_part = over_h(down_part)
    results = (middle + reduced[micro + 1]).astype(BF16)
    grad_query = jnp.concatenate(grad_query, axis=0)
    grad_kv = jnp.concatenate(grad_kvs, axis=0)
    (grad_kv,) = rotate(
        grad_kv,
        jnp.zeros((1, 2 * kv_width), F32),
        cosine_table,
        sine_table,
        range(KEY_VALUE_HEADS),
        ((0, micro * token_rows, 0, 2 * kv_width),),
        -1.0,
    )
    grad_pre = jnp.concatenate([grad_query, grad_kv], axis=1)
    grad_normed = cols_dot(grad_pre, w_qkv)
    grad_rows, gain_attn_sum = rms_backward(rows, recip_one, gain_attn, grad_normed)
    input_grad = grad_middle + grad_rows
    g_qkv = rows_dot(normed_low, grad_pre).astype(BF16)
    bias_sum = jnp.sum(grad_pre.astype(F32), axis=0)
    vector_sums = jnp.concatenate(
        [
            v.reshape(devices, -1)
            for v in (
                gain_attn_sum,
                bias_sum[:width],
                bias_sum[width : width + kv_width],
                bias_sum[width + kv_width :],
                gain_mlp_sum,
            )
        ],
        axis=1,
    )
    vector_sums = jnp.pad(vector_sums, ((0, 0), (0, 1024 - vector_sums.shape[1])))
    qkv_part, vector_part, gate_sum, up_sum = reduce(
        "reduce_last",
        5,
        far,
        fsdp,
        ("all", "all", "spread", "spread"),
        (
            g_qkv.reshape(blocks + (-1,)),
            vector_sums.reshape(far, 2, 2, 2, fsdp, 8, 128),
            gate_sum,
            up_sum,
        ),
    )
    vector_part = vector_part.reshape(-1)

    gate_grad, up_grad = cut_columns(far, True, (gate_sum, up_sum))

    return (
        results.reshape(1, micro, token_rows, width),
        input_grad.reshape(1, micro, token_rows, width),
        vector_part[cuts[0] : cuts[1]],
        qkv_part[:, :width],
        vector_part[cuts[1] : cuts[2]],
        qkv_part[:, width : width + kv_width],
        vector_part[cuts[2] : cuts[3]],
        qkv_part[:, width + kv_width :],
        vector_part[cuts[3] : cuts[4]],
        output_part,
        vector_part[cuts[4] : cuts[5]],
        gate_grad,
        up_grad,
        down_part,
    )


def solution(mesh):
    fsdp = mesh.shape["fsdp"]
    far = mesh.shape["seq"] // 8
    inner = Mesh(mesh.devices.reshape(far, 2, 2, 2, fsdp), ("h", "p", "y", "c", "x"))
    seq = ("h", "p", "y", "c")
    every = seq + ("x",)
    tokens = P("x", None, seq, None)
    matrix, vector = P(every, None), P(every)
    in_specs = (
        tokens,
        P("x", None, None),
        vector,
        matrix,
        vector,
        matrix,
        vector,
        matrix,
        vector,
        matrix,
        vector,
        matrix,
        matrix,
        matrix,
        tokens,
    )
    out_specs = (
        tokens,
        tokens,
        vector,
        matrix,
        vector,
        matrix,
        vector,
        matrix,
        vector,
        matrix,
        vector,
        matrix,
        matrix,
        matrix,
    )
    return jax.shard_map(
        functools.partial(body, (far, fsdp)),
        mesh=inner,
        in_specs=in_specs,
        out_specs=out_specs,
        check_vma=False,
    )
```

```python
import functools

import jax
import jax.numpy as jnp
from jax import lax
from jax.experimental import pallas as pl
from jax.experimental.pallas import tpu as pltpu
from jax.sharding import Mesh, PartitionSpec as P

QUERY_HEADS = 12
KEY_VALUE_HEADS = 2
HEAD_WIDTH = 128
EPSILON = 1e-06
THETA = 10000.0
GROUP = QUERY_HEADS // KEY_VALUE_HEADS
SCALE = HEAD_WIDTH ** (-0.5)
F32 = jnp.float32
BF16 = jnp.bfloat16
SWAP = [(0, 1), (1, 0)]


def locate(item_lengths, positions_at):
    ends = jnp.cumsum(item_lengths)
    starts = ends - item_lengths
    segment_ids = jnp.sum((ends[None, :] <= positions_at[:, None]).astype(jnp.int32), axis=1)
    onehot = segment_ids[:, None] == jnp.arange(item_lengths.shape[0], dtype=jnp.int32)[None, :]
    first = jnp.sum(jnp.where(onehot, starts[None, :], 0), axis=1)
    return (positions_at - first, first)


def rotary_tables(offsets, head_size):
    freqs = 1.0 / THETA ** (jnp.arange(0, head_size, 2, dtype=F32) / head_size)
    angles = offsets.astype(F32)[:, None] * freqs[None, :]
    cosine, sine = jnp.cos(angles), jnp.sin(angles)
    return (jnp.concatenate([cosine, cosine], axis=1), jnp.concatenate([-sine, sine], axis=1))


def rms_forward(rows, gain):
    recip = lax.rsqrt(jnp.mean(rows * rows, axis=-1, keepdims=True) + EPSILON)
    return (rows * recip * gain, recip)


def rms_backward(rows, recip, gain, upstream):
    weighted = upstream * gain
    grad_rows = recip * weighted - rows * (recip * recip * recip) * jnp.mean(
        rows * weighted, axis=-1, keepdims=True
    )
    gain_grad = jnp.sum(upstream * rows * recip, axis=0)
    return (grad_rows, gain_grad)


def dot(left, right, dims, out=F32):
    return lax.dot_general(left, right, ((dims[0], dims[1]), ((), ())), preferred_element_type=out)


def rows_dot(left, right):
    return dot(left, right, ((0,), (0,)))


def cols_dot(left, right):
    return dot(left, right, ((1,), (1,)))


def mat_dot(left, right):
    return dot(left, right, ((1,), (0,)))


def attend_forward_kernel(meta, q_ref, k_ref, v_ref, span_ref, o_ref, lse_ref):
    rows = q_ref.shape[0]
    queries = jnp.concatenate(
        [q_ref[:, h * HEAD_WIDTH : (h + 1) * HEAD_WIDTH] for h in range(GROUP)], axis=0
    )
    first, last = span_ref[0:1, :], span_ref[1:2, :]
    wide = GROUP * rows
    local = lax.broadcasted_iota(jnp.int32, (rows, 1), 0)

    def step(block, carry):
        top, total, accum = carry
        keys, values = k_ref[block], v_ref[block]
        scores = dot(keys, queries, ((1,), (1,))) * SCALE
        index = block * rows + local
        scores = jnp.where((index >= first) & (index <= last), scores, -1e30)
        new_top = jnp.maximum(top, jnp.max(scores, axis=0, keepdims=True))
        fade = jnp.exp(top - new_top)
        probs = jnp.exp(scores - new_top)
        total = total * fade + jnp.sum(probs, axis=0, keepdims=True)
        accum = accum * fade + dot(values, probs.astype(BF16), ((0,), (0,)))
        return (new_top, total, accum)

    top, total, accum = lax.fori_loop(
        meta[0],
        meta[1] + 1,
        step,
        (
            jnp.full((1, wide), -1e30, F32),
            jnp.zeros((1, wide), F32),
            jnp.zeros((HEAD_WIDTH, wide), F32),
        ),
    )
    attended = (accum / total).T.astype(BF16)
    for h in range(GROUP):
        o_ref[:, h * HEAD_WIDTH : (h + 1) * HEAD_WIDTH] = attended[h * rows : (h + 1) * rows]
    lse_ref[0] = top + jnp.log(total)


def attend_forward(number, meta, queries, stack, span):
    pieces, rows, _ = stack.shape
    width = queries.shape[1]
    part = width // KEY_VALUE_HEADS
    spec = pltpu.PrefetchScalarGridSpec(
        num_scalar_prefetch=1,
        grid=(KEY_VALUE_HEADS,),
        in_specs=[
            pl.BlockSpec((rows, part), lambda g, m: (number, g)),
            pl.BlockSpec((pieces, rows, HEAD_WIDTH), lambda g, m: (0, 0, g)),
            pl.BlockSpec((pieces, rows, HEAD_WIDTH), lambda g, m: (0, 0, KEY_VALUE_HEADS + g)),
            pl.BlockSpec((8, GROUP * rows), lambda g, m: (0, 0)),
        ],
        out_specs=[
            pl.BlockSpec((rows, part), lambda g, m: (0, g)),
            pl.BlockSpec((1, 1, GROUP * rows), lambda g, m: (g, 0, 0)),
        ],
    )
    return pl.pallas_call(
        attend_forward_kernel,
        grid_spec=spec,
        out_shape=(
            jax.ShapeDtypeStruct((rows, width), BF16),
            jax.ShapeDtypeStruct((KEY_VALUE_HEADS, 1, GROUP * rows), F32),
        ),
        cost_estimate=pl.CostEstimate(
            flops=4 * rows * rows * 6 * width, bytes_accessed=stack.size * 2, transcendentals=0
        ),
        name="attend_forward",
    )(meta, queries, stack, stack, span)


def attend_backward_kernel(
    meta, q_ref, do_ref, kv_ref, span_ref, lse_ref, cos_ref, sin_ref, dq_ref, dkv_ref, p_ref, dp_ref
):
    rows = q_ref.shape[0]
    wide = GROUP * rows
    first, last = span_ref[0:1, :], span_ref[1:2, :]
    local = lax.broadcasted_iota(jnp.int32, (rows, 1), 0)
    low = meta[0]
    cosine, sine = cos_ref[...], sin_ref[...]
    dkv_ref[...] = jnp.zeros_like(dkv_ref)
    for group in range(KEY_VALUE_HEADS):
        heads = range(group * GROUP, (group + 1) * GROUP)
        cols = [slice(h * HEAD_WIDTH, (h + 1) * HEAD_WIDTH) for h in heads]
        key_cols = slice(group * HEAD_WIDTH, (group + 1) * HEAD_WIDTH)
        start = (KEY_VALUE_HEADS + group) * HEAD_WIDTH
        value_cols = slice(start, start + HEAD_WIDTH)
        queries = jnp.concatenate([q_ref[:, c] for c in cols], axis=0)
        grads = jnp.concatenate([do_ref[:, c] for c in cols], axis=0)
        lse = lse_ref[group]

        def collect(block, delta):
            scores = dot(kv_ref[block, :, key_cols], queries, ((1,), (1,))) * SCALE
            index = block * rows + local
            probs = jnp.where((index >= first) & (index <= last), jnp.exp(scores - lse), 0.0)
            grad_probs = dot(kv_ref[block, :, value_cols], grads, ((1,), (1,)))
            p_ref[block - low] = probs
            dp_ref[block - low] = grad_probs
            return delta + jnp.sum(probs * grad_probs, axis=0, keepdims=True)

        delta = lax.fori_loop(low, meta[1] + 1, collect, jnp.zeros((1, wide), F32))

        def spread(block, accum):
            probs = p_ref[block - low]
            grad_scores = (probs * (dp_ref[block - low] - delta)).astype(BF16)
            dkv_ref[block, :, key_cols] = (mat_dot(grad_scores, queries) * SCALE).astype(BF16)
            dkv_ref[block, :, value_cols] = mat_dot(probs.astype(BF16), grads).astype(BF16)
            return accum + dot(kv_ref[block, :, key_cols], grad_scores, ((0,), (0,)))

        accum = lax.fori_loop(low, meta[1] + 1, spread, jnp.zeros((HEAD_WIDTH, wide), F32))
        grad_queries = (accum * SCALE).T
        for h in range(GROUP):
            part = grad_queries[h * rows : (h + 1) * rows]
            turned = pltpu.roll(part, HEAD_WIDTH // 2, 1)
            dq_ref[:, cols[h]] = (part * cosine - turned * sine).astype(BF16)


def attend_backward(number, meta, queries, grads, stack, span, lse, cosine, sine):
    pieces, rows, wide = stack.shape
    width = queries.shape[1]
    most = pieces // 2 + 1

    def own(columns):
        return pl.BlockSpec((rows, columns), lambda i, m: (number, 0))

    def whole(shape):
        return pl.BlockSpec(shape, lambda i, m: (0,) * len(shape))

    spec = pltpu.PrefetchScalarGridSpec(
        num_scalar_prefetch=1,
        grid=(1,),
        in_specs=[
            own(width),
            own(width),
            whole(stack.shape),
            whole(span.shape),
            whole(lse.shape),
            own(HEAD_WIDTH),
            own(HEAD_WIDTH),
        ],
        out_specs=[whole((rows, width)), whole(stack.shape)],
        scratch_shapes=[
            pltpu.VMEM((most, rows, GROUP * rows), F32),
            pltpu.VMEM((most, rows, GROUP * rows), F32),
        ],
    )
    return pl.pallas_call(
        attend_backward_kernel,
        grid_spec=spec,
        out_shape=(
            jax.ShapeDtypeStruct((rows, width), BF16),
            jax.ShapeDtypeStruct(stack.shape, BF16),
        ),
        cost_estimate=pl.CostEstimate(
            flops=0, bytes_accessed=COST, transcendentals=0
        ),
        name="attend_backward",
    )(meta, queries, grads, stack, span, lse, cosine, sine)


def hidden_kernel(
    token_ref,
    grad_ref,
    gate_ref,
    up_ref,
    down_ref,
    token_turned_ref,
    hidden_ref,
    turned_ref,
    dgate_ref,
    dup_ref,
):
    tokens = token_ref[...]
    token_turned_ref[...] = tokens.T
    gate_pre = mat_dot(tokens, gate_ref[...])
    up_pre = mat_dot(tokens, up_ref[...])
    grad_hidden = cols_dot(grad_ref[...], down_ref[...])
    sigma = jax.nn.sigmoid(gate_pre)
    activated = gate_pre * sigma
    hidden = activated * up_pre
    hidden_ref[...] = hidden.astype(BF16)
    turned_ref[...] = hidden.T.astype(BF16)
    dgate_ref[...] = (grad_hidden * up_pre * sigma * (1.0 + gate_pre * (1.0 - sigma))).astype(BF16)
    dup_ref[...] = (grad_hidden * activated).astype(BF16)


def hidden_units(rows, tokens, grads, w_gate, w_up, w_down):
    total, width = tokens.shape
    units = w_gate.shape[1]

    def tile(columns):
        return pl.BlockSpec((rows, columns), lambda i: (i, 0))

    def fixed(array):
        return pl.BlockSpec(array.shape, lambda i: (0, 0))

    return pl.pallas_call(
        hidden_kernel,
        grid=(total // rows,),
        in_specs=[tile(width), tile(width), fixed(w_gate), fixed(w_up), fixed(w_down)],
        out_specs=[
            pl.BlockSpec((width, rows), lambda i: (0, i)),
            tile(units),
            pl.BlockSpec((units, rows), lambda i: (0, i)),
            tile(units),
            tile(units),
        ],
        out_shape=(
            jax.ShapeDtypeStruct((width, total), BF16),
            jax.ShapeDtypeStruct((total, units), BF16),
            jax.ShapeDtypeStruct((units, total), BF16),
            jax.ShapeDtypeStruct((total, units), BF16),
            jax.ShapeDtypeStruct((total, units), BF16),
        ),
        cost_estimate=pl.CostEstimate(
            flops=6 * total * width * units, bytes_accessed=8 * total * width, transcendentals=0
        ),
        name="hidden_units",
    )(tokens, grads, w_gate, w_up, w_down)


def rotate_kernel(turned_heads, splits, sign, pre_ref, bias_ref, cos_ref, sin_ref, *outs):
    cosine, sine = cos_ref[...], sin_ref[...] * sign
    for head in range(pre_ref.shape[1] // HEAD_WIDTH):
        cols = slice(head * HEAD_WIDTH, (head + 1) * HEAD_WIDTH)
        part = pre_ref[:, cols] + bias_ref[:, cols]
        if head in turned_heads:
            part = part * cosine + pltpu.roll(part, HEAD_WIDTH // 2, 1) * sine
        part = part.astype(BF16)
        for (top, height, left, wide), out in zip(splits, outs):
            if left <= head * HEAD_WIDTH < left + wide:
                at = head * HEAD_WIDTH - left
                out[:, at : at + HEAD_WIDTH] = part[top : top + height]


def rotate(pre, bias, cosine, sine, turned_heads, splits, sign):
    return pl.pallas_call(
        functools.partial(rotate_kernel, tuple(turned_heads), splits, sign),
        out_shape=tuple(
            jax.ShapeDtypeStruct((height, wide), BF16) for _, height, _, wide in splits
        ),
        cost_estimate=pl.CostEstimate(flops=0, bytes_accessed=8 * pre.size, transcendentals=0),
        name="rotate",
    )(pre, bias, cosine, sine)


def cut_kernel(far, whole, *refs):
    count = len(refs) // 2
    for source, out in zip(refs[:count], refs[count:]):
        small = (out if whole else source).shape[1] // (8 * far)
        for h in range(far):
            for g in range(8):
                left, right = (h * 8 + g) * small, h * small
                if whole:
                    out[:, left : left + small] = source[g, :, right : right + small].astype(F32)
                else:
                    out[g, :, right : right + small] = source[:, left : left + small]


def cut_columns(far, whole, arrays):
    shapes = []
    for array in arrays:
        if whole:
            shapes.append(jax.ShapeDtypeStruct((array.shape[1], 8 * array.shape[2]), F32))
        else:
            shape = (8, array.shape[0], array.shape[1] // 8)
            shapes.append(jax.ShapeDtypeStruct(shape, array.dtype))
    return pl.pallas_call(
        functools.partial(cut_kernel, far, whole),
        out_shape=tuple(shapes),
        name="join_columns" if whole else "cut_columns",
    )(*arrays)


MESH = pl.DeviceIdType.MESH
PARTS, AHEAD = {"pair": 4, "pair8": 2}, {"pair": 2, "pair8": 1}
COST = 1024
ANY = pl.BlockSpec(memory_space=pl.ANY)


class Local:
    def __init__(self, source, buffer, target, sems):
        self.load = pltpu.make_async_copy(source, buffer, sems.at[0])
        self.store = pltpu.make_async_copy(buffer, target, sems.at[1])

    def start(self):
        self.load.start()

    def turn(self):
        self.load.wait()
        self.store.start()

    def wait(self):
        self.store.wait()


class Copies:
    def __init__(self, send_sems, recv_sems):
        self.send_sems, self.recv_sems, self.started = send_sems, recv_sems, []

    def start(self, source, target, device):
        number = len(self.started)
        copy = pltpu.make_async_remote_copy(
            src_ref=source,
            dst_ref=target,
            send_sem=self.send_sems.at[number],
            recv_sem=self.recv_sems.at[number],
            device_id=device,
            device_id_type=MESH,
        )
        copy.start()
        self.started.append(copy)
        return copy


def greet(devices):
    barrier = pltpu.get_barrier_semaphore()
    for device in devices:
        pl.semaphore_signal(barrier, inc=1, device_id=device, device_id_type=MESH)
    pl.semaphore_wait(barrier, len(devices))


def other_h(far, k):
    return {"h": lax.rem(lax.axis_index("h") + k, far)}


def flip(*axes):
    return {axis: 1 - lax.axis_index(axis) for axis in axes}


def corners():
    return [flip("p", "y"), flip("p", "c"), flip("y", "c"), flip("p", "y", "c")]


def gather_steps(kind, far, copies, source, out, local):
    ih, ip, iy, ic, ix = (lax.axis_index(name) for name in ("h", "p", "y", "c", "x"))
    every = kind in ("all", "all_y")

    def block(h, p, y=iy, x=ix):
        return out.at[h, p, y, ic, x] if every else out.at[h, p, y, ic]

    local.start()
    pieces = [(lax.rem(ih - k + far, far), p) for p in (ip, 1 - ip) for k in range(far)]
    count = len(pieces)
    arrivals, plane, cross, core = [None] * count, [None] * count, [None] * count, [None] * count
    columns = source.shape[-1]
    half = columns // 2 if columns % 256 == 0 and kind == "all" else columns

    def cut(ref, first):
        if half == columns:
            return ref
        return ref.at[:, pl.ds(0 if first else half, half)]

    for k in range(1, far):
        arrivals[k] = copies.start(source, block(ih, ip), other_h(far, k))
    for step in range(count + 3):
        if step < count:
            if arrivals[step] is not None:
                arrivals[step].wait_recv()
            h, p = pieces[step]
            held = source if step == 0 else block(h, p)
            if step < far:
                arrivals[far + step] = copies.start(held, block(h, p), flip("p"))
            plane[step] = [copies.start(held, block(h, p), flip("y"))]
            if every:
                plane[step].append(copies.start(held, block(h, p), flip("x")))
        if 0 <= step - 1 < count:
            h, p = pieces[step - 1]
            for copy in plane[step - 1]:
                copy.wait_recv()
            cross[step - 1] = []
            if every:
                ref = cut(block(h, p, x=1 - ix), True)
                cross[step - 1].append(copies.start(ref, ref, flip("y")))
                if half < columns:
                    ref = cut(block(h, p, y=1 - iy), False)
                    cross[step - 1].append(copies.start(ref, ref, flip("x")))
        if 0 <= step - 2 < count:
            h, p = pieces[step - 2]
            for copy in cross[step - 2]:
                copy.wait_recv()
            if step == 2:
                local.wait()
            ref = out.at[h, p, :, ic]
            core[step - 2] = copies.start(ref, ref, flip("c"))
        if 0 <= step - 3 < count:
            core[step - 3].wait_recv()
        yield


def group_steps(far, copies, source, out, local, delay):
    ip, iy, ic = (lax.axis_index(name) for name in ("p", "y", "c"))
    half = source.shape[0] // 2
    top, low = pl.ds(0, half), pl.ds(half, half)

    def rows(p, y, part):
        return out.at[p, y, ic, part]

    def forward(ref, axis):
        return copies.start(ref, ref, flip(axis))

    local.start()
    for _ in range(delay):
        yield
    first = [
        copies.start(source.at[top], rows(ip, iy, top), flip("y")),
        copies.start(source.at[low], rows(ip, iy, low), flip("p")),
    ]
    second = [
        copies.start(source.at[top], rows(ip, iy, top), flip("p")),
        copies.start(source.at[low], rows(ip, iy, low), flip("y")),
    ]
    core = [copies.start(source, out.at[ip, iy, ic], flip("c"))]
    yield
    first[0].wait_recv()
    second.append(forward(rows(ip, 1 - iy, top), "p"))
    core.append(forward(rows(ip, 1 - iy, top), "c"))
    first[1].wait_recv()
    second.append(forward(rows(1 - ip, iy, low), "y"))
    core.append(forward(rows(1 - ip, iy, low), "c"))
    yield
    for copy, p, y, part in (
        (second[0], 1 - ip, iy, top),
        (second[1], ip, 1 - iy, low),
        (second[2], 1 - ip, 1 - iy, top),
        (second[3], 1 - ip, 1 - iy, low),
    ):
        copy.wait_recv()
        core.append(forward(rows(p, y, part), "c"))
    yield
    for copy in core:
        copy.wait_recv()
    local.wait()


def pair_steps(far, copies, parts, place, local, delay, ahead):
    ih, ix = lax.axis_index("h"), lax.axis_index("x")
    local.start()
    for _ in range(delay):
        yield
    arrived, sent = [], []

    def send(i):
        if i < len(parts):
            target = place(ih, ix, i)
            arrived.append([copies.start(parts[i], target, other_h(far, k)) for k in range(1, far)])
            sent.append(copies.start(parts[i], target, flip("x")))

    for i in range(ahead):
        send(i)
    for i in range(len(parts)):
        yield
        send(i + ahead)
        for k in range(1, far):
            arrived[i][k - 1].wait_recv()
            ref = place(lax.rem(ih - k + far, far), ix, i)
            sent.append(copies.start(ref, ref, flip("x")))
    yield
    for copy in sent:
        copy.wait_recv()
    local.wait()


def spread_steps(far, copies, source, out, local, delay):
    ip, iy, ic = (lax.axis_index(name) for name in ("p", "y", "c"))
    me = (ip * 2 + iy) * 2 + ic
    local.start()
    for _ in range(delay):
        yield
    started = []
    for j in (1, 2, 4, 3, 5, 6, 7):
        p = 1 - ip if j & 4 else ip
        y = 1 - iy if j & 2 else iy
        c = 1 - ic if j & 1 else ic
        started.append(
            copies.start(source.at[(p * 2 + y) * 2 + c], out.at[me], {"p": p, "y": y, "c": c})
        )
    for _ in range(2 * far + 2):
        yield
    for copy in started:
        copy.wait_recv()
    local.wait()
    yield


def move_kernel(kinds, far, *refs):
    count = len(kinds)
    sources, outs = refs[:count], refs[count : 2 * count]
    buffers = refs[2 * count : 3 * count]
    send_sems, recv_sems, local_sems = refs[3 * count :]
    locals_ = []

    def local_copy(i, source, target):
        locals_.append(Local(source, buffers[i], target, local_sems.at[i]))
        return locals_[-1]

    ih, ip, iy, ic, ix = (lax.axis_index(name) for name in ("h", "p", "y", "c", "x"))
    partners = [flip("p"), flip("y"), flip("c")]
    if set(kinds) - {"spread", "group"}:
        partners += [other_h(far, k) for k in range(1, far)]
    if set(kinds) - {"seq", "group", "spread"}:
        partners.append(flip("x"))
    if "spread" in kinds:
        partners += corners()
    greet(partners)
    copies = Copies(send_sems, recv_sems)
    running = []
    for i, kind in enumerate(kinds):
        if kind == "spread":
            me = (ip * 2 + iy) * 2 + ic
            local = local_copy(i, sources[i].at[me], outs[i].at[me])
            running.append(spread_steps(far, copies, sources[i], outs[i], local, 0))
        elif kind == "group":
            place = outs[i].at[ip, iy, ic]
            local = local_copy(i, sources[i], place)
            delay = 3 if count > 1 else 0
            running.append(group_steps(far, copies, sources[i], outs[i], local, delay))
        elif kind in ("pair", "pair8"):
            local = outs[i].at[ih, :, ix] if kind == "pair8" else outs[i].at[ih, ix]
            local = local_copy(i, sources[i], local)
            step = (8 if kind == "pair8" else sources[i].shape[1]) // PARTS[kind]
            cuts = [pl.ds(part * step, step) for part in range(PARTS[kind])]
            if kind == "pair8":
                parts = [sources[i].at[c] for c in cuts]
            else:
                parts = [sources[i].at[:, c] for c in cuts]

            def place(h, x, part, out=outs[i], cuts=cuts, wide=kind == "pair8"):
                return out.at[h, cuts[part], x] if wide else out.at[h, x, :, cuts[part]]

            wait = (PARTS[kind] - AHEAD[kind] + 1) * kinds[:i].count("pair8")
            running.append(pair_steps(far, copies, parts, place, local, wait, AHEAD[kind]))
        else:
            place = (ih, ip, iy, ic) if kind == "seq" else (ih, ip, iy, ic, ix)
            local = local_copy(i, sources[i], outs[i].at[place])
            running.append(gather_steps(kind, far, copies, sources[i], outs[i], local))
    running = [job for job in running if next(job, "end") != "end"]
    for local in locals_:
        local.turn()
    while running:
        running = [job for job in running if next(job, "end") != "end"]
    for copy in copies.started:
        copy.wait_send()


def move(name, number, far, fsdp, kinds, arrays):
    shapes, total = [], 0
    pieces = 2 * far
    for kind, array in zip(kinds, arrays):
        if kind in ("all", "all_y"):
            lead, total = (far, 2, 2, 2, fsdp), total + (far - 1) + far + 5 * pieces
        elif kind == "seq":
            lead, total = (far, 2, 2, 2), total + (far - 1) + far + 2 * pieces
        elif kind == "group":
            lead, total = (2, 2, 2), total + 13
        elif kind == "pair":
            lead, total = (far, fsdp), total + PARTS[kind] * (2 * far - 1)
        elif kind == "pair8":
            lead, total = (far, 8, fsdp), total + PARTS[kind] * (2 * far - 1)
        else:
            lead, total = (), total + 7
        tail = array.shape[1:] if kind == "pair8" else array.shape
        shapes.append(jax.ShapeDtypeStruct(lead + tail, array.dtype))
    return pl.pallas_call(
        functools.partial(move_kernel, kinds, far),
        out_shape=tuple(shapes),
        in_specs=[ANY] * len(arrays),
        out_specs=tuple([ANY] * len(arrays)),
        scratch_shapes=[
            pltpu.VMEM(a.shape[1:] if kind == "spread" else a.shape, a.dtype)
            for kind, a in zip(kinds, arrays)
        ]
        + [
            pltpu.SemaphoreType.DMA((total,)),
            pltpu.SemaphoreType.DMA((total,)),
            pltpu.SemaphoreType.DMA((len(arrays), 2)),
        ],
        compiler_params=pltpu.CompilerParams(collective_id=number, has_side_effects=True),
        cost_estimate=pl.CostEstimate(flops=0, bytes_accessed=COST, transcendentals=0),
        name=name,
    )(*arrays)


def reduce_plan(kind, far, fsdp, tail):
    rows, columns = tail
    if kind == "group":
        step = rows // 4
        return ("p", "y"), [
            ((pl.ds(i * step, step), slice(None)), (step, columns), ("yp", "py")[i % 2])
            for i in range(4)
        ]
    if kind in ("seq", "seq_turned"):
        order = ("y", "p", "h") if kind == "seq" else ("p", "y", "h")
        return ("h", "p", "y"), [((slice(None), slice(None)), tail, order)]
    names = ("h", "p", "y", "x")
    if columns % 256:
        return names, [((slice(None), slice(None)), tail, ("x", "y", "p", "h"))]
    count = 4 if columns % 512 == 0 else 2
    step = columns // count
    orders = (("x", "y", "p", "h"), ("y", "x", "p", "h")) if kind == "all" else (("x", "y", "p", "h"),) * 2
    return names, [
        ((slice(None), pl.ds(i * step, step)), (rows, step), orders[i % 2]) for i in range(count)
    ]


def reduce_shapes(kind, far, fsdp, tail, dtype):
    length = {"h": far, "p": 2, "y": 2, "x": fsdp}
    names, parts = reduce_plan(kind, far, fsdp, tail)
    shapes = []
    for _, small, order in parts:
        left = list(names)
        full = tuple(length[n] for n in left) + small
        shapes += [full, full]
        for axis in order:
            left.remove(axis)
            lead = tuple(length[n] for n in left) + small
            shapes.append((far - 1,) + lead if axis == "h" else lead)
    return shapes


def reduce_steps(kind, far, fsdp, copies, source, out, scratch, local_sem):
    place = {name: lax.axis_index(name) for name in ("h", "p", "y", "x")}
    ic = lax.axis_index("c")
    length = {"h": far, "p": 2, "y": 2, "x": fsdp}
    core_dim = 2 if kind == "group" else 3
    names, parts = reduce_plan(kind, far, fsdp, out.shape)
    jobs, position = [], 0
    for cut, small, order in parts:
        count = 2 + len(order)
        jobs.append((cut, small, order, scratch[position : position + count]))
        position += count

    def view(c, cut):
        lead = [slice(None)] * core_dim + [c] + [slice(None)] * (len(names) - core_dim)
        return source.at[tuple(lead) + cut]

    def add(sums, brought, fixed, left, target=None, also=()):
        sizes = [1 if n in also else length[n] for n in left]
        total = 1
        for size in sizes:
            total *= size

        def one(number, _):
            index, rest = {}, number
            for n, size in reversed(list(zip(left, sizes))):
                index[n] = also[n] if n in also else rest % size
                rest = rest // size
            whole = tuple(fixed[n] if n in fixed else index[n] for n in names)
            value = sums[whole].astype(F32) + brought[tuple(index[n] for n in left)].astype(F32)
            if target is None:
                sums[whole] = value.astype(sums.dtype)
            else:
                target(value)
            return 0

        if total == 1:
            one(0, 0)
        else:
            lax.fori_loop(0, total, one, 0)

    loads, sent = [], []
    for i, (cut, small, order, refs) in enumerate(jobs):
        loads.append(pltpu.make_async_copy(view(ic, cut), refs[0], local_sem.at[i]))
        loads[i].start()
        sent.append(copies.start(view(1 - ic, cut), refs[1], flip("c")))
    yield
    for stage in range(len(jobs[0][2]) + 1):
        for i, (cut, small, order, refs) in enumerate(jobs):
            sums, brought = refs[0], refs[1 + stage]
            done = order[:stage]
            left = tuple(n for n in names if n not in done)
            fixed = {n: place[n] for n in done}
            if stage == 0:
                loads[i].wait()
            if stage > 0 and order[stage - 1] == "h":
                for copy in sent[i]:
                    copy.wait_recv()
            else:
                sent[i].wait_recv()
            if stage == len(order):
                if order[-1] == "h":
                    whole = tuple(place[n] for n in names)
                    value = sums[whole].astype(F32)
                    for k in range(far - 1):
                        value = value + brought[k].astype(F32)
                    out[cut] = value
                else:

                    def put(value, cut=cut):
                        out[cut] = value

                    add(sums, brought, fixed, left, put)
                continue
            axis = order[stage]
            if axis == "h":
                add(sums, brought, fixed, left)
                sent[i] = []
                for k in range(1, far):
                    goal = lax.rem(place["h"] + k, far)
                    whole = tuple(goal if n == "h" else place[n] for n in names)
                    sent[i].append(
                        copies.start(sums.at[whole], refs[2 + stage].at[k - 1], other_h(far, k))
                    )
            else:
                add(sums, brought, fixed, left, also={axis: 1 - place[axis]})
                index = tuple(
                    1 - place[n] if n == axis else fixed.get(n, slice(None)) for n in names
                )
                sent[i] = copies.start(sums.at[index], refs[2 + stage], flip(axis))
                add(sums, brought, fixed, left, also={axis: place[axis]})
        yield


def reduce_kernel(kinds, far, fsdp, counts, *refs):
    n = len(kinds)
    sources, outs = refs[:n], refs[n : 2 * n]
    scratch = refs[2 * n : -3]
    send_sems, recv_sems, local_sems = refs[-3:]
    partners = [flip("p"), flip("y"), flip("c")]
    if set(kinds) - {"group", "spread"}:
        partners += [other_h(far, k) for k in range(1, far)]
    if "all" in kinds or "all_x" in kinds:
        partners.append(flip("x"))
    if "spread" in kinds:
        partners += corners()
    greet(partners)
    copies = Copies(send_sems, recv_sems)
    running, position = [], 0
    for i, kind in enumerate(kinds):
        if kind == "spread":
            me = (lax.axis_index("p") * 2 + lax.axis_index("y")) * 2 + lax.axis_index("c")
            local = pltpu.make_async_copy(
                sources[i].at[me], outs[i].at[me], local_sems.at[i, 0]
            )
            running.append(spread_steps(far, copies, sources[i], outs[i], local, 1))
            continue
        part = scratch[position : position + counts[i]]
        position += counts[i]
        running.append(
            reduce_steps(
                kind, far, fsdp, copies, sources[i], outs[i], part, local_sems.at[i]
            )
        )
    while running:
        running = [job for job in running if next(job, "end") != "end"]
    for copy in copies.started:
        copy.wait_send()


def reduce(name, number, far, fsdp, kinds, arrays):
    shapes, scratch, counts, total = [], [], [], 0
    for kind, array in zip(kinds, arrays):
        if kind == "spread":
            shapes.append(jax.ShapeDtypeStruct(array.shape, array.dtype))
            counts.append(0)
            total += 7
            continue
        tail = array.shape[-2:]
        parts = reduce_plan(kind, far, fsdp, tail)[1]
        own = reduce_shapes(kind, far, fsdp, tail, array.dtype)
        counts.append(len(own))
        scratch += [pltpu.VMEM(shape, array.dtype) for shape in own]
        shapes.append(jax.ShapeDtypeStruct(tail, F32))
        total += sum(1 + len(order) + (far - 2 if "h" in order else 0) for _, _, order in parts)
    return pl.pallas_call(
        functools.partial(reduce_kernel, kinds, far, fsdp, tuple(counts)),
        out_shape=tuple(shapes),
        in_specs=[ANY] * len(arrays),
        out_specs=tuple(
            ANY if kind == "spread" else pl.BlockSpec(memory_space=pltpu.VMEM) for kind in kinds
        ),
        scratch_shapes=scratch
        + [
            pltpu.SemaphoreType.DMA((total,)),
            pltpu.SemaphoreType.DMA((total,)),
            pltpu.SemaphoreType.DMA((len(arrays), 4)),
        ],
        compiler_params=pltpu.CompilerParams(collective_id=number, has_side_effects=True),
        cost_estimate=pl.CostEstimate(flops=0, bytes_accessed=COST, transcendentals=0),
        name=name,
    )(*arrays)


def body(
    sizes,
    inputs,
    lengths,
    attn_gain,
    query_weight,
    query_bias,
    key_matrix,
    key_bias_vector,
    value_matrix,
    value_bias_vector,
    output_weight,
    mlp_gain,
    gate_weight,
    up_weight,
    down_weight,
    cotangent,
):
    far, fsdp = sizes
    micro, token_rows, width = inputs.shape[1:]
    shard = query_weight.shape[0]
    kv_width = key_matrix.shape[1]
    hidden_width = gate_weight.shape[1]
    devices = far * 8 * fsdp
    seq = far * 8
    ih, ip, iy, ic, ix = (lax.axis_index(name) for name in ("h", "p", "y", "c", "x"))
    me8 = (ip * 2 + iy) * 2 + ic
    me_seq = ih * 8 + me8

    def hop(array, axis, shift=1):
        if axis == "h":
            return lax.ppermute(array, "h", [(i, (i + shift) % far) for i in range(far)])
        return lax.ppermute(array, axis, SWAP)

    def pick(array, index, axis):
        return lax.dynamic_index_in_dim(array, index, axis, keepdims=False)

    slice_width = hidden_width // 8

    gate_cut, up_cut = cut_columns(far, False, (gate_weight, up_weight))

    vectors = jnp.concatenate(
        [attn_gain, query_bias, key_bias_vector, value_bias_vector, mlp_gain]
    ).astype(F32)
    vectors = jnp.pad(vectors, (0, 1024 - vectors.shape[0])).reshape(8, 128)
    w_qkv, vectors, gate_parts, up_parts, w_down = move(
        "gather_first",
        0,
        far,
        fsdp,
        ("all_y", "all", "spread", "spread", "pair"),
        (
            jnp.concatenate([query_weight, key_matrix, value_matrix], axis=1),
            vectors,
            gate_cut,
            up_cut,
            down_weight,
        ),
    )
    w_down = w_down.reshape(slice_width, width)
    w_qkv = w_qkv.reshape(width, -1)
    vectors = vectors.reshape(devices, 1024)
    cuts = [0]
    for part in (attn_gain, query_bias, key_bias_vector, value_bias_vector, mlp_gain):
        cuts.append(cuts[-1] + part.shape[0])
    gain_attn, b_query, b_key, b_value, gain_mlp = (
        vectors[:, cuts[i] : cuts[i + 1]].reshape(-1) for i in range(5)
    )
    rows = inputs[0].astype(F32).reshape(micro * token_rows, width)
    upstream_low = cotangent[0].reshape(micro * token_rows, width)
    positions_at = me_seq * token_rows + jnp.arange(token_rows, dtype=jnp.int32)
    tables, spans, metas = [], [], []
    for number in range(micro):
        offsets, first = locate(lengths[0, number], positions_at)
        tables.append(rotary_tables(offsets, HEAD_WIDTH))
        spans.append(
            jnp.concatenate(
                [
                    jnp.tile(first, GROUP)[None],
                    jnp.tile(positions_at, GROUP)[None],
                    jnp.zeros((6, GROUP * token_rows), jnp.int32),
                ],
                axis=0,
            )
        )
        low = jnp.maximum(first[0] // token_rows, me_seq - seq // 2)
        metas.append(jnp.stack([low, me_seq]).astype(jnp.int32))
    cosine_table = jnp.concatenate([t[0] for t in tables], axis=0)
    sine_table = jnp.concatenate([t[1] for t in tables], axis=0)

    normed, recip_one = rms_forward(rows, gain_attn)
    normed_low = normed.astype(BF16)
    pre = mat_dot(normed_low, w_qkv)
    heads = range(QUERY_HEADS + KEY_VALUE_HEADS)
    splits = ((0, micro * token_rows, 0, width),) + tuple(
        (m * token_rows, token_rows, width, 2 * kv_width) for m in range(micro)
    )
    biases = jnp.concatenate([b_query, b_key, b_value])[None]
    query_rotated, *own_kv = rotate(pre, biases, cosine_table, sine_table, heads, splits, 1.0)
    moved = move(
        "gather_second",
        1,
        far,
        fsdp,
        ("seq",) * micro + ("all_y", "pair8", "pair8", "group"),
        tuple(own_kv) + (output_weight, gate_parts, up_parts, upstream_low),
    )
    stacks = [part.reshape(seq, token_rows, 2 * kv_width) for part in moved[:micro]]
    w_output = moved[micro].reshape(width, width)
    w_gate, w_up = (part.reshape(width, slice_width) for part in moved[micro + 1 : micro + 3])
    upstream_all = moved[micro + 3].reshape(-1, width)
    attended, lses = [], []
    for m in range(micro):
        result, lse = attend_forward(m, metas[m], query_rotated, stacks[m], spans[m])
        attended.append(result)
        lses.append(lse)
    attended = jnp.concatenate(attended, axis=0)
    middle = rows + mat_dot(attended, w_output)
    normed_two, recip_two = rms_forward(middle, gain_mlp)
    (tokens,) = move("gather_tokens", 2, far, fsdp, ("group",), (normed_two.astype(BF16),))
    tokens = tokens.reshape(-1, width)

    tokens_turned, hidden, hidden_turned, grad_gate, grad_up = hidden_units(
        micro * token_rows, tokens, upstream_all, w_gate, w_up, w_down
    )
    group = (2, 2, 2, micro * token_rows, width)

    def over_x(grad, axis, other):
        grad = grad.astype(BF16)
        sent, other = lax.optimization_barrier((pick(grad, 1 - ix, axis), other))
        kept = pick(grad, ix, axis).astype(F32) + hop(sent, "x").astype(F32)
        return kept.astype(BF16), other

    def over_h(kept):
        total = pick(kept, ih, 0).astype(F32)
        for k in range(1, far):
            total = total + hop(pick(kept, (ih + k) % far, 0), "h", k).astype(F32)
        return total

    eight = (far, 8, fsdp, shard, slice_width)
    turned = tokens_turned.reshape(far, 8, fsdp, shard, -1)
    gate_sum, grad_up_last = over_x(dot(turned, grad_gate, ((4,), (0,))), 2, grad_up)
    up_sum, _ = over_x(dot(turned, grad_up_last, ((4,), (0,))), 2, ())
    grad_two = (cols_dot(grad_gate, w_gate) + cols_dot(grad_up, w_up)).astype(BF16)

    (grad_two,) = reduce("reduce_tokens", 3, far, fsdp, ("group",), (grad_two.reshape(group),))
    grad_norm, gain_mlp_sum = rms_backward(middle, recip_two, gain_mlp, grad_two)
    grad_middle = upstream_low.astype(F32) + grad_norm
    grad_branch = grad_middle.astype(BF16)
    grad_branch, gate_sum, up_sum = lax.optimization_barrier((grad_branch, gate_sum, up_sum))
    gate_sum = over_h(gate_sum).astype(BF16)
    grad_attended = cols_dot(grad_branch, w_output).astype(BF16)
    grad_kvs, grad_query = [], []
    for m in range(micro):
        query_part, grad_kv = attend_backward(
            m,
            metas[m],
            query_rotated,
            grad_attended,
            stacks[m],
            spans[m],
            lses[m],
            cosine_table,
            sine_table,
        )
        grad_kvs.append(grad_kv.reshape(far, 2, 2, 2, token_rows, 2 * kv_width))
        grad_query.append(query_part)

    blocks = (far, 2, 2, 2, fsdp, shard)
    grad_kvs, gate_sum, up_sum, hidden, hidden_turned = lax.optimization_barrier(
        (grad_kvs, gate_sum, up_sum, hidden, hidden_turned)
    )
    up_sum = over_h(up_sum).astype(BF16)
    down_part, _ = over_x(
        mat_dot(hidden_turned, upstream_all).reshape(far, fsdp, -1, width), 1, ()
    )
    final = mat_dot(hidden, w_down).astype(BF16)
    g_output = rows_dot(attended, grad_branch).astype(BF16)
    reduced = reduce(
        "reduce_second",
        4,
        far,
        fsdp,
        tuple("seq_turned" if m % 2 else "seq" for m in range(micro)) + ("all_x", "group"),
        tuple(grad_kvs) + (g_output.reshape(blocks + (width,)), final.reshape(group)),
    )
    grad_kvs, output_part = list(reduced[:micro]), reduced[micro]
    grad_kvs[0], down_part = lax.optimization_barrier((grad_kvs[0], down_part))
    down_part = over_h(down_part)
    results = (middle + reduced[micro + 1]).astype(BF16)
    grad_query = jnp.concatenate(grad_query, axis=0)
    grad_kv = jnp.concatenate(grad_kvs, axis=0)
    (grad_kv,) = rotate(
        grad_kv,
        jnp.zeros((1, 2 * kv_width), F32),
        cosine_table,
        sine_table,
        range(KEY_VALUE_HEADS),
        ((0, micro * token_rows, 0, 2 * kv_width),),
        -1.0,
    )
    grad_pre = jnp.concatenate([grad_query, grad_kv], axis=1)
    grad_normed = cols_dot(grad_pre, w_qkv)
    grad_rows, gain_attn_sum = rms_backward(rows, recip_one, gain_attn, grad_normed)
    input_grad = grad_middle + grad_rows
    g_qkv = rows_dot(normed_low, grad_pre).astype(BF16)
    bias_sum = jnp.sum(grad_pre.astype(F32), axis=0)
    vector_sums = jnp.concatenate(
        [
            v.reshape(devices, -1)
            for v in (
                gain_attn_sum,
                bias_sum[:width],
                bias_sum[width : width + kv_width],
                bias_sum[width + kv_width :],
                gain_mlp_sum,
            )
        ],
        axis=1,
    )
    vector_sums = jnp.pad(vector_sums, ((0, 0), (0, 1024 - vector_sums.shape[1])))
    qkv_part, vector_part, gate_sum, up_sum = reduce(
        "reduce_last",
        5,
        far,
        fsdp,
        ("all", "all", "spread", "spread"),
        (
            g_qkv.reshape(blocks + (-1,)),
            vector_sums.reshape(far, 2, 2, 2, fsdp, 8, 128),
            gate_sum,
            up_sum,
        ),
    )
    vector_part = vector_part.reshape(-1)

    gate_grad, up_grad = cut_columns(far, True, (gate_sum, up_sum))

    return (
        results.reshape(1, micro, token_rows, width),
        input_grad.reshape(1, micro, token_rows, width),
        vector_part[cuts[0] : cuts[1]],
        qkv_part[:, :width],
        vector_part[cuts[1] : cuts[2]],
        qkv_part[:, width : width + kv_width],
        vector_part[cuts[2] : cuts[3]],
        qkv_part[:, width + kv_width :],
        vector_part[cuts[3] : cuts[4]],
        output_part,
        vector_part[cuts[4] : cuts[5]],
        gate_grad,
        up_grad,
        down_part,
    )


def solution(mesh):
    fsdp = mesh.shape["fsdp"]
    far = mesh.shape["seq"] // 8
    inner = Mesh(mesh.devices.reshape(far, 2, 2, 2, fsdp), ("h", "p", "y", "c", "x"))
    seq = ("h", "p", "y", "c")
    every = seq + ("x",)
    tokens = P("x", None, seq, None)
    matrix, vector = P(every, None), P(every)
    in_specs = (
        tokens,
        P("x", None, None),
        vector,
        matrix,
        vector,
        matrix,
        vector,
        matrix,
        vector,
        matrix,
        vector,
        matrix,
        matrix,
        matrix,
        tokens,
    )
    out_specs = (
        tokens,
        tokens,
        vector,
        matrix,
        vector,
        matrix,
        vector,
        matrix,
        vector,
        matrix,
        vector,
        matrix,
        matrix,
        matrix,
    )
    return jax.shard_map(
        functools.partial(body, (far, fsdp)),
        mesh=inner,
        in_specs=in_specs,
        out_specs=out_specs,
        check_vma=False,
    )
```
